128 devices in a mesh: orb: 128 (over y, z, x, core).
Axes of the slice: x: 4, y: 4, z: 4, core: 2. Of those that a mesh axis runs over, the one named last changes fastest.
Arguments:
- orbitals: float32 [256, 48, 64, 128], P('orb'), may hold values from -6 to 6
- pair_list: int32 [128, 6, 2], P('orb'), may hold values from 0 to 255, as said below
- pair_count: int32 [128], P('orb'), may hold values from 1 to 6, 256 in all
- box_offset: int32 [256, 3], replicated, may hold values from 0 to 24
Outputs:
- exchange: float32 [256, 48, 64, 128], P('orb')
The draws below stay inside these ranges and needn't reach their ends.
Inputs may be any that keep to these rules, and one draw needn't show every extreme that they name: `pair_list`: every orbital named in row d is owned by a device d - 1 to d + 1; the two orbitals of a pair differ; slot 0 of every row pairs with an orbital of a device exactly 1 away. `pair_count`: they sum to 256.
All inputs are finite; a program needn't handle non-finite values. No bound on the sum of `pair_count` on one device may be relied on, other than what follows from the above.
Results may differ from the reference program's by a relative error of at most 0.0003.
Values sent between devices are 32-bit elements; how exact they have to be, the bound alone decides.
No kernel may reach another device: no remote copies, remote signals or barrier semaphores. Data moves between devices by JAX's collectives and lax.ppermute only.
A program may use at most 128 MiB of HBM per device.

```python
import math
import jax
import jax.numpy as jnp
import numpy as np
from jax import lax

BOX_X = 48
BOX_Y = 64
BOX_Z = 128
ORB_DEV = 2
SLOTS = 6
REACH = 1
SWEEPS = 12
RANKS = 128
ORBS = 256


def draw_pair_list(key, part):
    subkeys = jax.random.split(jax.random.fold_in(key, 7), 4)
    device = jnp.arange(RANKS, dtype=jnp.int32)[:, None]
    lead_shift = jax.random.randint(subkeys[0], (RANKS, SLOTS), -REACH, REACH + 1)
    lead_device = jnp.clip(device + lead_shift, 0, RANKS - 1)
    partner_shift = jax.random.randint(subkeys[1], (RANKS, SLOTS), -REACH, REACH + 1)
    boundary = jnp.where(device + REACH < RANKS, REACH, -REACH)
    slot_zero = jnp.arange(SLOTS, dtype=jnp.int32)[None, :] == 0
    partner_shift = jnp.where(slot_zero, boundary, partner_shift)
    partner_device = jnp.clip(device + partner_shift, 0, RANKS - 1)
    leading = lead_device * ORB_DEV + jax.random.randint(subkeys[2], (RANKS, SLOTS), 0, ORB_DEV)
    partner_local = jax.random.randint(subkeys[3], (RANKS, SLOTS), 0, ORB_DEV)
    partner = partner_device * ORB_DEV + partner_local
    partner = jnp.where(partner == leading, partner_device * ORB_DEV + (partner_local + 1) % ORB_DEV, partner)
    return jnp.stack([leading, partner], -1).astype(jnp.int32)


def touch_ends(array, key, low, largest):
    longest = array.shape.index(max(array.shape))
    spots = []
    for shift in (0, 1):
        where = [jax.random.randint(jax.random.fold_in(key, axis), (), 0, length) for axis, length in enumerate(array.shape)]
        where[longest] = (where[longest] + shift) % array.shape[longest]
        spots.append(tuple(where))
    return array.at[spots[0]].set(low).at[spots[1]].set(largest)


def block_scale(stream_key, shape, shards, least, top_value):
    def one(dim, blocks):
        draws = jax.random.uniform(jax.random.fold_in(jax.random.fold_in(stream_key, 6), dim), (blocks,), jnp.float32, least / len(shards), top_value / len(shards))
        return jnp.repeat(jnp.exp(draws), shape[dim] // blocks).reshape((-1,) + (1,) * (len(shape) - dim - 1))

    loudness = one(*shards[0])
    for cut in shards[1:]:
        loudness = loudness * one(*cut)
    return loudness


def profile(amount, total, bound, slope):
    loads = [(1 << 20) // math.isqrt(grade ** slope) + 1 for grade in range(2, amount + 1)]
    rest, holding = total - bound - (amount - 1), [1] * (amount - 1)
    while rest > 0:
        movable = [i for i in range(amount - 1) if holding[i] < bound]
        whole, left = sum([loads[i] for i in movable]), rest
        for i in movable:
            more = min(bound - holding[i], max(1, left * loads[i] // whole), rest)
            holding[i] = holding[i] + more
            rest = rest - more
    return np.array([bound] + holding)


def uneven_parts(rng, number_of, total, bound, skew):
    if number_of == 2:
        one = jax.random.randint(rng, (), max(1, total - bound), min(bound, total - 1) + 1)
        return jnp.stack([one, total - one])
    sizes = jnp.asarray(profile(number_of, total, bound, skew), jnp.int32)
    couples = (number_of - 1) // 2
    donor, receiver = sizes[1:1 + 2 * couples:2], sizes[2:2 + 2 * couples:2]
    slack = jnp.minimum(donor - 1, bound - receiver)
    shifted = jax.random.randint(jax.random.fold_in(rng, 1), (couples,), 0, 1 << 20) % (slack + 1)
    sizes = sizes.at[1:1 + 2 * couples:2].set(donor - shifted).at[2:2 + 2 * couples:2].set(receiver + shifted)
    return sizes[jax.random.permutation(jax.random.fold_in(rng, 2), number_of)]


def normal_values(key, extent, deviation, bound, cuts=(), kind=jnp.bfloat16):
    drawn = deviation * jax.random.normal(key, extent, jnp.float32)
    if cuts:
        drawn = drawn * block_scale(key, extent, cuts, -0.22, 0.18)
    return jnp.clip(drawn, -bound, bound).astype(kind)


def setup_inputs(seed: int = 0) -> dict:
    streams_of = jax.random.split(jax.random.key(seed), 5)
    return {
        "orbitals": normal_values(streams_of[0], (ORBS, BOX_X, BOX_Y, BOX_Z), 1.0, 6.0, ((0, 128),), jnp.float32),
        "pair_list": draw_pair_list(jax.random.fold_in(streams_of[4], 71), 0),
        "pair_count": uneven_parts(streams_of[2], RANKS, ORBS, SLOTS, 2).astype(jnp.int32),
        "box_offset": touch_ends(jax.random.randint(streams_of[3], (ORBS, 3), 0, BOX_X // 2 + 1), jax.random.fold_in(streams_of[3], 1), 0, (BOX_X // 2 + 1) - 1).astype(jnp.int32),
    }


def jacobi_solve(source_term):
    def sweep(sweep_index, potential):
        padded = jnp.pad(potential, 1)
        beside = padded[2:, 1:-1, 1:-1] + padded[:-2, 1:-1, 1:-1]
        beside = beside + padded[1:-1, 2:, 1:-1] + padded[1:-1, :-2, 1:-1]
        beside = beside + padded[1:-1, 1:-1, 2:] + padded[1:-1, 1:-1, :-2]
        return (beside + source_term) / 6.0
    return lax.fori_loop(0, SWEEPS, sweep, jnp.zeros_like(source_term))


def displaced(values_in, corner):
    margin = BOX_X // 2
    padded = jnp.pad(values_in, margin)
    return lax.dynamic_slice(padded, (corner[0], corner[1], corner[2]), values_in.shape)


def pair_terms(leading_box, partner_box, offset_gap):
    margin = BOX_X // 2
    partner = displaced(partner_box, margin - offset_gap)
    potential = jacobi_solve(leading_box * partner)
    own_term = potential * partner
    back_term = displaced(potential * leading_box, margin + offset_gap)
    return own_term, back_term


def reference(orbitals, pair_list, pair_count, box_offset):
    flat_pairs = pair_list.reshape(RANKS * SLOTS, 2)
    owners = jnp.repeat(jnp.arange(RANKS, dtype=jnp.int32), SLOTS)
    slot_index = jnp.tile(jnp.arange(SLOTS, dtype=jnp.int32), RANKS)
    live_mask = slot_index < pair_count[owners]

    def visit_pair(accum, element):
        pair_entry, is_live = element

        def add_pair(current):
            leading, partner = pair_entry[0], pair_entry[1]
            offset_gap = box_offset[partner] - box_offset[leading]
            own_term, back_term = pair_terms(orbitals[leading], orbitals[partner], offset_gap)
            current = current.at[leading].add(own_term)
            return current.at[partner].add(back_term)

        def unchanged(current):
            return current

        return lax.cond(is_live, add_pair, unchanged, accum), None

    start_value = jnp.zeros(orbitals.shape, jnp.float32)
    exchange, unused = lax.scan(visit_pair, start_value, (flat_pairs, live_mask))
    return exchange
```

```python
import functools

import jax
import jax.numpy as jnp
import ml_dtypes
import numpy as np
from jax import lax
from jax.experimental import pallas as pl
from jax.experimental.pallas import tpu as pltpu
from jax.sharding import PartitionSpec as P

BOX_X, BOX_Y, BOX_Z = 48, 64, 128
BOX = (BOX_X, BOX_Y, BOX_Z)
ORB_DEV = 2
SLOTS = 6
TILES = BOX_Y // 8
PLANE = BOX_Y + 8
STENCIL_ROWS = (BOX_X + 2) * PLANE + 8
MARGIN = 24
WIDE = BOX_Y + MARGIN
SHIFT_PLANES = BOX_X + 2 * MARGIN + 1
SHIFT_ROWS = SHIFT_PLANES * WIDE
STENCIL_UNROLL = 8
BLOCK = 8
F32 = jnp.float32
BF16 = jnp.bfloat16


def sine_basis():
    k = np.arange(1, BOX_Z + 1)
    basis = np.sqrt(2.0 / (BOX_Z + 1)) * np.sin(np.pi * np.outer(k, k) / (BOX_Z + 1))
    high = basis.astype(np.float32).astype(ml_dtypes.bfloat16)
    low = (basis - high.astype(np.float64)).astype(ml_dtypes.bfloat16)
    half = np.concatenate([high, low], 1)
    weights = np.concatenate([half, half], 0)
    values = np.tile(2.0 * np.cos(np.pi * k / (BOX_Z + 1)), (8, 1)).astype(np.float32)
    return weights, values


def stencil_row(x):
    return pl.multiple_of(8 + (x + 1) * PLANE, 8)


def shift_row(x):
    return pl.multiple_of((x + MARGIN) * WIDE + MARGIN, 8)


def zero_rows(ref, rows):
    zeros = jnp.zeros((8, BOX_Z), F32)

    def body(k, _):
        ref[pl.ds(pl.multiple_of(k * 8, 8), 8), :] = zeros
        return 0

    lax.fori_loop(0, rows // 8, body, 0, unroll=8)


def sweep(source, target, centre, other=None, factor=None):
    def plane(x, carry):
        behind, here = carry
        row = stencil_row(x)
        ahead_row = stencil_row(x + 1)
        ahead = [source[pl.ds(ahead_row + 8 * t, 8), :] for t in range(TILES)]
        for t in range(TILES):
            above = source[pl.ds(row + 8 * t - 1, 8), :]
            below = source[pl.ds(row + 8 * t + 1, 8), :]
            total = (behind[t] + ahead[t]) + (above + below) + centre * here[t]
            if other is not None:
                total = total + factor * other[pl.ds(row + 8 * t, 8), :]
            target[pl.ds(row + 8 * t, 8), :] = total
        return here, ahead

    first = [source[pl.ds(stencil_row(-1) + 8 * t, 8), :] for t in range(TILES)]
    second = [source[pl.ds(stencil_row(0) + 8 * t, 8), :] for t in range(TILES)]
    lax.fori_loop(0, BOX_X, plane, (first, second), unroll=STENCIL_UNROLL)


def along_z(rows, weights):
    high = rows.astype(BF16)
    low = (rows - high.astype(F32)).astype(BF16)
    product = jnp.dot(
        jnp.concatenate([high, low], 1), weights[...], preferred_element_type=F32
    )
    return product[:, :BOX_Z] + product[:, BOX_Z:]


def solve_pair(lead, shift, partner, bufs, weights, values, gap, accum, lead_slot, partner_slot):
    gap_x, gap_y, gap_z = gap
    lane = lax.broadcasted_iota(jnp.int32, (8, BOX_Z), 1)
    one, two, three = bufs
    centre = values[...]

    inside = (lane >= gap_z) & (lane < BOX_Z + gap_z)
    turn = jnp.where(gap_z < 0, gap_z + BOX_Z, gap_z)

    def density_block(block, _):
        parts = []
        for q in range(BLOCK):
            x = block * BLOCK + q
            base = (x - gap_x + MARGIN) * WIDE + MARGIN - gap_y
            for t in range(TILES):
                value = shift[pl.ds(base + 8 * t, 8), :]
                value = jnp.where(inside, pltpu.roll(value, turn, 1), 0.0)
                partner[x, pl.ds(8 * t, 8), :] = value
                parts.append(value * lead[x, pl.ds(8 * t, 8), :])
        spectral = along_z(jnp.concatenate(parts, 0), weights)
        for q in range(BLOCK):
            row = stencil_row(block * BLOCK + q)
            one[pl.ds(row, BOX_Y), :] = spectral[q * BOX_Y : (q + 1) * BOX_Y]
        return 0

    lax.fori_loop(0, BOX_X // BLOCK, density_block, 0)

    sweep(one, three, centre + 6.0)
    sweep(three, one, centre)
    sweep(one, two, centre, three, 36.0)
    sweep(two, one, centre)
    sweep(one, three, centre, three, 1296.0)
    sweep(three, one, centre)
    sweep(one, two, centre)
    sweep(two, one, centre)
    sweep(one, two, centre)
    sweep(two, one, centre)
    sweep(one, two, centre, three, 46656.0)
    scale = 1.0 / (6.0 * 6.0 * 1296.0 * 46656.0)

    def potential_block(block, _):
        rows = jnp.concatenate(
            [two[pl.ds(stencil_row(block * BLOCK + q), BOX_Y), :] for q in range(BLOCK)], 0
        )
        potential = along_z(rows, weights) * scale
        for q in range(BLOCK):
            x = block * BLOCK + q
            for t in range(TILES):
                at = pl.ds(8 * t, 8)
                value = potential[q * BOX_Y + 8 * t : q * BOX_Y + 8 * t + 8]
                accum[lead_slot, x, at, :] = (
                    accum[lead_slot, x, at, :] + value * partner[x, at, :]
                )
                shift[pl.ds(shift_row(x) + 8 * t, 8), :] = value * lead[x, at, :]
        return 0

    lax.fori_loop(0, BOX_X // BLOCK, potential_block, 0)

    back_inside = (lane >= -gap_z) & (lane < BOX_Z - gap_z)
    back_turn = jnp.where(gap_z > 0, BOX_Z - gap_z, -gap_z)

    def back_block(block, _):
        for q in range(BLOCK):
            x = block * BLOCK + q
            base = (x + gap_x + MARGIN) * WIDE + MARGIN + gap_y
            for t in range(TILES):
                at = pl.ds(8 * t, 8)
                value = shift[pl.ds(base + 8 * t, 8), :]
                value = jnp.where(back_inside, pltpu.roll(value, back_turn, 1), 0.0)
                accum[partner_slot, x, at, :] = accum[partner_slot, x, at, :] + value
        return 0

    lax.fori_loop(0, BOX_X // BLOCK, back_block, 0)


def stage_kernel(stage, table, offsets, weights, values, own, mate, *rest):
    if stage == 0:
        (out, lead, shift, partner, one, two, three, accum, sem, acc_sem) = rest
    else:
        (remote, _, out, remote_out, lead, shift, partner, one, two, three, accum, sem, acc_sem) = rest
    here, mate_id = table[26], table[26] ^ 1
    across = jnp.where(here % 2 == 0, here - 1, here + 1)

    def place(orbital):
        device = orbital // ORB_DEV
        return jnp.where(
            device == here, 0, jnp.where(device == mate_id, 2, 4)
        ) + orbital % ORB_DEV

    def entry(e):
        lead_id, partner_id = table[2 * e], table[2 * e + 1]
        is_own = e < SLOTS
        live = jnp.where(is_own, e, e - SLOTS) < jnp.where(is_own, table[24], table[25])
        lead_dev, partner_dev = lead_id // ORB_DEV, partner_id // ORB_DEV
        both_across = (lead_dev == across) & (partner_dev == across)
        both_here = (lead_dev == here) & (partner_dev == here)
        mine = live & ((is_own & ~both_across) | (~is_own & both_here))
        lead_slot, partner_slot = place(lead_id), place(partner_id)
        top = jnp.maximum(lead_slot, partner_slot)
        due = jnp.where(top < 4, 0, top - 3)
        return mine & (due == stage), lead_id, partner_id, lead_slot, partner_slot

    def touches(slot):
        found = jnp.bool_(False)
        for e in range(2 * SLOTS):
            active, _, _, a, b = entry(e)
            found = found | (active & ((a == slot) | (b == slot)))
        return found

    def fetch(slot, target, semaphore, start):
        sources = [own.at[0], own.at[1], mate.at[0], mate.at[1]]
        if stage:
            sources.append(remote.at[0])
        if not start:
            pltpu.make_async_copy(sources[0], target, semaphore).wait()
            return
        for k, source in enumerate(sources):
            @pl.when(jnp.minimum(slot, 4) == k)
            def _():
                pltpu.make_async_copy(source, target, semaphore).start()

    def zero_box(slot):
        def body(x, _):
            for t in range(TILES):
                accum[slot, x, pl.ds(8 * t, 8), :] = jnp.zeros((8, BOX_Z), F32)
            return 0

        lax.fori_loop(0, BOX_X, body, 0)

    touched = [touches(s) for s in range(4)]
    if stage == 0:
        for s in range(4):
            zero_box(s)
    else:
        for s in range(4):
            @pl.when(touched[s])
            def _():
                pltpu.make_async_copy(out.at[s], accum.at[s], acc_sem.at[s]).start()
        zero_box(4)

    zero_rows(shift, SHIFT_ROWS)
    for buf in (one, two, three):
        zero_rows(buf, STENCIL_ROWS)

    if stage:
        for s in range(4):
            @pl.when(touched[s])
            def _():
                pltpu.make_async_copy(out.at[s], accum.at[s], acc_sem.at[s]).wait()

    window = shift.reshape(SHIFT_PLANES, WIDE, BOX_Z).at[
        pl.ds(MARGIN, BOX_X), pl.ds(MARGIN, BOX_Y), :
    ]

    def visit(e, _):
        active, lead_id, partner_id, lead_slot, partner_slot = entry(e)

        @pl.when(active)
        def _():
            fetch(lead_slot, lead, sem.at[0], True)
            fetch(partner_slot, window, sem.at[1], True)
            gap = [offsets[3 * partner_id + k] - offsets[3 * lead_id + k] for k in range(3)]
            fetch(lead_slot, lead, sem.at[0], False)
            fetch(partner_slot, window, sem.at[1], False)
            solve_pair(
                lead, shift, partner, (one, two, three), weights, values, gap, accum,
                jnp.minimum(lead_slot, 4), jnp.minimum(partner_slot, 4),
            )

        return 0

    lax.fori_loop(0, 2 * SLOTS, visit, 0)

    copies = []
    if stage == 0:
        flags = [None] * 4
    else:
        flags = touched
    for s in range(4):
        copy = pltpu.make_async_copy(accum.at[s], out.at[s], acc_sem.at[s])
        if flags[s] is None:
            copy.start()
        else:
            pl.when(flags[s])(copy.start)
        copies.append((copy, flags[s]))
    if stage:
        copy = pltpu.make_async_copy(accum.at[4], remote_out.at[0], acc_sem.at[4])
        copy.start()
        copies.append((copy, None))
    for copy, flag in copies:
        if flag is None:
            copy.wait()
        else:
            pl.when(flag)(copy.wait)


def run_stage(stage, table, offsets, weights, values, own, mate, remote=None, accum=None):
    smem = pl.BlockSpec(memory_space=pltpu.SMEM)
    vmem = pl.BlockSpec(memory_space=pltpu.VMEM)
    anywhere = pl.BlockSpec(memory_space=pl.ANY)
    four = jax.ShapeDtypeStruct((4,) + BOX, F32)
    one = jax.ShapeDtypeStruct((1,) + BOX, F32)
    operands = [table, offsets, weights, values, own, mate]
    specs = [smem, smem, vmem, vmem, anywhere, anywhere]
    boxes = 4
    aliases = {}
    shapes = four
    outs = anywhere
    if stage:
        operands += [remote, accum]
        specs += [anywhere, anywhere]
        boxes = 5
        aliases = {7: 0}
        shapes = (four, one)
        outs = (anywhere, anywhere)
    return pl.pallas_call(
        functools.partial(stage_kernel, stage),
        out_shape=shapes,
        in_specs=specs,
        out_specs=outs,
        input_output_aliases=aliases,
        scratch_shapes=[
            pltpu.VMEM(BOX, F32),
            pltpu.VMEM((SHIFT_ROWS, BOX_Z), F32),
            pltpu.VMEM(BOX, F32),
            pltpu.VMEM((STENCIL_ROWS, BOX_Z), F32),
            pltpu.VMEM((STENCIL_ROWS, BOX_Z), F32),
            pltpu.VMEM((STENCIL_ROWS, BOX_Z), F32),
            pltpu.VMEM((boxes,) + BOX, F32),
            pltpu.SemaphoreType.DMA((2,)),
            pltpu.SemaphoreType.DMA((5,)),
        ],
        compiler_params=pltpu.CompilerParams(vmem_limit_bytes=40 << 20),
        cost_estimate=pl.CostEstimate(
            flops=50_000_000, bytes_accessed=20_000_000, transcendentals=0
        ),
        name="stage_" + "abc"[stage],
    )(*operands)


def local(orbitals, pair_list, pair_count, box_offset):
    position = lax.axis_index("orb")
    count = lax.axis_size("orb")
    mates = [(d, d ^ 1) for d in range(count)]
    across = [(d, d + 1) for d in range(1, count - 1, 2)]
    across = across + [(b, a) for a, b in across]
    row = jnp.concatenate([pair_list.reshape(-1), pair_count])
    far_row = lax.ppermute(row, "orb", across)
    table = jnp.concatenate(
        [row[:12], far_row[:12], row[12:], far_row[12:], position[None].astype(jnp.int32)]
    )
    offsets = box_offset.reshape(-1)
    mate = lax.ppermute(orbitals, "orb", mates)
    far_first = lax.ppermute(orbitals[:1], "orb", across)
    far_second = lax.ppermute(orbitals[1:], "orb", across)
    weights, values = sine_basis()
    weights, values = jnp.asarray(weights), jnp.asarray(values)
    fixed = (table, offsets, weights, values, orbitals, mate)
    accum = run_stage(0, *fixed)
    accum, for_first = run_stage(1, *fixed, far_first, accum)
    back_first = lax.ppermute(for_first, "orb", across)
    accum, for_second = run_stage(2, *fixed, far_second, accum)
    back_second = lax.ppermute(for_second, "orb", across)
    back_mate = lax.ppermute(accum[2:], "orb", mates)
    first = accum[0] + back_mate[0] + back_first[0]
    second = accum[1] + back_mate[1] + back_second[0]
    return jnp.stack([first, second])


def solution(mesh):
    placed = (P("orb", None, None, None), P("orb", None, None), P("orb"), P())
    return jax.shard_map(
        local, mesh=mesh, in_specs=placed, out_specs=P("orb", None, None, None), check_vma=False
    )
```

```python
import functools

import jax
import jax.numpy as jnp
import ml_dtypes
import numpy as np
from jax import lax
from jax.experimental import pallas as pl
from jax.experimental.pallas import tpu as pltpu
from jax.sharding import PartitionSpec as P

BOX_X, BOX_Y, BOX_Z = 48, 64, 128
BOX = (BOX_X, BOX_Y, BOX_Z)
ORB_DEV = 2
SLOTS = 6
TILES = BOX_Y // 8
PLANE = BOX_Y + 8
STENCIL_ROWS = (BOX_X + 2) * PLANE + 8
MARGIN = 24
WIDE = BOX_Y + MARGIN
SHIFT_PLANES = BOX_X + 2 * MARGIN + 1
SHIFT_ROWS = SHIFT_PLANES * WIDE
STENCIL_UNROLL = 8
BLOCK = 16
F32 = jnp.float32
BF16 = jnp.bfloat16


def sine_basis():
    k = np.arange(1, BOX_Z + 1)
    basis = np.sqrt(2.0 / (BOX_Z + 1)) * np.sin(np.pi * np.outer(k, k) / (BOX_Z + 1))
    high = basis.astype(np.float32).astype(ml_dtypes.bfloat16)
    low = (basis - high.astype(np.float64)).astype(ml_dtypes.bfloat16)
    half = np.concatenate([high, low], 1)
    weights = np.concatenate([half, half], 0)
    values = np.tile(2.0 * np.cos(np.pi * k / (BOX_Z + 1)), (8, 1)).astype(np.float32)
    return weights, values


def stencil_row(x):
    return pl.multiple_of(8 + (x + 1) * PLANE, 8)


def shift_row(x):
    return pl.multiple_of((x + MARGIN) * WIDE + MARGIN, 8)


def zero_rows(ref, first, rows):
    for k in range(rows // 8):
        ref[pl.ds(first + 8 * k, 8), :] = jnp.zeros((8, BOX_Z), F32)


def zero_margins(ref):
    def plane(p, _):
        row = pl.multiple_of(p * WIDE, 8)
        zero_rows(ref, row, MARGIN)

        @pl.when((p < MARGIN) | (p >= MARGIN + BOX_X))
        def _():
            zero_rows(ref, row + MARGIN, BOX_Y)

        return 0

    lax.fori_loop(0, SHIFT_PLANES, plane, 0)


def zero_borders(ref):
    zero_rows(ref, 0, 8 + PLANE)
    zero_rows(ref, STENCIL_ROWS - PLANE, PLANE)

    def plane(x, _):
        zero_rows(ref, pl.multiple_of(8 + (x + 1) * PLANE + BOX_Y, 8), 8)
        return 0

    lax.fori_loop(0, BOX_X, plane, 0)


def zero_box(ref):
    def plane(x, _):
        for t in range(TILES):
            ref[x, pl.ds(8 * t, 8), :] = jnp.zeros((8, BOX_Z), F32)
        return 0

    lax.fori_loop(0, BOX_X, plane, 0, unroll=2)


def sweep(source, target, centre, other=None, factor=None):
    def plane(x, carry):
        behind, here = carry
        row = stencil_row(x)
        ahead_row = stencil_row(x + 1)
        ahead = [source[pl.ds(ahead_row + 8 * t, 8), :] for t in range(TILES)]
        for t in range(TILES):
            above = source[pl.ds(row + 8 * t - 1, 8), :]
            below = source[pl.ds(row + 8 * t + 1, 8), :]
            total = (behind[t] + ahead[t]) + (above + below) + centre * here[t]
            if other is not None:
                total = total + factor * other[pl.ds(row + 8 * t, 8), :]
            target[pl.ds(row + 8 * t, 8), :] = total
        return here, ahead

    first = [source[pl.ds(stencil_row(-1) + 8 * t, 8), :] for t in range(TILES)]
    second = [source[pl.ds(stencil_row(0) + 8 * t, 8), :] for t in range(TILES)]
    lax.fori_loop(0, BOX_X, plane, (first, second), unroll=STENCIL_UNROLL)


def along_z(rows, weights):
    high = rows.astype(BF16)
    low = (rows - high.astype(F32)).astype(BF16)
    product = jnp.dot(
        jnp.concatenate([high, low], 1), weights[...], preferred_element_type=F32
    )
    return product[:, :BOX_Z] + product[:, BOX_Z:]


def solve_pair(lead, shift, partner, bufs, weights, values, gap, accum, lead_slot, partner_slot):
    gap_x, gap_y, gap_z = gap
    lane = lax.broadcasted_iota(jnp.int32, (8, BOX_Z), 1)
    one, two, three = bufs
    centre = values[...]

    inside = (lane >= gap_z) & (lane < BOX_Z + gap_z)
    turn = jnp.where(gap_z < 0, gap_z + BOX_Z, gap_z)

    def density_block(block, _):
        parts = []
        for q in range(BLOCK):
            x = block * BLOCK + q
            base = (x - gap_x + MARGIN) * WIDE + MARGIN - gap_y
            for t in range(TILES):
                value = shift[pl.ds(base + 8 * t, 8), :]
                value = jnp.where(inside, pltpu.roll(value, turn, 1), 0.0)
                partner[x, pl.ds(8 * t, 8), :] = value
                parts.append(value * lead[x, pl.ds(8 * t, 8), :])
        spectral = along_z(jnp.concatenate(parts, 0), weights)
        for q in range(BLOCK):
            row = stencil_row(block * BLOCK + q)
            one[pl.ds(row, BOX_Y), :] = spectral[q * BOX_Y : (q + 1) * BOX_Y]
        return 0

    lax.fori_loop(0, BOX_X // BLOCK, density_block, 0)

    sweep(one, three, centre + 6.0)
    sweep(three, one, centre)
    sweep(one, two, centre, three, 36.0)
    sweep(two, one, centre)
    sweep(one, three, centre, three, 1296.0)
    sweep(three, one, centre)
    sweep(one, two, centre)
    sweep(two, one, centre)
    sweep(one, two, centre)
    sweep(two, one, centre)
    sweep(one, two, centre, three, 46656.0)
    scale = 1.0 / (6.0 * 6.0 * 1296.0 * 46656.0)

    def potential_block(block, _):
        rows = jnp.concatenate(
            [two[pl.ds(stencil_row(block * BLOCK + q), BOX_Y), :] for q in range(BLOCK)], 0
        )
        potential = along_z(rows, weights) * scale
        for q in range(BLOCK):
            x = block * BLOCK + q
            for t in range(TILES):
                at = pl.ds(8 * t, 8)
                value = potential[q * BOX_Y + 8 * t : q * BOX_Y + 8 * t + 8]
                accum[lead_slot, x, at, :] = (
                    accum[lead_slot, x, at, :] + value * partner[x, at, :]
                )
                shift[pl.ds(shift_row(x) + 8 * t, 8), :] = value * lead[x, at, :]
        return 0

    lax.fori_loop(0, BOX_X // BLOCK, potential_block, 0)

    back_inside = (lane >= -gap_z) & (lane < BOX_Z - gap_z)
    back_turn = jnp.where(gap_z > 0, BOX_Z - gap_z, -gap_z)

    def back_block(block, _):
        for q in range(BLOCK):
            x = block * BLOCK + q
            base = (x + gap_x + MARGIN) * WIDE + MARGIN + gap_y
            for t in range(TILES):
                at = pl.ds(8 * t, 8)
                value = shift[pl.ds(base + 8 * t, 8), :]
                value = jnp.where(back_inside, pltpu.roll(value, back_turn, 1), 0.0)
                accum[partner_slot, x, at, :] = accum[partner_slot, x, at, :] + value
        return 0

    lax.fori_loop(0, BOX_X // BLOCK, back_block, 0)


REMOTE = 4
QUOTA = 2


def first_kernel(row, count, own, payload, note, sem):
    lane = lax.broadcasted_iota(jnp.int32, (8, BOX_Z), 1)
    value = jnp.where(lane == 2 * SLOTS, count[0].astype(F32), 0.0)
    for e in range(SLOTS):
        for k in range(2):
            value = jnp.where(lane == 2 * e + k, row[0, e, k].astype(F32), value)
    note[...] = jnp.zeros_like(note)
    note[0:8, :] = value
    box = pltpu.make_async_copy(own.at[0], payload.at[pl.ds(0, BOX_X)], sem.at[0])
    extra = pltpu.make_async_copy(note, payload.at[BOX_X], sem.at[1])
    box.start()
    extra.start()
    box.wait()
    extra.wait()


def second_kernel(own, box, sem):
    copy = pltpu.make_async_copy(own.at[1], box, sem)
    copy.start()
    copy.wait()


def stage_kernel(stage, row, count, position, offsets, weights, values, own, mate, *rest):
    if stage == 0:
        (accum, *rest) = rest
    elif stage == 1:
        (payload, _, accum, leaving, *rest) = rest
        remote = payload.at[pl.ds(0, BOX_X)]
    elif stage == 2:
        (payload, remote, _, accum, leaving, *rest) = rest
    else:
        (payload, _, accum, leaving, *rest) = rest
    lead, shift, partner, one, two, three, work, note, sem, note_sem = rest
    here = position[0]
    mate_id = here ^ 1
    is_left = here % 2 == 1
    across = jnp.where(is_left, here + 1, here - 1)

    if stage:
        copy = pltpu.make_async_copy(payload.at[BOX_X, pl.ds(0, 8), :], note, note_sem)
        copy.start()
        copy.wait()

    def near(e, k):
        return row[0, e, k]

    def far(e, k):
        return note[0, 2 * e + k].astype(jnp.int32)

    def place(orbital):
        device = orbital // ORB_DEV
        local_slot = orbital % ORB_DEV
        return jnp.where(
            device == here, local_slot, jnp.where(device == mate_id, 2 + local_slot, REMOTE)
        )

    work[0] = 0

    def push(wanted, lead_id, partner_id):
        @pl.when(wanted)
        def _():
            k = work[0]
            base = 1 + 5 * k
            work[0] = k + 1
            work[base] = place(lead_id)
            work[base + 1] = place(partner_id)
            for axis in range(3):
                work[base + 2 + axis] = offsets[3 * partner_id + axis] - offsets[3 * lead_id + axis]

    if stage in (0, 3):
        seen = jnp.int32(0)
        for e in range(SLOTS):
            lead_id, partner_id = near(e, 0), near(e, 1)
            inside = (
                (e < count[0])
                & (lead_id // ORB_DEV != across)
                & (partner_id // ORB_DEV != across)
            )
            early = seen < QUOTA
            push(inside & (early if stage == 0 else ~early), lead_id, partner_id)
            seen = seen + inside.astype(jnp.int32)
    if stage == 3:
        far_count = note[0, 2 * SLOTS].astype(jnp.int32)
        for e in range(SLOTS):
            lead_id, partner_id = far(e, 0), far(e, 1)
            push(
                (e < far_count)
                & (lead_id // ORB_DEV == here)
                & (partner_id // ORB_DEV == here),
                lead_id,
                partner_id,
            )
    if stage in (1, 2):
        far_count = note[0, 2 * SLOTS].astype(jnp.int32)
        left = jnp.where(is_left, here, across)
        right = jnp.where(is_left, across, here)
        entries = []
        load_left, load_right = jnp.int32(0), jnp.int32(0)
        for side in range(2):
            use_near = is_left if side == 0 else ~is_left
            other = right if side == 0 else left
            limit = jnp.where(use_near, count[0], far_count)
            for e in range(SLOTS):
                a = jnp.where(use_near, near(e, 0), far(e, 0))
                b = jnp.where(use_near, near(e, 1), far(e, 1))
                a_dev, b_dev = a // ORB_DEV, b // ORB_DEV
                on_left = (a_dev == left) | (b_dev == left)
                on_right = (a_dev == right) | (b_dev == right)
                crosses = (e < limit) & (
                    (a_dev == other) != (b_dev == other)
                )
                free = crosses & on_left & on_right
                fixed = crosses & ~free
                left_bit = jnp.where(a_dev == left, a, b) % ORB_DEV
                right_bit = jnp.where(a_dev == right, a, b) % ORB_DEV
                if side == 0:
                    load_left = load_left + fixed.astype(jnp.int32)
                else:
                    load_right = load_right + fixed.astype(jnp.int32)
                entries.append((side, a, b, free, fixed, left_bit, right_bit))
        for side, a, b, free, fixed, left_bit, right_bit in entries:
            go_left = (load_left < load_right) | (
                (load_left == load_right) & (right_bit <= left_bit)
            )
            load_left = load_left + (free & go_left).astype(jnp.int32)
            load_right = load_right + (free & ~go_left).astype(jnp.int32)
            at_left = (free & go_left) | (fixed if side == 0 else jnp.bool_(False))
            at_right = (free & ~go_left) | (fixed if side == 1 else jnp.bool_(False))
            mine = (at_left & is_left) | (at_right & ~is_left)
            bit = jnp.where(is_left, right_bit, left_bit)
            push(mine & (bit == stage - 1), a, b)

    total = work[0]
    sources = [own.at[0], own.at[1], mate.at[0], mate.at[1]]
    if stage in (1, 2):
        sources.append(remote)

    def window(buf):
        return shift.at[buf].reshape(SHIFT_PLANES, WIDE, BOX_Z).at[
            pl.ds(MARGIN, BOX_X), pl.ds(MARGIN, BOX_Y), :
        ]

    def fetch(k, buf):
        for which, target in ((0, lead.at[buf]), (1, window(buf))):
            slot = work[1 + 5 * k + which]
            for s, source in enumerate(sources):
                @pl.when(slot == s)
                def _():
                    pltpu.make_async_copy(source, target, sem.at[which, buf]).start()

    @pl.when(total > 0)
    def _():
        fetch(0, 0)
        for buf in (one, two, three):
            zero_borders(buf)
        zero_margins(shift.at[0])

        @pl.when(total > 1)
        def _():
            zero_margins(shift.at[1])

    if stage == 0:
        for slot in range(REMOTE + 1):
            zero_box(accum.at[slot])

    def visit(k, _):
        buf = k % 2
        pltpu.make_async_copy(sources[0], lead.at[buf], sem.at[0, buf]).wait()
        pltpu.make_async_copy(sources[0], window(buf), sem.at[1, buf]).wait()

        @pl.when(k + 1 < total)
        def _():
            fetch(k + 1, 1 - buf)

        base = 1 + 5 * k
        solve_pair(
            lead.at[buf], shift.at[buf], partner, (one, two, three), weights, values,
            [work[base + 2 + axis] for axis in range(3)], accum, work[base], work[base + 1],
        )
        return 0

    lax.fori_loop(0, total, visit, 0)

    if stage:
        boxes = accum.at[pl.ds(2, 2)] if stage == 3 else accum.at[REMOTE]
        copy = pltpu.make_async_copy(boxes, leaving, note_sem)
        copy.start()
        copy.wait()
    if stage == 1:
        @pl.when(total > 0)
        def _():
            zero_box(accum.at[REMOTE])


SMEM = pl.BlockSpec(memory_space=pltpu.SMEM)
VMEM = pl.BlockSpec(memory_space=pltpu.VMEM)
HBM = pl.BlockSpec(memory_space=pltpu.HBM)


def run_stage(stage, fixed, remote, accum):
    carried = [] if accum is None else [accum]
    operands = list(fixed) + list(remote) + carried
    specs = [SMEM] * 4 + [VMEM] * 2 + [HBM] * 2 + [HBM] * len(remote) + [VMEM] * len(carried)
    shapes = [jax.ShapeDtypeStruct((REMOTE + 1,) + BOX, F32)]
    outs = [VMEM]
    if stage:
        shapes.append(jax.ShapeDtypeStruct(((2,) if stage == 3 else ()) + BOX, F32))
        outs.append(VMEM)
    return pl.pallas_call(
        functools.partial(stage_kernel, stage),
        out_shape=shapes,
        in_specs=specs,
        out_specs=outs,
        input_output_aliases={len(operands) - 1: 0} if carried else {},
        scratch_shapes=[
            pltpu.VMEM((2,) + BOX, F32),
            pltpu.VMEM((2, SHIFT_ROWS, BOX_Z), F32),
            pltpu.VMEM(BOX, F32),
            pltpu.VMEM((STENCIL_ROWS, BOX_Z), F32),
            pltpu.VMEM((STENCIL_ROWS, BOX_Z), F32),
            pltpu.VMEM((STENCIL_ROWS, BOX_Z), F32),
            pltpu.SMEM((1 + 5 * 2 * SLOTS,), jnp.int32),
            pltpu.SMEM((8, BOX_Z), F32),
            pltpu.SemaphoreType.DMA((2, 2)),
            pltpu.SemaphoreType.DMA,
        ],
        compiler_params=pltpu.CompilerParams(vmem_limit_bytes=28 << 20),
        cost_estimate=pl.CostEstimate(
            flops=200_000_000, bytes_accessed=20_000_000, transcendentals=0
        ),
        name="stage_" + "abcd"[stage],
    )(*operands)


def total_kernel(box, accum, mate, remote, *rest):
    result, chunk, sem = rest[-3:]

    def add(x, _):
        for t in range(TILES):
            at = pl.ds(8 * t, 8)
            chunk[x, at, :] = accum[box, x, at, :] + mate[box, x, at, :] + remote[x, at, :]
        pltpu.make_async_copy(chunk.at[x], result.at[box, x], sem).start()
        return 0

    lax.fori_loop(0, BOX_X, add, 0, unroll=2)
    pltpu.make_async_copy(chunk, result.at[box], sem).wait()


def run_total(box, accum, mate, remote, result=None):
    operands = [accum, mate, remote]
    specs = [VMEM, VMEM, VMEM]
    aliases = {}
    if result is not None:
        operands.append(result)
        specs.append(HBM)
        aliases = {3: 0}
    return pl.pallas_call(
        functools.partial(total_kernel, box),
        out_shape=jax.ShapeDtypeStruct((ORB_DEV,) + BOX, F32),
        in_specs=specs,
        out_specs=HBM,
        input_output_aliases=aliases,
        scratch_shapes=[pltpu.VMEM(BOX, F32), pltpu.SemaphoreType.DMA],
        compiler_params=pltpu.CompilerParams(vmem_limit_bytes=4 << 20),
        name="total_" + "ab"[box],
    )(*operands)


def local(orbitals, pair_list, pair_count, box_offset):
    position = lax.axis_index("orb").astype(jnp.int32)[None]
    devices = lax.axis_size("orb")
    mates = [(d, d ^ 1) for d in range(devices)]
    across = [(d, d + 1) for d in range(1, devices - 1, 2)]
    across = across + [(b, a) for a, b in across]
    payload = pl.pallas_call(
        first_kernel,
        out_shape=jax.ShapeDtypeStruct((BOX_X + 1, BOX_Y, BOX_Z), F32),
        in_specs=[SMEM, SMEM, HBM],
        out_specs=HBM,
        scratch_shapes=[pltpu.VMEM((BOX_Y, BOX_Z), F32), pltpu.SemaphoreType.DMA((2,))],
        name="first_box",
    )(pair_list, pair_count, orbitals)
    payload, held = lax.optimization_barrier((payload, orbitals))
    far_first = lax.ppermute(payload, "orb", across)
    mate = lax.ppermute(held, "orb", mates)
    second = pl.pallas_call(
        second_kernel,
        out_shape=jax.ShapeDtypeStruct(BOX, F32),
        in_specs=[HBM],
        out_specs=HBM,
        scratch_shapes=[pltpu.SemaphoreType.DMA],
        name="second_box",
    )(held)
    far_second = lax.ppermute(second, "orb", across)
    weights, values = sine_basis()
    fixed = (
        pair_list, pair_count, position, box_offset.reshape(-1),
        jnp.asarray(weights), jnp.asarray(values), orbitals, mate,
    )
    (accum,) = run_stage(0, fixed, (), None)
    accum, for_first = run_stage(1, fixed, (far_first,), accum)
    back_first = lax.ppermute(for_first, "orb", across)
    accum, for_second = run_stage(2, fixed, (far_first, far_second), accum)
    for_second, back_first, accum = lax.optimization_barrier((for_second, back_first, accum))
    back_second = lax.ppermute(for_second, "orb", across)
    accum, for_mate = run_stage(3, fixed, (far_first,), accum)
    back_mate = lax.ppermute(for_mate, "orb", mates)
    result = run_total(0, accum, back_mate, back_first)
    return run_total(1, accum, back_mate, back_second, result)


def solution(mesh):
    placed = (P("orb", None, None, None), P("orb", None, None), P("orb"), P())
    return jax.shard_map(
        local, mesh=mesh, in_specs=placed, out_specs=P("orb", None, None, None), check_vma=False
    )
```

```python
import functools

import jax
import jax.numpy as jnp
import ml_dtypes
import numpy as np
from jax import lax
from jax.experimental import pallas as pl
from jax.experimental.pallas import tpu as pltpu
from jax.sharding import PartitionSpec as P

BOX_X, BOX_Y, BOX_Z = 48, 64, 128
BOX = (BOX_X, BOX_Y, BOX_Z)
ORB_DEV = 2
SLOTS = 6
TILES = BOX_Y // 8
PLANE = BOX_Y + 8
STENCIL_ROWS = (BOX_X + 2) * PLANE + 8
MARGIN = 24
WIDE = BOX_Y + MARGIN
SHIFT_PLANES = BOX_X + 2 * MARGIN + 1
SHIFT_ROWS = SHIFT_PLANES * WIDE
STENCIL_UNROLL = 8
BLOCK = 24
F32 = jnp.float32
BF16 = jnp.bfloat16


def sine_basis():
    k = np.arange(1, BOX_Z + 1)
    basis = np.sqrt(2.0 / (BOX_Z + 1)) * np.sin(np.pi * np.outer(k, k) / (BOX_Z + 1))
    high = basis.astype(np.float32).astype(ml_dtypes.bfloat16)
    low = (basis - high.astype(np.float64)).astype(ml_dtypes.bfloat16)
    half = np.concatenate([high, low], 1)
    weights = np.concatenate([half, half], 0)
    values = np.tile(2.0 * np.cos(np.pi * k / (BOX_Z + 1)), (8, 1)).astype(np.float32)
    return weights, values


def stencil_row(x):
    return pl.multiple_of(8 + (x + 1) * PLANE, 8)


def shift_row(x):
    return pl.multiple_of((x + MARGIN) * WIDE + MARGIN, 8)


def zero_rows(ref, first, rows):
    for k in range(rows // 8):
        ref[pl.ds(first + 8 * k, 8), :] = jnp.zeros((8, BOX_Z), F32)


def zero_margins(ref):
    def plane(p, _):
        row = pl.multiple_of(p * WIDE, 8)
        zero_rows(ref, row, MARGIN)

        @pl.when((p < MARGIN) | (p >= MARGIN + BOX_X))
        def _():
            zero_rows(ref, row + MARGIN, BOX_Y)

        return 0

    lax.fori_loop(0, SHIFT_PLANES, plane, 0)


def zero_borders(ref):
    zero_rows(ref, 0, 8 + PLANE)
    zero_rows(ref, STENCIL_ROWS - PLANE, PLANE)

    def plane(x, _):
        zero_rows(ref, pl.multiple_of(8 + (x + 1) * PLANE + BOX_Y, 8), 8)
        return 0

    lax.fori_loop(0, BOX_X, plane, 0)


def zero_box(ref):
    def plane(x, _):
        for t in range(TILES):
            ref[x, pl.ds(8 * t, 8), :] = jnp.zeros((8, BOX_Z), F32)
        return 0

    lax.fori_loop(0, BOX_X, plane, 0, unroll=2)


def sweep(source, target, centre, other=None, factor=None):
    def plane(x, carry):
        behind, here = carry
        row = stencil_row(x)
        ahead_row = stencil_row(x + 1)
        ahead = [source[pl.ds(ahead_row + 8 * t, 8), :] for t in range(TILES)]
        for t in range(TILES):
            above = source[pl.ds(row + 8 * t - 1, 8), :]
            below = source[pl.ds(row + 8 * t + 1, 8), :]
            total = (behind[t] + ahead[t]) + (above + below) + centre * here[t]
            if other is not None:
                total = total + factor * other[pl.ds(row + 8 * t, 8), :]
            target[pl.ds(row + 8 * t, 8), :] = total
        return here, ahead

    first = [source[pl.ds(stencil_row(-1) + 8 * t, 8), :] for t in range(TILES)]
    second = [source[pl.ds(stencil_row(0) + 8 * t, 8), :] for t in range(TILES)]
    lax.fori_loop(0, BOX_X, plane, (first, second), unroll=STENCIL_UNROLL)


def along_z(rows, weights):
    high = rows.astype(BF16)
    low = (rows - high.astype(F32)).astype(BF16)
    product = jnp.dot(
        jnp.concatenate([high, low], 1), weights[...], preferred_element_type=F32
    )
    return product[:, :BOX_Z] + product[:, BOX_Z:]


def solve_pair(lead, shift, partner, bufs, weights, values, gap, accum, lead_slot, partner_slot):
    gap_x, gap_y, gap_z = gap
    lane = lax.broadcasted_iota(jnp.int32, (8, BOX_Z), 1)
    one, two, three = bufs
    centre = values[...]

    inside = (lane >= gap_z) & (lane < BOX_Z + gap_z)
    turn = jnp.where(gap_z < 0, gap_z + BOX_Z, gap_z)

    def density_block(block, _):
        parts = []
        for q in range(BLOCK):
            x = block * BLOCK + q
            base = (x - gap_x + MARGIN) * WIDE + MARGIN - gap_y
            for t in range(TILES):
                value = shift[pl.ds(base + 8 * t, 8), :]
                value = jnp.where(inside, pltpu.roll(value, turn, 1), 0.0)
                partner[x, pl.ds(8 * t, 8), :] = value
                parts.append(value * lead[x, pl.ds(8 * t, 8), :])
        spectral = along_z(jnp.concatenate(parts, 0), weights)
        for q in range(BLOCK):
            row = stencil_row(block * BLOCK + q)
            one[pl.ds(row, BOX_Y), :] = spectral[q * BOX_Y : (q + 1) * BOX_Y]
        return 0

    lax.fori_loop(0, BOX_X // BLOCK, density_block, 0)

    sweep(one, three, centre + 6.0)
    sweep(three, one, centre)
    sweep(one, two, centre, three, 36.0)
    sweep(two, one, centre)
    sweep(one, three, centre, three, 1296.0)
    sweep(three, one, centre)
    sweep(one, two, centre)
    sweep(two, one, centre)
    sweep(one, two, centre)
    sweep(two, one, centre)
    sweep(one, two, centre, three, 46656.0)
    scale = 1.0 / (6.0 * 6.0 * 1296.0 * 46656.0)

    def potential_block(block, _):
        rows = jnp.concatenate(
            [two[pl.ds(stencil_row(block * BLOCK + q), BOX_Y), :] for q in range(BLOCK)], 0
        )
        potential = along_z(rows, weights) * scale
        for q in range(BLOCK):
            x = block * BLOCK + q
            for t in range(TILES):
                at = pl.ds(8 * t, 8)
                value = potential[q * BOX_Y + 8 * t : q * BOX_Y + 8 * t + 8]
                accum[lead_slot, x, at, :] = (
                    accum[lead_slot, x, at, :] + value * partner[x, at, :]
                )
                shift[pl.ds(shift_row(x) + 8 * t, 8), :] = value * lead[x, at, :]
        return 0

    lax.fori_loop(0, BOX_X // BLOCK, potential_block, 0)

    back_inside = (lane >= -gap_z) & (lane < BOX_Z - gap_z)
    back_turn = jnp.where(gap_z > 0, BOX_Z - gap_z, -gap_z)

    def back_block(block, _):
        for q in range(BLOCK):
            x = block * BLOCK + q
            base = (x + gap_x + MARGIN) * WIDE + MARGIN + gap_y
            for t in range(TILES):
                at = pl.ds(8 * t, 8)
                value = shift[pl.ds(base + 8 * t, 8), :]
                value = jnp.where(back_inside, pltpu.roll(value, back_turn, 1), 0.0)
                accum[partner_slot, x, at, :] = accum[partner_slot, x, at, :] + value
        return 0

    lax.fori_loop(0, BOX_X // BLOCK, back_block, 0)


REMOTE = 4
QUOTA = 2


def first_kernel(row, count, own, payload, sem):
    box = pltpu.make_async_copy(own.at[0], payload.at[pl.ds(0, BOX_X)], sem)
    box.start()
    lane = lax.broadcasted_iota(jnp.int32, (8, BOX_Z), 1)
    value = jnp.where(lane == 2 * SLOTS, count[0].astype(F32), 0.0)
    for e in range(SLOTS):
        for k in range(2):
            value = jnp.where(lane == 2 * e + k, row[0, e, k].astype(F32), value)
    payload[BOX_X] = jnp.zeros((BOX_Y, BOX_Z), F32)
    payload[BOX_X, 0:8, :] = value
    box.wait()


def second_kernel(own, box, sem):
    copy = pltpu.make_async_copy(own.at[1], box, sem)
    copy.start()
    copy.wait()


def stage_kernel(stage, row, count, position, offsets, weights, values, own, mate, *rest):
    if stage == 0:
        (accum, *rest) = rest
    elif stage == 1:
        (payload, _, accum, leaving, *rest) = rest
        remote = payload.at[pl.ds(0, BOX_X)]
    elif stage == 2:
        (payload, remote, _, accum, leaving, *rest) = rest
    else:
        (payload, _, accum, leaving, *rest) = rest
    lead, shift, partner, one, two, three, work, note, sem, note_sem = rest
    here = position[0]
    mate_id = here ^ 1
    is_left = here % 2 == 1
    across = jnp.where(is_left, here + 1, here - 1)

    if stage:
        copy = pltpu.make_async_copy(payload.at[BOX_X, pl.ds(0, 8), :], note, note_sem)
        copy.start()
        copy.wait()

    def near(e, k):
        return row[0, e, k]

    def far(e, k):
        return note[0, 2 * e + k].astype(jnp.int32)

    def place(orbital):
        device = orbital // ORB_DEV
        local_slot = orbital % ORB_DEV
        return jnp.where(
            device == here, local_slot, jnp.where(device == mate_id, 2 + local_slot, REMOTE)
        )

    work[0] = 0

    def push(wanted, lead_id, partner_id):
        @pl.when(wanted)
        def _():
            k = work[0]
            base = 1 + 5 * k
            work[0] = k + 1
            work[base] = place(lead_id)
            work[base + 1] = place(partner_id)
            for axis in range(3):
                work[base + 2 + axis] = offsets[3 * partner_id + axis] - offsets[3 * lead_id + axis]

    if stage in (0, 3):
        seen = jnp.int32(0)
        for e in range(SLOTS):
            lead_id, partner_id = near(e, 0), near(e, 1)
            inside = (
                (e < count[0])
                & (lead_id // ORB_DEV != across)
                & (partner_id // ORB_DEV != across)
            )
            early = seen < QUOTA
            push(inside & (early if stage == 0 else ~early), lead_id, partner_id)
            seen = seen + inside.astype(jnp.int32)
    if stage == 3:
        far_count = note[0, 2 * SLOTS].astype(jnp.int32)
        for e in range(SLOTS):
            lead_id, partner_id = far(e, 0), far(e, 1)
            push(
                (e < far_count)
                & (lead_id // ORB_DEV == here)
                & (partner_id // ORB_DEV == here),
                lead_id,
                partner_id,
            )
    if stage in (1, 2):
        far_count = note[0, 2 * SLOTS].astype(jnp.int32)
        left = jnp.where(is_left, here, across)
        right = jnp.where(is_left, across, here)
        entries = []
        load_left, load_right = jnp.int32(0), jnp.int32(0)
        for side in range(2):
            use_near = is_left if side == 0 else ~is_left
            other = right if side == 0 else left
            limit = jnp.where(use_near, count[0], far_count)
            for e in range(SLOTS):
                a = jnp.where(use_near, near(e, 0), far(e, 0))
                b = jnp.where(use_near, near(e, 1), far(e, 1))
                a_dev, b_dev = a // ORB_DEV, b // ORB_DEV
                on_left = (a_dev == left) | (b_dev == left)
                on_right = (a_dev == right) | (b_dev == right)
                crosses = (e < limit) & (
                    (a_dev == other) != (b_dev == other)
                )
                free = crosses & on_left & on_right
                fixed = crosses & ~free
                left_bit = jnp.where(a_dev == left, a, b) % ORB_DEV
                right_bit = jnp.where(a_dev == right, a, b) % ORB_DEV
                if side == 0:
                    load_left = load_left + fixed.astype(jnp.int32)
                else:
                    load_right = load_right + fixed.astype(jnp.int32)
                entries.append((side, a, b, free, fixed, left_bit, right_bit))
        for side, a, b, free, fixed, left_bit, right_bit in entries:
            go_left = (load_left < load_right) | (
                (load_left == load_right) & (right_bit <= left_bit)
            )
            load_left = load_left + (free & go_left).astype(jnp.int32)
            load_right = load_right + (free & ~go_left).astype(jnp.int32)
            at_left = (free & go_left) | (fixed if side == 0 else jnp.bool_(False))
            at_right = (free & ~go_left) | (fixed if side == 1 else jnp.bool_(False))
            mine = (at_left & is_left) | (at_right & ~is_left)
            bit = jnp.where(is_left, right_bit, left_bit)
            push(mine & (bit == stage - 1), a, b)

    total = work[0]
    sources = [own.at[0], own.at[1], mate.at[0], mate.at[1]]
    if stage in (1, 2):
        sources.append(remote)

    def window(buf):
        return shift.at[buf].reshape(SHIFT_PLANES, WIDE, BOX_Z).at[
            pl.ds(MARGIN, BOX_X), pl.ds(MARGIN, BOX_Y), :
        ]

    def fetch(k, buf):
        for which, target in ((0, lead.at[buf]), (1, window(buf))):
            slot = work[1 + 5 * k + which]
            for s, source in enumerate(sources):
                @pl.when(slot == s)
                def _():
                    pltpu.make_async_copy(source, target, sem.at[which, buf]).start()

    @pl.when(total > 0)
    def _():
        fetch(0, 0)
        for buf in (one, two, three):
            zero_borders(buf)
        zero_margins(shift.at[0])

        @pl.when(total > 1)
        def _():
            zero_margins(shift.at[1])

    if stage == 0:
        for slot in range(REMOTE + 1):
            zero_box(accum.at[slot])

    def visit(k, _):
        buf = k % 2
        pltpu.make_async_copy(sources[0], lead.at[buf], sem.at[0, buf]).wait()
        pltpu.make_async_copy(sources[0], window(buf), sem.at[1, buf]).wait()

        @pl.when(k + 1 < total)
        def _():
            fetch(k + 1, 1 - buf)

        base = 1 + 5 * k
        solve_pair(
            lead.at[buf], shift.at[buf], partner, (one, two, three), weights, values,
            [work[base + 2 + axis] for axis in range(3)], accum, work[base], work[base + 1],
        )
        return 0

    lax.fori_loop(0, total, visit, 0)

    if stage:
        boxes = accum.at[pl.ds(2, 2)] if stage == 3 else accum.at[REMOTE]
        copy = pltpu.make_async_copy(boxes, leaving, note_sem)
        copy.start()
        copy.wait()
    if stage == 1:
        @pl.when(total > 0)
        def _():
            zero_box(accum.at[REMOTE])


SMEM = pl.BlockSpec(memory_space=pltpu.SMEM)
VMEM = pl.BlockSpec(memory_space=pltpu.VMEM)
HBM = pl.BlockSpec(memory_space=pltpu.HBM)


def run_stage(stage, fixed, remote, accum):
    carried = [] if accum is None else [accum]
    operands = list(fixed) + list(remote) + carried
    specs = [SMEM] * 4 + [VMEM] * 2 + [HBM] * 2 + [HBM] * len(remote) + [VMEM] * len(carried)
    shapes = [jax.ShapeDtypeStruct((REMOTE + 1,) + BOX, F32)]
    outs = [VMEM]
    if stage:
        shapes.append(jax.ShapeDtypeStruct(((2,) if stage == 3 else ()) + BOX, F32))
        outs.append(VMEM)
    return pl.pallas_call(
        functools.partial(stage_kernel, stage),
        out_shape=shapes,
        in_specs=specs,
        out_specs=outs,
        input_output_aliases={len(operands) - 1: 0} if carried else {},
        scratch_shapes=[
            pltpu.VMEM((2,) + BOX, F32),
            pltpu.VMEM((2, SHIFT_ROWS, BOX_Z), F32),
            pltpu.VMEM(BOX, F32),
            pltpu.VMEM((STENCIL_ROWS, BOX_Z), F32),
            pltpu.VMEM((STENCIL_ROWS, BOX_Z), F32),
            pltpu.VMEM((STENCIL_ROWS, BOX_Z), F32),
            pltpu.SMEM((1 + 5 * 2 * SLOTS,), jnp.int32),
            pltpu.SMEM((8, BOX_Z), F32),
            pltpu.SemaphoreType.DMA((2, 2)),
            pltpu.SemaphoreType.DMA,
        ],
        compiler_params=pltpu.CompilerParams(vmem_limit_bytes=28 << 20),
        cost_estimate=pl.CostEstimate(
            flops=200_000_000, bytes_accessed=20_000_000, transcendentals=0
        ),
        name="stage_" + "abcd"[stage],
    )(*operands)


def total_kernel(box, accum, mate, remote, *rest):
    result, chunk, sem = rest[-3:]

    def add(x, _):
        for t in range(TILES):
            at = pl.ds(8 * t, 8)
            chunk[x, at, :] = accum[box, x, at, :] + mate[box, x, at, :] + remote[x, at, :]
        pltpu.make_async_copy(chunk.at[x], result.at[box, x], sem).start()
        return 0

    lax.fori_loop(0, BOX_X, add, 0, unroll=2)
    pltpu.make_async_copy(chunk, result.at[box], sem).wait()


def run_total(box, accum, mate, remote, result=None):
    operands = [accum, mate, remote]
    specs = [VMEM, VMEM, VMEM]
    aliases = {}
    if result is not None:
        operands.append(result)
        specs.append(HBM)
        aliases = {3: 0}
    return pl.pallas_call(
        functools.partial(total_kernel, box),
        out_shape=jax.ShapeDtypeStruct((ORB_DEV,) + BOX, F32),
        in_specs=specs,
        out_specs=HBM,
        input_output_aliases=aliases,
        scratch_shapes=[pltpu.VMEM(BOX, F32), pltpu.SemaphoreType.DMA],
        compiler_params=pltpu.CompilerParams(vmem_limit_bytes=4 << 20),
        name="total_" + "ab"[box],
    )(*operands)


def local(orbitals, pair_list, pair_count, box_offset):
    position = lax.axis_index("orb").astype(jnp.int32)[None]
    devices = lax.axis_size("orb")
    mates = [(d, d ^ 1) for d in range(devices)]
    across = [(d, d + 1) for d in range(1, devices - 1, 2)]
    across = across + [(b, a) for a, b in across]
    payload = pl.pallas_call(
        first_kernel,
        out_shape=jax.ShapeDtypeStruct((BOX_X + 1, BOX_Y, BOX_Z), F32),
        in_specs=[SMEM, SMEM, HBM],
        out_specs=VMEM,
        scratch_shapes=[pltpu.SemaphoreType.DMA],
        name="first_box",
    )(pair_list, pair_count, orbitals)
    payload, held = lax.optimization_barrier((payload, orbitals))
    far_first = lax.ppermute(payload, "orb", across)
    mate = lax.ppermute(held, "orb", mates)
    second = pl.pallas_call(
        second_kernel,
        out_shape=jax.ShapeDtypeStruct(BOX, F32),
        in_specs=[HBM],
        out_specs=VMEM,
        scratch_shapes=[pltpu.SemaphoreType.DMA],
        name="second_box",
    )(held)
    far_second = lax.ppermute(second, "orb", across)
    weights, values = sine_basis()
    fixed = (
        pair_list, pair_count, position, box_offset.reshape(-1),
        jnp.asarray(weights), jnp.asarray(values), orbitals, mate,
    )
    (accum,) = run_stage(0, fixed, (), None)
    accum, for_first = run_stage(1, fixed, (far_first,), accum)
    back_first = lax.ppermute(for_first, "orb", across)
    accum, for_second = run_stage(2, fixed, (far_first, far_second), accum)
    for_second, back_first, accum = lax.optimization_barrier((for_second, back_first, accum))
    back_second = lax.ppermute(for_second, "orb", across)
    accum, for_mate = run_stage(3, fixed, (far_first,), accum)
    back_mate = lax.ppermute(for_mate, "orb", mates)
    result = run_total(0, accum, back_mate, back_first)
    return run_total(1, accum, back_mate, back_second, result)


def solution(mesh):
    placed = (P("orb", None, None, None), P("orb", None, None), P("orb"), P())
    return jax.shard_map(
        local, mesh=mesh, in_specs=placed, out_specs=P("orb", None, None, None), check_vma=False
    )
```

```python
import functools

import jax
import jax.numpy as jnp
import ml_dtypes
import numpy as np
from jax import lax
from jax.experimental import pallas as pl
from jax.experimental.pallas import tpu as pltpu
from jax.sharding import PartitionSpec as P

BOX_X, BOX_Y, BOX_Z = 48, 64, 128
BOX = (BOX_X, BOX_Y, BOX_Z)
ORB_DEV = 2
SLOTS = 6
TILES = BOX_Y // 8
PLANE = BOX_Y + 8
STENCIL_ROWS = (BOX_X + 2) * PLANE + 8
MARGIN = 24
WIDE = BOX_Y + MARGIN
SHIFT_PLANES = BOX_X + 2
SHIFT_ROWS = SHIFT_PLANES * WIDE
STENCIL_UNROLL = 8
BLOCK = 24
CHUNKS = 6
F32 = jnp.float32
BF16 = jnp.bfloat16


def sine_basis():
    k = np.arange(1, BOX_Z + 1)
    basis = np.sqrt(2.0 / (BOX_Z + 1)) * np.sin(np.pi * np.outer(k, k) / (BOX_Z + 1))
    high = basis.astype(np.float32).astype(ml_dtypes.bfloat16)
    low = (basis - high.astype(np.float64)).astype(ml_dtypes.bfloat16)
    half = np.concatenate([high, low], 1)
    weights = np.concatenate([half, half], 0)
    values = np.tile(2.0 * np.cos(np.pi * k / (BOX_Z + 1)), (8, 1)).astype(np.float32)
    return weights, values


def stencil_row(x):
    return pl.multiple_of(8 + (x + 1) * PLANE, 8)


def shift_row(x):
    return pl.multiple_of((x + 1) * WIDE + MARGIN, 8)


def shifted_plane(x):
    return jnp.where((x >= 0) & (x < BOX_X), x + 1, 0) * WIDE + MARGIN


def zero_rows(ref, first, rows):
    for k in range(rows // 8):
        ref[pl.ds(first + 8 * k, 8), :] = jnp.zeros((8, BOX_Z), F32)


def zero_margins(ref):
    zero_rows(ref, 0, WIDE)
    zero_rows(ref, SHIFT_ROWS - WIDE, WIDE)

    def plane(p, _):
        zero_rows(ref, pl.multiple_of((p + 1) * WIDE, 8), MARGIN)
        return 0

    lax.fori_loop(0, BOX_X, plane, 0)


def zero_borders(ref):
    zero_rows(ref, 0, 8 + PLANE)
    zero_rows(ref, STENCIL_ROWS - PLANE, PLANE)

    def plane(x, _):
        zero_rows(ref, pl.multiple_of(8 + (x + 1) * PLANE + BOX_Y, 8), 8)
        return 0

    lax.fori_loop(0, BOX_X, plane, 0)


def zero_box(ref):
    def plane(x, _):
        for t in range(TILES):
            ref[x, pl.ds(8 * t, 8), :] = jnp.zeros((8, BOX_Z), F32)
        return 0

    lax.fori_loop(0, BOX_X, plane, 0, unroll=2)


def sweep(source, target, centre, other=None, factor=None):
    def plane(x, carry):
        behind, here = carry
        row = stencil_row(x)
        ahead_row = stencil_row(x + 1)
        ahead = [source[pl.ds(ahead_row + 8 * t, 8), :] for t in range(TILES)]
        for t in range(TILES):
            above = source[pl.ds(row + 8 * t - 1, 8), :]
            below = source[pl.ds(row + 8 * t + 1, 8), :]
            total = (behind[t] + ahead[t]) + (above + below) + centre * here[t]
            if other is not None:
                total = total + factor * other[pl.ds(row + 8 * t, 8), :]
            target[pl.ds(row + 8 * t, 8), :] = total
        return here, ahead

    first = [source[pl.ds(stencil_row(-1) + 8 * t, 8), :] for t in range(TILES)]
    second = [source[pl.ds(stencil_row(0) + 8 * t, 8), :] for t in range(TILES)]
    lax.fori_loop(0, BOX_X, plane, (first, second), unroll=STENCIL_UNROLL)


def along_z(rows, weights):
    high = rows.astype(BF16)
    low = (rows - high.astype(F32)).astype(BF16)
    product = jnp.dot(
        jnp.concatenate([high, low], 1), weights[...], preferred_element_type=F32
    )
    return product[:, :BOX_Z] + product[:, BOX_Z:]


def solve_pair(lead, shift, partner, bufs, weights, values, gap, accum, lead_slot, partner_slot):
    gap_x, gap_y, gap_z = gap
    lane = lax.broadcasted_iota(jnp.int32, (8, BOX_Z), 1)
    one, two, three = bufs
    centre = values[...]

    inside = (lane >= gap_z) & (lane < BOX_Z + gap_z)
    turn = jnp.where(gap_z < 0, gap_z + BOX_Z, gap_z)

    def density_block(block, _):
        parts = []
        for q in range(BLOCK):
            x = block * BLOCK + q
            base = shifted_plane(x - gap_x) - gap_y
            for t in range(TILES):
                value = shift[pl.ds(base + 8 * t, 8), :]
                value = jnp.where(inside, pltpu.roll(value, turn, 1), 0.0)
                partner[x, pl.ds(8 * t, 8), :] = value
                parts.append(value * lead[x, pl.ds(8 * t, 8), :])
        spectral = along_z(jnp.concatenate(parts, 0), weights)
        for q in range(BLOCK):
            row = stencil_row(block * BLOCK + q)
            one[pl.ds(row, BOX_Y), :] = spectral[q * BOX_Y : (q + 1) * BOX_Y]
        return 0

    lax.fori_loop(0, BOX_X // BLOCK, density_block, 0)

    sweep(one, three, centre + 6.0)
    sweep(three, one, centre)
    sweep(one, two, centre, three, 36.0)
    sweep(two, one, centre)
    sweep(one, three, centre, three, 1296.0)
    sweep(three, one, centre)
    sweep(one, two, centre)
    sweep(two, one, centre)
    sweep(one, two, centre)
    sweep(two, one, centre)
    sweep(one, two, centre, three, 46656.0)
    scale = 1.0 / (6.0 * 6.0 * 1296.0 * 46656.0)

    def potential_block(block, _):
        rows = jnp.concatenate(
            [two[pl.ds(stencil_row(block * BLOCK + q), BOX_Y), :] for q in range(BLOCK)], 0
        )
        potential = along_z(rows, weights) * scale
        for q in range(BLOCK):
            x = block * BLOCK + q
            for t in range(TILES):
                at = pl.ds(8 * t, 8)
                value = potential[q * BOX_Y + 8 * t : q * BOX_Y + 8 * t + 8]
                accum[lead_slot, x, at, :] = (
                    accum[lead_slot, x, at, :] + value * partner[x, at, :]
                )
                shift[pl.ds(shift_row(x) + 8 * t, 8), :] = value * lead[x, at, :]
        return 0

    lax.fori_loop(0, BOX_X // BLOCK, potential_block, 0)

    back_inside = (lane >= -gap_z) & (lane < BOX_Z - gap_z)
    back_turn = jnp.where(gap_z > 0, BOX_Z - gap_z, -gap_z)

    def back_block(block, _):
        for q in range(BLOCK):
            x = block * BLOCK + q
            base = shifted_plane(x + gap_x) + gap_y
            for t in range(TILES):
                at = pl.ds(8 * t, 8)
                value = shift[pl.ds(base + 8 * t, 8), :]
                value = jnp.where(back_inside, pltpu.roll(value, back_turn, 1), 0.0)
                accum[partner_slot, x, at, :] = accum[partner_slot, x, at, :] + value
        return 0

    lax.fori_loop(0, BOX_X // BLOCK, back_block, 0)


REMOTE = 4
QUOTA = 2
ROOM = 2


def forward_box(box, target, buf, arrived, left):
    planes = BOX_X // CHUNKS
    pieces = [pl.ds(c * planes, planes) for c in range(CHUNKS)]
    for c, at in enumerate(pieces):
        pltpu.make_async_copy(box.at[at], buf.at[at], arrived.at[c]).start()
    for c, at in enumerate(pieces):
        pltpu.make_async_copy(box.at[at], buf.at[at], arrived.at[c]).wait()
        pltpu.make_async_copy(buf.at[at], target.at[at], left.at[c]).start()
    for c, at in enumerate(pieces):
        pltpu.make_async_copy(buf.at[at], target.at[at], left.at[c]).wait()


def first_kernel(row, count, own, payload, note, note_sem, buf, arrived, left):
    lane = lax.broadcasted_iota(jnp.int32, (8, BOX_Z), 1)
    value = jnp.where(lane == 2 * SLOTS, count[0].astype(F32), 0.0)
    for e in range(SLOTS):
        for k in range(2):
            value = jnp.where(lane == 2 * e + k, row[0, k, e].astype(F32), value)
    note[...] = jnp.zeros_like(note)
    note[0:8, :] = value
    extra = pltpu.make_async_copy(note, payload.at[BOX_X], note_sem)
    extra.start()
    forward_box(own.at[0], payload, buf, arrived, left)
    extra.wait()


def second_kernel(own, target, buf, arrived, left):
    forward_box(own.at[1], target, buf, arrived, left)


def stage_kernel(stage, row, count, position, offsets, weights, values, own, mate, *rest):
    if stage == 0:
        (accum, *rest) = rest
    elif stage == 1:
        (payload, _, accum, leaving, *rest) = rest
        remote = payload.at[pl.ds(0, BOX_X)]
    else:
        (payload, remote, _, accum, leaving, leaving_mate, *rest) = rest
    lead, shift, partner, one, two, three, work, note, sem, note_sem = rest
    here = position[0]
    mate_id = here ^ 1
    is_left = here % 2 == 1
    across = jnp.where(is_left, here + 1, here - 1)

    if stage:
        copy = pltpu.make_async_copy(payload.at[BOX_X, pl.ds(0, 8), :], note, note_sem)
        copy.start()
        copy.wait()

    def near(e, k):
        return row[0, k, e]

    def far(e, k):
        return note[0, 2 * e + k].astype(jnp.int32)

    def place(orbital):
        device = orbital // ORB_DEV
        local_slot = orbital % ORB_DEV
        return jnp.where(
            device == here, local_slot, jnp.where(device == mate_id, 2 + local_slot, REMOTE)
        )

    work[0] = 0

    def push(wanted, lead_id, partner_id):
        @pl.when(wanted)
        def _():
            k = work[0]
            base = 1 + 5 * k
            work[0] = k + 1
            work[base] = place(lead_id)
            work[base + 1] = place(partner_id)
            for axis in range(3):
                work[base + 2 + axis] = offsets[3 * partner_id + axis] - offsets[3 * lead_id + axis]

    inner = []
    seen = jnp.int32(0)
    for e in range(SLOTS):
        lead_id, partner_id = near(e, 0), near(e, 1)
        inside = (
            (e < count[0])
            & (lead_id // ORB_DEV != across)
            & (partner_id // ORB_DEV != across)
        )
        inner.append((inside, seen - QUOTA, lead_id, partner_id))
        seen = seen + inside.astype(jnp.int32)
    if stage == 0:
        for inside, order, lead_id, partner_id in inner:
            push(inside & (order < 0), lead_id, partner_id)
    else:
        seen = jnp.maximum(seen - QUOTA, 0)
        inner = [(inside & (order >= 0), order, a, b) for inside, order, a, b in inner]
        far_count = note[0, 2 * SLOTS].astype(jnp.int32)
        for e in range(SLOTS):
            lead_id, partner_id = far(e, 0), far(e, 1)
            inside = (
                (e < far_count)
                & (lead_id // ORB_DEV == here)
                & (partner_id // ORB_DEV == here)
            )
            inner.append((inside, seen, lead_id, partner_id))
            seen = seen + inside.astype(jnp.int32)
    if stage:
        firsts = jnp.int32(0)
        left = jnp.where(is_left, here, across)
        right = jnp.where(is_left, across, here)
        entries = []
        load_left, load_right = jnp.int32(0), jnp.int32(0)
        for side in range(2):
            use_near = is_left if side == 0 else ~is_left
            other = right if side == 0 else left
            limit = jnp.where(use_near, count[0], far_count)
            for e in range(SLOTS):
                a = jnp.where(use_near, near(e, 0), far(e, 0))
                b = jnp.where(use_near, near(e, 1), far(e, 1))
                a_dev, b_dev = a // ORB_DEV, b // ORB_DEV
                on_left = (a_dev == left) | (b_dev == left)
                on_right = (a_dev == right) | (b_dev == right)
                crosses = (e < limit) & (
                    (a_dev == other) != (b_dev == other)
                )
                free = crosses & on_left & on_right
                fixed = crosses & ~free
                left_bit = jnp.where(a_dev == left, a, b) % ORB_DEV
                right_bit = jnp.where(a_dev == right, a, b) % ORB_DEV
                if side == 0:
                    load_left = load_left + fixed.astype(jnp.int32)
                else:
                    load_right = load_right + fixed.astype(jnp.int32)
                entries.append((side, a, b, free, fixed, left_bit, right_bit))
        for side, a, b, free, fixed, left_bit, right_bit in entries:
            go_left = (load_left < load_right) | (
                (load_left == load_right) & (right_bit <= left_bit)
            )
            load_left = load_left + (free & go_left).astype(jnp.int32)
            load_right = load_right + (free & ~go_left).astype(jnp.int32)
            at_left = (free & go_left) | (fixed if side == 0 else jnp.bool_(False))
            at_right = (free & ~go_left) | (fixed if side == 1 else jnp.bool_(False))
            mine = (at_left & is_left) | (at_right & ~is_left)
            bit = jnp.where(is_left, right_bit, left_bit)
            firsts = firsts + (mine & (bit == 0)).astype(jnp.int32)
            push(mine & (bit == stage - 1), a, b)
        for inside, order, a, b in inner:
            soon = order < ROOM - firsts
            push(inside & (soon if stage == 1 else ~soon), a, b)

    total = work[0]
    sources = [own.at[0], own.at[1], mate.at[0], mate.at[1]]
    if stage:
        sources.append(remote)

    def window(buf):
        return shift.at[buf].reshape(SHIFT_PLANES, WIDE, BOX_Z).at[
            pl.ds(1, BOX_X), pl.ds(MARGIN, BOX_Y), :
        ]

    def fetch(k, buf):
        for which, target in ((0, lead.at[buf]), (1, window(buf))):
            slot = work[1 + 5 * k + which]
            for s, source in enumerate(sources):
                @pl.when(slot == s)
                def _():
                    pltpu.make_async_copy(source, target, sem.at[which, buf]).start()

    @pl.when(total > 0)
    def _():
        fetch(0, 0)
        for buf in (one, two, three):
            zero_borders(buf)
        zero_margins(shift.at[0])

        @pl.when(total > 1)
        def _():
            zero_margins(shift.at[1])

    if stage == 0:
        for slot in range(REMOTE + 1):
            zero_box(accum.at[slot])

    def visit(k, _):
        buf = k % 2
        pltpu.make_async_copy(sources[0], lead.at[buf], sem.at[0, buf]).wait()
        pltpu.make_async_copy(sources[0], window(buf), sem.at[1, buf]).wait()

        @pl.when(k + 1 < total)
        def _():
            fetch(k + 1, 1 - buf)

        base = 1 + 5 * k
        solve_pair(
            lead.at[buf], shift.at[buf], partner, (one, two, three), weights, values,
            [work[base + 2 + axis] for axis in range(3)], accum, work[base], work[base + 1],
        )
        return 0

    lax.fori_loop(0, total, visit, 0)

    if stage:
        def leave(x, _):
            for t in range(TILES):
                at = pl.ds(8 * t, 8)
                leaving[x, at, :] = accum[REMOTE, x, at, :]
                if stage == 1:
                    accum[REMOTE, x, at, :] = jnp.zeros((8, BOX_Z), F32)
                else:
                    for box in range(ORB_DEV):
                        leaving_mate[box, x, at, :] = accum[2 + box, x, at, :]
            return 0

        lax.fori_loop(0, BOX_X, leave, 0, unroll=2)


SMEM = pl.BlockSpec(memory_space=pltpu.SMEM)
VMEM = pl.BlockSpec(memory_space=pltpu.VMEM)
HBM = pl.BlockSpec(memory_space=pltpu.HBM)


def run_stage(stage, fixed, remote, accum):
    carried = [] if accum is None else [accum]
    operands = list(fixed) + list(remote) + carried
    specs = [SMEM] * 4 + [VMEM] * 2 + [HBM] * 2 + [HBM] * len(remote) + [VMEM] * len(carried)
    shapes = [jax.ShapeDtypeStruct((REMOTE + 1,) + BOX, F32)]
    outs = [VMEM]
    if stage:
        shapes += [jax.ShapeDtypeStruct(shape + BOX, F32) for shape in ((), (2,))[:stage]]
        outs += [VMEM] * stage
    return pl.pallas_call(
        functools.partial(stage_kernel, stage),
        out_shape=shapes,
        in_specs=specs,
        out_specs=outs,
        input_output_aliases={len(operands) - 1: 0} if carried else {},
        scratch_shapes=[
            pltpu.VMEM((2,) + BOX, F32),
            pltpu.VMEM((2, SHIFT_ROWS, BOX_Z), F32),
            pltpu.VMEM(BOX, F32),
            pltpu.VMEM((STENCIL_ROWS, BOX_Z), F32),
            pltpu.VMEM((STENCIL_ROWS, BOX_Z), F32),
            pltpu.VMEM((STENCIL_ROWS, BOX_Z), F32),
            pltpu.SMEM((1 + 5 * 2 * SLOTS,), jnp.int32),
            pltpu.SMEM((8, BOX_Z), F32),
            pltpu.SemaphoreType.DMA((2, 2)),
            pltpu.SemaphoreType.DMA,
        ],
        compiler_params=pltpu.CompilerParams(vmem_limit_bytes=28 << 20),
        cost_estimate=pl.CostEstimate(
            flops=200_000_000, bytes_accessed=20_000_000, transcendentals=0
        ),
        name="stage_" + "abc"[stage],
    )(*operands)


def total_kernel(box, accum, mate, remote, *rest):
    result, chunk, sem = rest[-3:]

    def add(x, _):
        for t in range(TILES):
            at = pl.ds(8 * t, 8)
            chunk[x, at, :] = accum[box, x, at, :] + mate[box, x, at, :] + remote[x, at, :]
        pltpu.make_async_copy(chunk.at[x], result.at[box, x], sem).start()
        return 0

    lax.fori_loop(0, BOX_X, add, 0, unroll=2)
    pltpu.make_async_copy(chunk, result.at[box], sem).wait()


def run_total(box, accum, mate, remote, result=()):
    return pl.pallas_call(
        functools.partial(total_kernel, box),
        out_shape=jax.ShapeDtypeStruct((ORB_DEV,) + BOX, F32),
        in_specs=[VMEM, VMEM, VMEM] + [HBM] * len(result),
        out_specs=HBM,
        input_output_aliases={3: 0} if result else {},
        scratch_shapes=[pltpu.VMEM(BOX, F32), pltpu.SemaphoreType.DMA],
        compiler_params=pltpu.CompilerParams(vmem_limit_bytes=4 << 20),
        name="total_" + "ab"[box],
    )(accum, mate, remote, *result)


def local(orbitals, pair_list, pair_count, box_offset):
    position = lax.axis_index("orb").astype(jnp.int32)[None]
    pair_list = jnp.transpose(pair_list, (0, 2, 1))
    devices = lax.axis_size("orb")
    mates = [(d, d ^ 1) for d in range(devices)]
    across = [(d, d + 1) for d in range(1, devices - 1, 2)]
    across = across + [(b, a) for a, b in across]
    staging = [
        pltpu.VMEM(BOX, F32),
        pltpu.SemaphoreType.DMA((CHUNKS,)),
        pltpu.SemaphoreType.DMA((CHUNKS,)),
    ]
    payload = pl.pallas_call(
        first_kernel,
        out_shape=jax.ShapeDtypeStruct((BOX_X + 1, BOX_Y, BOX_Z), F32),
        in_specs=[SMEM, SMEM, HBM],
        out_specs=HBM,
        scratch_shapes=[pltpu.VMEM((BOX_Y, BOX_Z), F32), pltpu.SemaphoreType.DMA] + staging,
        compiler_params=pltpu.CompilerParams(vmem_limit_bytes=3 << 20),
        name="first_box",
    )(pair_list, pair_count, orbitals)
    payload, held = lax.optimization_barrier((payload, orbitals))
    far_first = lax.ppermute(payload, "orb", across)
    mate = lax.ppermute(held, "orb", mates)
    second = pl.pallas_call(
        second_kernel,
        out_shape=jax.ShapeDtypeStruct(BOX, F32),
        in_specs=[HBM],
        out_specs=HBM,
        scratch_shapes=staging,
        compiler_params=pltpu.CompilerParams(vmem_limit_bytes=3 << 20),
        name="second_box",
    )(held)
    far_second = lax.ppermute(second, "orb", across)
    weights, values = sine_basis()
    fixed = (
        pair_list, pair_count, position, box_offset.reshape(-1),
        jnp.asarray(weights), jnp.asarray(values), orbitals, mate,
    )
    (accum,) = run_stage(0, fixed, (), None)
    accum, for_first = run_stage(1, fixed, (far_first,), accum)
    back_first = lax.ppermute(for_first, "orb", across)
    accum, for_second, for_mate = run_stage(2, fixed, (far_first, far_second), accum)
    for_second, back_first = lax.optimization_barrier((for_second, back_first))
    back_second = lax.ppermute(for_second, "orb", across)
    back_mate = lax.ppermute(for_mate, "orb", mates)
    result = run_total(0, accum, back_mate, back_first)
    return run_total(1, accum, back_mate, back_second, (result,))


def solution(mesh):
    placed = (P("orb", None, None, None), P("orb", None, None), P("orb"), P())
    return jax.shard_map(
        local, mesh=mesh, in_specs=placed, out_specs=P("orb", None, None, None), check_vma=False
    )
```

```python
import functools

import jax
import jax.numpy as jnp
import ml_dtypes
import numpy as np
from jax import lax
from jax.experimental import pallas as pl
from jax.experimental.pallas import tpu as pltpu
from jax.sharding import PartitionSpec as P

BOX_X, BOX_Y, BOX_Z = 48, 64, 128
BOX = (BOX_X, BOX_Y, BOX_Z)
ROWS = BOX_X * BOX_Y
ORB_DEV = 2
SLOTS = 6
TILES = BOX_Y // 8
PLANE = BOX_Y + 8
STENCIL_ROWS = (BOX_X + 2) * PLANE + 8
MARGIN = 24
WIDE = BOX_Y + MARGIN
SHIFT_PLANES = BOX_X + 2
SHIFT_ROWS = SHIFT_PLANES * WIDE
STENCIL_UNROLL = 8
BLOCK = 24
CHUNKS = 6
F32 = jnp.float32
BF16 = jnp.bfloat16


def sine_basis():
    k = np.arange(1, BOX_Z + 1)
    basis = np.sqrt(2.0 / (BOX_Z + 1)) * np.sin(np.pi * np.outer(k, k) / (BOX_Z + 1))
    high = basis.astype(np.float32).astype(ml_dtypes.bfloat16)
    low = (basis - high.astype(np.float64)).astype(ml_dtypes.bfloat16)
    half = np.concatenate([high, low], 1)
    weights = np.concatenate([half, half], 0)
    values = np.tile(2.0 * np.cos(np.pi * k / (BOX_Z + 1)), (8, 1)).astype(np.float32)
    return weights, values


def stencil_row(x):
    return pl.multiple_of(8 + (x + 1) * PLANE, 8)


def shift_row(x):
    return pl.multiple_of((x + 1) * WIDE + MARGIN, 8)


def shifted_plane(x):
    return jnp.where((x >= 0) & (x < BOX_X), x + 1, 0) * WIDE + MARGIN


def zero_rows(ref, first, rows):
    for k in range(rows // 8):
        ref[pl.ds(first + 8 * k, 8), :] = jnp.zeros((8, BOX_Z), F32)


def zero_margins(ref):
    zero_rows(ref, 0, WIDE)
    zero_rows(ref, SHIFT_ROWS - WIDE, WIDE)

    def plane(p, _):
        zero_rows(ref, pl.multiple_of((p + 1) * WIDE, 8), MARGIN)
        return 0

    lax.fori_loop(0, BOX_X, plane, 0, unroll=8)


def zero_borders(ref):
    zero_rows(ref, 0, 8 + PLANE)
    zero_rows(ref, STENCIL_ROWS - PLANE, PLANE)

    def plane(x, _):
        zero_rows(ref, pl.multiple_of(8 + (x + 1) * PLANE + BOX_Y, 8), 8)
        return 0

    lax.fori_loop(0, BOX_X, plane, 0, unroll=16)


def zero_box(ref):
    def plane(x, _):
        for t in range(TILES):
            ref[x, pl.ds(8 * t, 8), :] = jnp.zeros((8, BOX_Z), F32)
        return 0

    lax.fori_loop(0, BOX_X, plane, 0, unroll=2)


def sweep(source, target, centre, other=None, factor=None):
    def plane(x, carry):
        behind, here = carry
        row = stencil_row(x)
        ahead_row = stencil_row(x + 1)
        ahead = [source[pl.ds(ahead_row + 8 * t, 8), :] for t in range(TILES)]
        for t in range(TILES):
            above = source[pl.ds(row + 8 * t - 1, 8), :]
            below = source[pl.ds(row + 8 * t + 1, 8), :]
            total = (behind[t] + ahead[t]) + (above + below) + centre * here[t]
            if other is not None:
                total = total + factor * other[pl.ds(row + 8 * t, 8), :]
            target[pl.ds(row + 8 * t, 8), :] = total
        return here, ahead

    first = [source[pl.ds(stencil_row(-1) + 8 * t, 8), :] for t in range(TILES)]
    second = [source[pl.ds(stencil_row(0) + 8 * t, 8), :] for t in range(TILES)]
    lax.fori_loop(0, BOX_X, plane, (first, second), unroll=STENCIL_UNROLL)


def along_z(rows, weights):
    high = rows.astype(BF16)
    low = (rows - high.astype(F32)).astype(BF16)
    product = jnp.dot(
        jnp.concatenate([high, low], 1), weights[...], preferred_element_type=F32
    )
    return product[:, :BOX_Z] + product[:, BOX_Z:]


def solve_pair(lead, shift, partner, bufs, weights, values, gap, accum, lead_slot, partner_slot):
    gap_x, gap_y, gap_z = gap
    lane = lax.broadcasted_iota(jnp.int32, (8, BOX_Z), 1)
    one, two, three = bufs
    centre = values[...]

    inside = (lane >= gap_z) & (lane < BOX_Z + gap_z)
    turn = jnp.where(gap_z < 0, gap_z + BOX_Z, gap_z)

    def density_block(block, _):
        parts = []
        for q in range(BLOCK):
            x = block * BLOCK + q
            base = shifted_plane(x - gap_x) - gap_y
            for t in range(TILES):
                value = shift[pl.ds(base + 8 * t, 8), :]
                value = jnp.where(inside, pltpu.roll(value, turn, 1), 0.0)
                partner[x, pl.ds(8 * t, 8), :] = value
                parts.append(value * lead[x, pl.ds(8 * t, 8), :])
        spectral = along_z(jnp.concatenate(parts, 0), weights)
        for q in range(BLOCK):
            row = stencil_row(block * BLOCK + q)
            one[pl.ds(row, BOX_Y), :] = spectral[q * BOX_Y : (q + 1) * BOX_Y]
        return 0

    lax.fori_loop(0, BOX_X // BLOCK, density_block, 0)

    sweep(one, three, centre + 6.0)
    sweep(three, one, centre)
    sweep(one, two, centre, three, 36.0)
    sweep(two, one, centre)
    sweep(one, three, centre, three, 1296.0)
    sweep(three, one, centre)
    sweep(one, two, centre)
    sweep(two, one, centre)
    sweep(one, two, centre)
    sweep(two, one, centre)
    sweep(one, two, centre, three, 46656.0)
    scale = 1.0 / (6.0 * 6.0 * 1296.0 * 46656.0)

    def potential_block(block, _):
        rows = jnp.concatenate(
            [two[pl.ds(stencil_row(block * BLOCK + q), BOX_Y), :] for q in range(BLOCK)], 0
        )
        potential = along_z(rows, weights) * scale
        for q in range(BLOCK):
            x = block * BLOCK + q
            for t in range(TILES):
                at = pl.ds(8 * t, 8)
                value = potential[q * BOX_Y + 8 * t : q * BOX_Y + 8 * t + 8]
                accum[lead_slot, x, at, :] = (
                    accum[lead_slot, x, at, :] + value * partner[x, at, :]
                )
                shift[pl.ds(shift_row(x) + 8 * t, 8), :] = value * lead[x, at, :]
        return 0

    lax.fori_loop(0, BOX_X // BLOCK, potential_block, 0)

    back_inside = (lane >= -gap_z) & (lane < BOX_Z - gap_z)
    back_turn = jnp.where(gap_z > 0, BOX_Z - gap_z, -gap_z)

    def back_block(block, _):
        for q in range(BLOCK):
            x = block * BLOCK + q
            base = shifted_plane(x + gap_x) + gap_y
            for t in range(TILES):
                at = pl.ds(8 * t, 8)
                value = shift[pl.ds(base + 8 * t, 8), :]
                value = jnp.where(back_inside, pltpu.roll(value, back_turn, 1), 0.0)
                accum[partner_slot, x, at, :] = accum[partner_slot, x, at, :] + value
        return 0

    lax.fori_loop(0, BOX_X // BLOCK, back_block, 0)


REMOTE = 4
QUOTA = 2
ROOM = 2


PIECES = [pl.ds(c * (BOX_X // CHUNKS), BOX_X // CHUNKS) for c in range(CHUNKS)]


def start_box(box, buf, arrived):
    for c, at in enumerate(PIECES):
        pltpu.make_async_copy(box.at[at], buf.at[at], arrived.at[c]).start()


def finish_box(box, target, buf, arrived, left):
    for c, at in enumerate(PIECES):
        pltpu.make_async_copy(box.at[at], buf.at[at], arrived.at[c]).wait()
        pltpu.make_async_copy(buf.at[at], target.at[at], left.at[c]).start()
    for c, at in enumerate(PIECES):
        pltpu.make_async_copy(buf.at[at], target.at[at], left.at[c]).wait()


def first_kernel(listed, count, own, payload, row, note, note_sem, buf, arrived, left):
    start_box(own.at[0], buf, arrived)
    copy = pltpu.make_async_copy(listed, row, note_sem)
    copy.start()
    copy.wait()
    lane = lax.broadcasted_iota(jnp.int32, (8, BOX_Z), 1)
    value = jnp.where(lane == 2 * SLOTS, count[0].astype(F32), 0.0)
    for e in range(SLOTS):
        for k in range(2):
            value = jnp.where(lane == 2 * e + k, row[0, k, e].astype(F32), value)
    note[...] = jnp.zeros_like(note)
    note[0:8, :] = value
    extra = pltpu.make_async_copy(note, payload.at[BOX_X], note_sem)
    extra.start()
    finish_box(own.at[0], payload, buf, arrived, left)
    extra.wait()


def second_kernel(own, target, buf, arrived, left):
    start_box(own.at[1], buf, arrived)
    finish_box(own.at[1], target, buf, arrived, left)


def stage_kernel(stage, row, count, position, offsets, weights, values, own, mate, *rest):
    if stage == 0:
        (accum, *rest) = rest
    elif stage == 1:
        (payload, _, accum, leaving, *rest) = rest
        remote = payload.at[pl.ds(0, BOX_X)]
    else:
        (payload, remote, _, accum, leaving, mate_first, mate_second, *rest) = rest
        leaving_mate = (mate_first, mate_second)
    lead, shift, partner, one, two, three, work, note, far_row, sem, note_sem = rest
    here = position[0]
    mate_id = here ^ 1
    is_left = here % 2 == 1
    across = jnp.where(is_left, here + 1, here - 1)

    def clear():
        for buf in (one, two, three):
            zero_borders(buf)
        for buf in range(2):
            zero_margins(shift.at[buf])

    if stage:
        copy = pltpu.make_async_copy(payload.at[BOX_X, pl.ds(0, 8), :], note, note_sem)
        copy.start()
        clear()
        copy.wait()
        for k in range(2 * SLOTS + 1):
            far_row[k] = note[0, k].astype(jnp.int32)

    def near(e, k):
        return row[0, k, e]

    def far(e, k):
        return far_row[2 * e + k]

    def place(orbital):
        device = orbital // ORB_DEV
        local_slot = orbital % ORB_DEV
        return jnp.where(
            device == here, local_slot, jnp.where(device == mate_id, 2 + local_slot, REMOTE)
        )

    work[0] = 0

    def push(wanted, lead_id, partner_id):
        @pl.when(wanted)
        def _():
            k = work[0]
            base = 1 + 5 * k
            work[0] = k + 1
            work[base] = place(lead_id)
            work[base + 1] = place(partner_id)
            for axis in range(3):
                work[base + 2 + axis] = offsets[3 * partner_id + axis] - offsets[3 * lead_id + axis]

    inner = []
    seen = jnp.int32(0)
    for e in range(SLOTS):
        lead_id, partner_id = near(e, 0), near(e, 1)
        inside = (
            (e < count[0])
            & (lead_id // ORB_DEV != across)
            & (partner_id // ORB_DEV != across)
        )
        inner.append((inside, seen - QUOTA, lead_id, partner_id))
        seen = seen + inside.astype(jnp.int32)
    if stage == 0:
        for inside, order, lead_id, partner_id in inner:
            push(inside & (order < 0), lead_id, partner_id)
    else:
        seen = jnp.maximum(seen - QUOTA, 0)
        inner = [(inside & (order >= 0), order, a, b) for inside, order, a, b in inner]
        far_count = far_row[2 * SLOTS]
        for e in range(SLOTS):
            lead_id, partner_id = far(e, 0), far(e, 1)
            inside = (
                (e < far_count)
                & (lead_id // ORB_DEV == here)
                & (partner_id // ORB_DEV == here)
            )
            inner.append((inside, seen, lead_id, partner_id))
            seen = seen + inside.astype(jnp.int32)
    if stage:
        firsts = jnp.int32(0)
        left = jnp.where(is_left, here, across)
        right = jnp.where(is_left, across, here)
        entries = []
        load_left, load_right = jnp.int32(0), jnp.int32(0)
        for side in range(2):
            use_near = is_left if side == 0 else ~is_left
            other = right if side == 0 else left
            limit = jnp.where(use_near, count[0], far_count)
            for e in range(SLOTS):
                a = jnp.where(use_near, near(e, 0), far(e, 0))
                b = jnp.where(use_near, near(e, 1), far(e, 1))
                a_dev, b_dev = a // ORB_DEV, b // ORB_DEV
                on_left = (a_dev == left) | (b_dev == left)
                on_right = (a_dev == right) | (b_dev == right)
                crosses = (e < limit) & (
                    (a_dev == other) != (b_dev == other)
                )
                free = crosses & on_left & on_right
                fixed = crosses & ~free
                left_bit = jnp.where(a_dev == left, a, b) % ORB_DEV
                right_bit = jnp.where(a_dev == right, a, b) % ORB_DEV
                if side == 0:
                    load_left = load_left + fixed.astype(jnp.int32)
                else:
                    load_right = load_right + fixed.astype(jnp.int32)
                entries.append((side, a, b, free, fixed, left_bit, right_bit))
        for side, a, b, free, fixed, left_bit, right_bit in entries:
            go_left = (load_left < load_right) | (
                (load_left == load_right) & (right_bit <= left_bit)
            )
            load_left = load_left + (free & go_left).astype(jnp.int32)
            load_right = load_right + (free & ~go_left).astype(jnp.int32)
            at_left = (free & go_left) | (fixed if side == 0 else jnp.bool_(False))
            at_right = (free & ~go_left) | (fixed if side == 1 else jnp.bool_(False))
            mine = (at_left & is_left) | (at_right & ~is_left)
            bit = jnp.where(is_left, right_bit, left_bit)
            firsts = firsts + (mine & (bit == 0)).astype(jnp.int32)
            push(mine & (bit == stage - 1), a, b)
        for inside, order, a, b in inner:
            soon = order < ROOM - firsts
            push(inside & (soon if stage == 1 else ~soon), a, b)

    total = work[0]
    sources = [own.at[0], own.at[1], mate.at[0], mate.at[1]]
    if stage:
        sources.append(remote)

    def window(buf):
        return shift.at[buf].reshape(SHIFT_PLANES, WIDE, BOX_Z).at[
            pl.ds(1, BOX_X), pl.ds(MARGIN, BOX_Y), :
        ]

    def fetch(k, buf):
        for which, target in ((0, lead.at[buf]), (1, window(buf))):
            slot = work[1 + 5 * k + which]
            for s, source in enumerate(sources):
                @pl.when(slot == s)
                def _():
                    for at in PIECES:
                        pltpu.make_async_copy(
                            source.at[at], target.at[at], sem.at[which, buf]
                        ).start()

    @pl.when(total > 0)
    def _():
        fetch(0, 0)

    if stage == 0:
        clear()
        for slot in range(REMOTE + 1):
            zero_box(accum.at[slot])

    def visit(k, _):
        buf = k % 2
        pltpu.make_async_copy(sources[0], lead.at[buf], sem.at[0, buf]).wait()
        pltpu.make_async_copy(sources[0], window(buf), sem.at[1, buf]).wait()

        @pl.when(k + 1 < total)
        def _():
            fetch(k + 1, 1 - buf)

        base = 1 + 5 * k
        solve_pair(
            lead.at[buf], shift.at[buf], partner, (one, two, three), weights, values,
            [work[base + 2 + axis] for axis in range(3)], accum, work[base], work[base + 1],
        )
        return 0

    lax.fori_loop(0, total, visit, 0)

    if stage:
        def leave(x, _):
            for t in range(TILES):
                at = pl.ds(8 * t, 8)
                leaving[pl.ds(pl.multiple_of(x * BOX_Y + 8 * t, 8), 8), :] = accum[REMOTE, x, at, :]
                if stage == 1:
                    accum[REMOTE, x, at, :] = jnp.zeros((8, BOX_Z), F32)
                else:
                    for box in range(ORB_DEV):
                        leaving_mate[box][x, at, :] = accum[2 + box, x, at, :]
            return 0

        lax.fori_loop(0, BOX_X, leave, 0, unroll=2)
        zero_rows(leaving, ROWS, leaving.shape[0] - ROWS)


SMEM = pl.BlockSpec(memory_space=pltpu.SMEM)
VMEM = pl.BlockSpec(memory_space=pltpu.VMEM)
HBM = pl.BlockSpec(memory_space=pltpu.HBM)


def run_stage(stage, fixed, remote, accum):
    carried = [] if accum is None else [accum]
    operands = list(fixed) + list(remote) + carried
    specs = [SMEM] * 4 + [VMEM] * 2 + [HBM] * 2 + [HBM] * len(remote) + [VMEM] * len(carried)
    shapes = [jax.ShapeDtypeStruct((REMOTE + 1,) + BOX, F32)]
    outs = [VMEM]
    if stage:
        leaving = [(ROWS + 16, BOX_Z)] if stage == 1 else [(ROWS + 8, BOX_Z), BOX, BOX]
        shapes += [jax.ShapeDtypeStruct(shape, F32) for shape in leaving]
        outs += [VMEM] * len(leaving)
    return pl.pallas_call(
        functools.partial(stage_kernel, stage),
        out_shape=shapes,
        in_specs=specs,
        out_specs=outs,
        input_output_aliases={len(operands) - 1: 0} if carried else {},
        scratch_shapes=[
            pltpu.VMEM((2,) + BOX, F32),
            pltpu.VMEM((2, SHIFT_ROWS, BOX_Z), F32),
            pltpu.VMEM(BOX, F32),
            pltpu.VMEM((STENCIL_ROWS, BOX_Z), F32),
            pltpu.VMEM((STENCIL_ROWS, BOX_Z), F32),
            pltpu.VMEM((STENCIL_ROWS, BOX_Z), F32),
            pltpu.SMEM((1 + 5 * 2 * SLOTS,), jnp.int32),
            pltpu.SMEM((8, BOX_Z), F32),
            pltpu.SMEM((2 * SLOTS + 1,), jnp.int32),
            pltpu.SemaphoreType.DMA((2, 2)),
            pltpu.SemaphoreType.DMA,
        ],
        compiler_params=pltpu.CompilerParams(vmem_limit_bytes=28 << 20),
        cost_estimate=pl.CostEstimate(
            flops=200_000_000, bytes_accessed=20_000_000, transcendentals=0
        ),
        name="stage_" + "abc"[stage],
    )(*operands)


def total_kernel(box, accum, mate, remote, *rest):
    result, chunk, sem = rest[-3:]

    def add(x, _):
        for t in range(TILES):
            at = pl.ds(8 * t, 8)
            far = remote[pl.ds(pl.multiple_of(x * BOX_Y + 8 * t, 8), 8), :]
            chunk[x, at, :] = accum[box, x, at, :] + mate[x, at, :] + far
        pltpu.make_async_copy(chunk.at[x], result.at[box, x], sem).start()
        return 0

    lax.fori_loop(0, BOX_X, add, 0, unroll=2)
    pltpu.make_async_copy(chunk, result.at[box], sem).wait()


def run_total(box, accum, mate, remote, result=()):
    return pl.pallas_call(
        functools.partial(total_kernel, box),
        out_shape=jax.ShapeDtypeStruct((ORB_DEV,) + BOX, F32),
        in_specs=[VMEM, VMEM, VMEM] + [HBM] * len(result),
        out_specs=HBM,
        input_output_aliases={3: 0} if result else {},
        scratch_shapes=[pltpu.VMEM(BOX, F32), pltpu.SemaphoreType.DMA],
        compiler_params=pltpu.CompilerParams(vmem_limit_bytes=4 << 20),
        name="total_" + "ab"[box],
    )(accum, mate, remote, *result)


def local(orbitals, pair_list, pair_count, box_offset):
    position = lax.axis_index("orb").astype(jnp.int32)[None]
    pair_list = jnp.transpose(pair_list, (0, 2, 1))
    devices = lax.axis_size("orb")
    mates = [(d, d ^ 1) for d in range(devices)]
    across = [(d, d + 1) for d in range(1, devices - 1, 2)]
    across = across + [(b, a) for a, b in across]
    staging = [
        pltpu.VMEM(BOX, F32),
        pltpu.SemaphoreType.DMA((CHUNKS,)),
        pltpu.SemaphoreType.DMA((CHUNKS,)),
    ]
    payload = pl.pallas_call(
        first_kernel,
        out_shape=jax.ShapeDtypeStruct((BOX_X + 1, BOX_Y, BOX_Z), F32),
        in_specs=[HBM, SMEM, HBM],
        out_specs=HBM,
        scratch_shapes=[
            pltpu.SMEM((1, 2, SLOTS), jnp.int32),
            pltpu.VMEM((BOX_Y, BOX_Z), F32),
            pltpu.SemaphoreType.DMA,
        ]
        + staging,
        compiler_params=pltpu.CompilerParams(vmem_limit_bytes=3 << 20),
        name="first_box",
    )(pair_list, pair_count, orbitals)
    payload, held = lax.optimization_barrier((payload, orbitals))
    far_first = lax.ppermute(payload, "orb", across)
    mate = lax.ppermute(held, "orb", mates)
    second = pl.pallas_call(
        second_kernel,
        out_shape=jax.ShapeDtypeStruct(BOX, F32),
        in_specs=[HBM],
        out_specs=HBM,
        scratch_shapes=staging,
        compiler_params=pltpu.CompilerParams(vmem_limit_bytes=3 << 20),
        name="second_box",
    )(held)
    far_second = lax.ppermute(second, "orb", across)
    weights, values = sine_basis()
    fixed = (
        pair_list, pair_count, position, box_offset.reshape(-1),
        jnp.asarray(weights), jnp.asarray(values), orbitals, mate,
    )
    (accum,) = run_stage(0, fixed, (), None)
    accum, for_first = run_stage(1, fixed, (far_first,), accum)
    back_first = lax.ppermute(for_first, "orb", across)
    accum, for_second, *for_mate = run_stage(2, fixed, (far_first, far_second), accum)
    back_second = lax.ppermute(for_second, "orb", across)
    back_mate = [lax.ppermute(box, "orb", mates) for box in for_mate]
    result = run_total(0, accum, back_mate[0], back_first)
    return run_total(1, accum, back_mate[1], back_second, (result,))


def solution(mesh):
    placed = (P("orb", None, None, None), P("orb", None, None), P("orb"), P())
    return jax.shard_map(
        local, mesh=mesh, in_specs=placed, out_specs=P("orb", None, None, None), check_vma=False
    )
```

```python
import functools

import jax
import jax.numpy as jnp
import ml_dtypes
import numpy as np
from jax import lax
from jax.experimental import pallas as pl
from jax.experimental.pallas import tpu as pltpu
from jax.sharding import PartitionSpec as P

BOX_X, BOX_Y, BOX_Z = 48, 64, 128
BOX = (BOX_X, BOX_Y, BOX_Z)
ROWS = BOX_X * BOX_Y
ORB_DEV = 2
SLOTS = 6
TILES = BOX_Y // 8
PLANE = BOX_Y + 8
STENCIL_ROWS = (BOX_X + 2) * PLANE + 8
MARGIN = 24
WIDE = BOX_Y + MARGIN
SHIFT_PLANES = BOX_X + 2
SHIFT_ROWS = SHIFT_PLANES * WIDE
STENCIL_UNROLL = 8
BLOCK = 24
CHUNKS = 6
F32 = jnp.float32
BF16 = jnp.bfloat16


def sine_basis():
    k = np.arange(1, BOX_Z + 1)
    basis = np.sqrt(2.0 / (BOX_Z + 1)) * np.sin(np.pi * np.outer(k, k) / (BOX_Z + 1))
    high = basis.astype(np.float32).astype(ml_dtypes.bfloat16)
    low = (basis - high.astype(np.float64)).astype(ml_dtypes.bfloat16)
    half = np.concatenate([high, low], 1)
    weights = np.concatenate([half, half], 0)
    values = np.tile(2.0 * np.cos(np.pi * k / (BOX_Z + 1)), (8, 1)).astype(np.float32)
    return weights, values


def stencil_row(x):
    return pl.multiple_of(8 + (x + 1) * PLANE, 8)


def shift_row(x):
    return pl.multiple_of((x + 1) * WIDE + MARGIN, 8)


def shifted_plane(x):
    return jnp.where((x >= 0) & (x < BOX_X), x + 1, 0) * WIDE + MARGIN


def zero_rows(ref, first, rows):
    for k in range(rows // 8):
        ref[pl.ds(first + 8 * k, 8), :] = jnp.zeros((8, BOX_Z), F32)


def zero_margins(ref):
    zero_rows(ref, 0, WIDE)
    zero_rows(ref, SHIFT_ROWS - WIDE, WIDE)

    def plane(p, _):
        zero_rows(ref, pl.multiple_of((p + 1) * WIDE, 8), MARGIN)
        return 0

    lax.fori_loop(0, BOX_X, plane, 0, unroll=8)


def zero_borders(ref):
    zero_rows(ref, 0, 8 + PLANE)
    zero_rows(ref, STENCIL_ROWS - PLANE, PLANE)

    def plane(x, _):
        zero_rows(ref, pl.multiple_of(8 + (x + 1) * PLANE + BOX_Y, 8), 8)
        return 0

    lax.fori_loop(0, BOX_X, plane, 0, unroll=16)


def zero_box(ref):
    def plane(x, _):
        for t in range(TILES):
            ref[x, pl.ds(8 * t, 8), :] = jnp.zeros((8, BOX_Z), F32)
        return 0

    lax.fori_loop(0, BOX_X, plane, 0, unroll=2)


def sweep(source, target, centre, other=None, factor=None):
    def plane(x, carry):
        behind, here = carry
        row = stencil_row(x)
        ahead_row = stencil_row(x + 1)
        ahead = [source[pl.ds(ahead_row + 8 * t, 8), :] for t in range(TILES)]
        for t in range(TILES):
            above = source[pl.ds(row + 8 * t - 1, 8), :]
            below = source[pl.ds(row + 8 * t + 1, 8), :]
            total = (behind[t] + ahead[t]) + (above + below) + centre * here[t]
            if other is not None:
                total = total + factor * other[pl.ds(row + 8 * t, 8), :]
            target[pl.ds(row + 8 * t, 8), :] = total
        return here, ahead

    first = [source[pl.ds(stencil_row(-1) + 8 * t, 8), :] for t in range(TILES)]
    second = [source[pl.ds(stencil_row(0) + 8 * t, 8), :] for t in range(TILES)]
    lax.fori_loop(0, BOX_X, plane, (first, second), unroll=STENCIL_UNROLL)


def along_z(rows, weights):
    high = rows.astype(BF16)
    low = (rows - high.astype(F32)).astype(BF16)
    product = jnp.dot(
        jnp.concatenate([high, low], 1), weights[...], preferred_element_type=F32
    )
    return product[:, :BOX_Z] + product[:, BOX_Z:]


def solve_pair(lead, shift, partner, bufs, weights, values, gap, accum, lead_slot, partner_slot):
    gap_x, gap_y, gap_z = gap
    lane = lax.broadcasted_iota(jnp.int32, (8, BOX_Z), 1)
    one, two, three = bufs
    centre = values[...]

    inside = (lane >= gap_z) & (lane < BOX_Z + gap_z)
    turn = jnp.where(gap_z < 0, gap_z + BOX_Z, gap_z)

    def density_block(block, _):
        parts = []
        for q in range(BLOCK):
            x = block * BLOCK + q
            base = shifted_plane(x - gap_x) - gap_y
            for t in range(TILES):
                value = shift[pl.ds(base + 8 * t, 8), :]
                value = jnp.where(inside, pltpu.roll(value, turn, 1), 0.0)
                partner[x, pl.ds(8 * t, 8), :] = value
                parts.append(value * lead[x, pl.ds(8 * t, 8), :])
        spectral = along_z(jnp.concatenate(parts, 0), weights)
        for q in range(BLOCK):
            row = stencil_row(block * BLOCK + q)
            one[pl.ds(row, BOX_Y), :] = spectral[q * BOX_Y : (q + 1) * BOX_Y]
        return 0

    lax.fori_loop(0, BOX_X // BLOCK, density_block, 0)

    sweep(one, three, centre + 6.0)
    sweep(three, one, centre)
    sweep(one, two, centre, three, 36.0)
    sweep(two, one, centre)
    sweep(one, three, centre, three, 1296.0)
    sweep(three, one, centre)
    sweep(one, two, centre)
    sweep(two, one, centre)
    sweep(one, two, centre)
    sweep(two, one, centre)
    sweep(one, two, centre, three, 46656.0)
    scale = 1.0 / (6.0 * 6.0 * 1296.0 * 46656.0)

    def potential_block(block, _):
        rows = jnp.concatenate(
            [two[pl.ds(stencil_row(block * BLOCK + q), BOX_Y), :] for q in range(BLOCK)], 0
        )
        potential = along_z(rows, weights) * scale
        for q in range(BLOCK):
            x = block * BLOCK + q
            for t in range(TILES):
                at = pl.ds(8 * t, 8)
                value = potential[q * BOX_Y + 8 * t : q * BOX_Y + 8 * t + 8]
                accum[lead_slot, x, at, :] = (
                    accum[lead_slot, x, at, :] + value * partner[x, at, :]
                )
                shift[pl.ds(shift_row(x) + 8 * t, 8), :] = value * lead[x, at, :]
        return 0

    lax.fori_loop(0, BOX_X // BLOCK, potential_block, 0)

    back_inside = (lane >= -gap_z) & (lane < BOX_Z - gap_z)
    back_turn = jnp.where(gap_z > 0, BOX_Z - gap_z, -gap_z)

    def back_block(block, _):
        for q in range(BLOCK):
            x = block * BLOCK + q
            base = shifted_plane(x + gap_x) + gap_y
            for t in range(TILES):
                at = pl.ds(8 * t, 8)
                value = shift[pl.ds(base + 8 * t, 8), :]
                value = jnp.where(back_inside, pltpu.roll(value, back_turn, 1), 0.0)
                accum[partner_slot, x, at, :] = accum[partner_slot, x, at, :] + value
        return 0

    lax.fori_loop(0, BOX_X // BLOCK, back_block, 0)


REMOTE = 4
QUOTA = 2
ROOM = 2


PIECES = [pl.ds(c * (BOX_X // CHUNKS), BOX_X // CHUNKS) for c in range(CHUNKS)]


def start_box(box, buf, arrived):
    for c, at in enumerate(PIECES):
        pltpu.make_async_copy(box.at[at], buf.at[at], arrived.at[c]).start()


def finish_box(box, target, buf, arrived, left):
    for c, at in enumerate(PIECES):
        pltpu.make_async_copy(box.at[at], buf.at[at], arrived.at[c]).wait()
        pltpu.make_async_copy(buf.at[at], target.at[at], left.at[c]).start()
    for c, at in enumerate(PIECES):
        pltpu.make_async_copy(buf.at[at], target.at[at], left.at[c]).wait()


def first_kernel(listed, count, own, payload, row, note, note_sem, buf, arrived, left):
    start_box(own.at[0], buf, arrived)
    copy = pltpu.make_async_copy(listed, row, note_sem)
    copy.start()
    copy.wait()
    lane = lax.broadcasted_iota(jnp.int32, (8, BOX_Z), 1)
    value = jnp.where(lane == 2 * SLOTS, count[0].astype(F32), 0.0)
    for e in range(SLOTS):
        for k in range(2):
            value = jnp.where(lane == 2 * e + k, row[0, k, e].astype(F32), value)
    note[...] = jnp.zeros_like(note)
    note[0:8, :] = value
    extra = pltpu.make_async_copy(note, payload.at[BOX_X], note_sem)
    extra.start()
    finish_box(own.at[0], payload, buf, arrived, left)
    extra.wait()


def second_kernel(own, target, buf, arrived, left):
    start_box(own.at[1], buf, arrived)
    finish_box(own.at[1], target, buf, arrived, left)


LIST = 1 + 5 * 2 * SLOTS


def stage_kernel(stage, *refs):
    if stage == 0:
        table, weights, values, own, mate_first, mate_second, accum, later, *rest = refs
        sources = [mate_first.at[pl.ds(0, BOX_X)], mate_second]
        letter = mate_first
    elif stage == 1:
        table, left_over, weights, values, own, mate_first, mate_second, letter, _, *rest = refs
        accum, leaving, later, *rest = rest
        sources = [mate_first.at[pl.ds(0, BOX_X)], mate_second, letter.at[pl.ds(0, BOX_X)]]
    else:
        work, weights, values, own, mate_first, mate_second, remote, _, *rest = refs
        accum, leaving, leave_first, leave_second, *rest = rest
        sources = [mate_first.at[pl.ds(0, BOX_X)], mate_second, remote]
    sources = [own.at[0], own.at[1]] + sources
    lead, shift, partner, one, two, three, sem, *rest = rest

    def clear():
        for buf in (one, two, three):
            zero_borders(buf)
        for buf in range(2):
            zero_margins(shift.at[buf])

    if stage < 2:
        work, note, other, note_sem = rest
        here = table[13]
        mate_id = here ^ 1
        is_left = here % 2 == 1
        across = jnp.where(is_left, here + 1, here - 1)
        copy = pltpu.make_async_copy(letter.at[BOX_X, pl.ds(0, 8), :], note, note_sem)
        copy.start()
        clear()
        copy.wait()
        for k in range(2 * SLOTS + 1):
            other[k] = note[0, k].astype(jnp.int32)
        work[0] = 0
        later[0] = 0

        def place(orbital):
            device = orbital // ORB_DEV
            local_slot = orbital % ORB_DEV
            return jnp.where(
                device == here, local_slot, jnp.where(device == mate_id, 2 + local_slot, REMOTE)
            )

        def push(queue, wanted, lead_id, partner_id):
            @pl.when(wanted)
            def _():
                k = queue[0]
                base = 1 + 5 * k
                queue[0] = k + 1
                queue[base] = place(lead_id)
                queue[base + 1] = place(partner_id)
                for axis in range(3):
                    queue[base + 2 + axis] = (
                        table[14 + 3 * partner_id + axis] - table[14 + 3 * lead_id + axis]
                    )

        rows = []
        for side in range(2):
            use_near = (here % 2 == side) if stage == 0 else (is_left if side == 0 else ~is_left)
            owner = jnp.where(use_near, here, mate_id if stage == 0 else across)
            limit = jnp.where(use_near, table[12], other[12])
            entries = []
            for e in range(SLOTS):
                a = jnp.where(use_near, table[2 * e], other[2 * e])
                b = jnp.where(use_near, table[2 * e + 1], other[2 * e + 1])
                entries.append((e < limit, a, b, a // ORB_DEV, b // ORB_DEV))
            rows.append((owner, entries))

    if stage == 0:
        inner, load = [], []
        for owner, entries in rows:
            beyond = jnp.where(owner % 2 == 1, owner + 1, owner - 1)
            crossing = jnp.int32(0)
            for live, a, b, a_dev, b_dev in entries:
                inside = live & (a_dev != beyond) & (b_dev != beyond)
                half = live & ((a_dev == beyond) != (b_dev == beyond))
                crossing = crossing + half.astype(jnp.int32)
                inner.append((inside, a, b))
            load.append(crossing)
        number = jnp.int32(0)
        for inside, _, _ in inner:
            number = number + inside.astype(jnp.int32)
        even_share = jnp.clip((number + load[1] - load[0] + 1) >> 1, 0, number)
        seen = jnp.int32(0)
        for inside, a, b in inner:
            mine = inside & ((seen < even_share) == (here % 2 == 0))
            early = work[0] < QUOTA
            push(work, mine & early, a, b)
            push(later, mine & ~early, a, b)
            seen = seen + inside.astype(jnp.int32)

    if stage == 1:
        (left, left_row), (right, right_row) = rows
        plan = []
        load_left, load_right = jnp.int32(0), jnp.int32(0)
        for side, (row, far) in enumerate(((left_row, right), (right_row, left))):
            for live, a, b, a_dev, b_dev in row:
                on_left = (a_dev == left) | (b_dev == left)
                on_right = (a_dev == right) | (b_dev == right)
                crosses = live & ((a_dev == far) != (b_dev == far))
                given = live & (a_dev == far) & (b_dev == far)
                free = crosses & on_left & on_right
                fixed = crosses & ~free
                left_bit = jnp.where(a_dev == left, a, b) % ORB_DEV
                right_bit = jnp.where(a_dev == right, a, b) % ORB_DEV
                if side == 0:
                    load_left = load_left + fixed.astype(jnp.int32)
                    load_right = load_right + given.astype(jnp.int32)
                else:
                    load_right = load_right + fixed.astype(jnp.int32)
                    load_left = load_left + given.astype(jnp.int32)
                plan.append((side, a, b, free, fixed, given, left_bit, right_bit))
        rest_of = []
        for side, a, b, free, fixed, given, left_bit, right_bit in plan:
            go_left = (load_left < load_right) | (
                (load_left == load_right) & (right_bit <= left_bit)
            )
            load_left = load_left + (free & go_left).astype(jnp.int32)
            load_right = load_right + (free & ~go_left).astype(jnp.int32)
            stays_left, stays_right = free & go_left, free & ~go_left
            if side == 0:
                stays_left = stays_left | fixed
            else:
                stays_right = stays_right | fixed
            mine = (stays_left & is_left) | (stays_right & ~is_left)
            bit = jnp.where(is_left, right_bit, left_bit)
            push(work, mine & (bit == 0), a, b)
            push(later, mine & (bit == 1), a, b)
            taken = given & (~is_left if side == 0 else is_left)
            rest_of.append((taken, a, b))
        for taken, a, b in rest_of:
            room = work[0] < ROOM
            push(work, taken & room, a, b)
            push(later, taken & ~room, a, b)

        def hand_over(k, _):
            source = 1 + 5 * k
            room = work[0] < ROOM
            for queue, wanted in ((work, room), (later, ~room)):
                @pl.when(wanted)
                def _():
                    base = 1 + 5 * queue[0]
                    queue[0] = queue[0] + 1
                    for field in range(5):
                        queue[base + field] = left_over[source + field]
            return 0

        lax.fori_loop(0, left_over[0], hand_over, 0)

    total = work[0]

    def window(buf):
        return shift.at[buf].reshape(SHIFT_PLANES, WIDE, BOX_Z).at[
            pl.ds(1, BOX_X), pl.ds(MARGIN, BOX_Y), :
        ]

    def fetch(k, buf):
        for which, target in ((0, lead.at[buf]), (1, window(buf))):
            slot = work[1 + 5 * k + which]
            for s, source in enumerate(sources):
                @pl.when(slot == s)
                def _():
                    for at in PIECES:
                        pltpu.make_async_copy(
                            source.at[at], target.at[at], sem.at[which, buf]
                        ).start()

    @pl.when(total > 0)
    def _():
        fetch(0, 0)

    if stage == 0:
        for slot in range(REMOTE + 1):
            zero_box(accum.at[slot])
    if stage == 2:
        clear()

    def visit(k, _):
        buf = k % 2
        pltpu.make_async_copy(sources[0], lead.at[buf], sem.at[0, buf]).wait()
        pltpu.make_async_copy(sources[0], window(buf), sem.at[1, buf]).wait()

        @pl.when(k + 1 < total)
        def _():
            fetch(k + 1, 1 - buf)

        base = 1 + 5 * k
        solve_pair(
            lead.at[buf], shift.at[buf], partner, (one, two, three), weights, values,
            [work[base + 2 + axis] for axis in range(3)], accum, work[base], work[base + 1],
        )
        return 0

    lax.fori_loop(0, total, visit, 0)

    if stage:
        def leave(x, _):
            for t in range(TILES):
                at = pl.ds(8 * t, 8)
                leaving[pl.ds(pl.multiple_of(x * BOX_Y + 8 * t, 8), 8), :] = accum[REMOTE, x, at, :]
                if stage == 1:
                    accum[REMOTE, x, at, :] = jnp.zeros((8, BOX_Z), F32)
                else:
                    for box in range(ORB_DEV):
                        (leave_first, leave_second)[box][x, at, :] = accum[2 + box, x, at, :]
            return 0

        lax.fori_loop(0, BOX_X, leave, 0, unroll=2)
        zero_rows(leaving, ROWS, leaving.shape[0] - ROWS)


SMEM = pl.BlockSpec(memory_space=pltpu.SMEM)
VMEM = pl.BlockSpec(memory_space=pltpu.VMEM)
HBM = pl.BlockSpec(memory_space=pltpu.HBM)


def run_stage(stage, lists, fixed, remote=(), accum=()):
    operands = [*lists, *fixed, *remote, *accum]
    specs = (
        [SMEM] * len(lists) + [VMEM] * 2 + [HBM] * 3 + [HBM] * len(remote) + [VMEM] * len(accum)
    )
    queue = jax.ShapeDtypeStruct((LIST,), jnp.int32)
    leaving = ([], [(ROWS + 16, BOX_Z)], [(ROWS + 8, BOX_Z), BOX, BOX])[stage]
    shapes = [jax.ShapeDtypeStruct(shape, F32) for shape in [(REMOTE + 1,) + BOX] + leaving]
    outs = [VMEM] * len(shapes)
    scratch = [
        pltpu.VMEM((2,) + BOX, F32),
        pltpu.VMEM((2, SHIFT_ROWS, BOX_Z), F32),
        pltpu.VMEM(BOX, F32),
        pltpu.VMEM((STENCIL_ROWS, BOX_Z), F32),
        pltpu.VMEM((STENCIL_ROWS, BOX_Z), F32),
        pltpu.VMEM((STENCIL_ROWS, BOX_Z), F32),
        pltpu.SemaphoreType.DMA((2, 2)),
    ]
    if stage < 2:
        shapes.append(queue)
        outs.append(SMEM)
        scratch += [
            pltpu.SMEM((LIST,), jnp.int32),
            pltpu.SMEM((8, BOX_Z), F32),
            pltpu.SMEM((2 * SLOTS + 1,), jnp.int32),
            pltpu.SemaphoreType.DMA,
        ]
    return pl.pallas_call(
        functools.partial(stage_kernel, stage),
        out_shape=shapes,
        in_specs=specs,
        out_specs=outs,
        input_output_aliases={len(operands) - 1: 0} if accum else {},
        scratch_shapes=scratch,
        compiler_params=pltpu.CompilerParams(vmem_limit_bytes=24 << 20),
        cost_estimate=pl.CostEstimate(
            flops=200_000_000, bytes_accessed=20_000_000, transcendentals=0
        ),
        name="stage_" + "abc"[stage],
    )(*operands)


def total_kernel(box, accum, mate, remote, *rest):
    result, chunk, sem = rest[-3:]

    def add(x, _):
        for t in range(TILES):
            at = pl.ds(8 * t, 8)
            far = remote[pl.ds(pl.multiple_of(x * BOX_Y + 8 * t, 8), 8), :]
            chunk[x, at, :] = accum[box, x, at, :] + mate[x, at, :] + far
        pltpu.make_async_copy(chunk.at[x], result.at[box, x], sem).start()
        return 0

    lax.fori_loop(0, BOX_X, add, 0, unroll=2)
    pltpu.make_async_copy(chunk, result.at[box], sem).wait()


def run_total(box, accum, mate, remote, result=()):
    return pl.pallas_call(
        functools.partial(total_kernel, box),
        out_shape=jax.ShapeDtypeStruct((ORB_DEV,) + BOX, F32),
        in_specs=[VMEM, VMEM, VMEM] + [HBM] * len(result),
        out_specs=HBM,
        input_output_aliases={3: 0} if result else {},
        scratch_shapes=[pltpu.VMEM(BOX, F32), pltpu.SemaphoreType.DMA],
        compiler_params=pltpu.CompilerParams(vmem_limit_bytes=4 << 20),
        name="total_" + "ab"[box],
    )(accum, mate, remote, *result)


def local(orbitals, pair_list, pair_count, box_offset):
    position = lax.axis_index("orb").astype(jnp.int32)[None]
    devices = lax.axis_size("orb")
    mates = [(d, d ^ 1) for d in range(devices)]
    across = [(d, d + 1) for d in range(1, devices - 1, 2)]
    across = across + [(b, a) for a, b in across]
    staging = [
        pltpu.VMEM(BOX, F32),
        pltpu.SemaphoreType.DMA((CHUNKS,)),
        pltpu.SemaphoreType.DMA((CHUNKS,)),
    ]
    payload = pl.pallas_call(
        first_kernel,
        out_shape=jax.ShapeDtypeStruct((BOX_X + 1, BOX_Y, BOX_Z), F32),
        in_specs=[HBM, SMEM, HBM],
        out_specs=HBM,
        scratch_shapes=[
            pltpu.SMEM((1, 2, SLOTS), jnp.int32),
            pltpu.VMEM((BOX_Y, BOX_Z), F32),
            pltpu.SemaphoreType.DMA,
        ]
        + staging,
        compiler_params=pltpu.CompilerParams(vmem_limit_bytes=60 << 20),
        name="first_box",
    )(jnp.transpose(pair_list, (0, 2, 1)), pair_count, orbitals)
    far_first = lax.ppermute(payload, "orb", across)
    mate_first = lax.ppermute(payload, "orb", mates)
    second = pl.pallas_call(
        second_kernel,
        out_shape=jax.ShapeDtypeStruct(BOX, F32),
        in_specs=[HBM],
        out_specs=HBM,
        scratch_shapes=staging,
        compiler_params=pltpu.CompilerParams(vmem_limit_bytes=60 << 20),
        name="second_box",
    )(orbitals)
    far_second = lax.ppermute(second, "orb", across)
    mate_second = lax.ppermute(second, "orb", mates)
    weights, values = sine_basis()
    fixed = (jnp.asarray(weights), jnp.asarray(values), orbitals, mate_first, mate_second)
    table = jnp.concatenate([pair_list.reshape(-1), pair_count, position, box_offset.reshape(-1)])
    accum, left_over = run_stage(0, [table], fixed)
    accum, for_first, later = run_stage(1, [table, left_over], fixed, [far_first], [accum])
    back_first = lax.ppermute(for_first, "orb", across)
    accum, for_second, *for_mate = run_stage(2, [later], fixed, [far_second], [accum])
    back_second = lax.ppermute(for_second, "orb", across)
    back_mate = [lax.ppermute(box, "orb", mates) for box in for_mate]
    result = run_total(0, accum, back_mate[0], back_first)
    return run_total(1, accum, back_mate[1], back_second, (result,))


def solution(mesh):
    placed = (P("orb", None, None, None), P("orb", None, None), P("orb"), P())
    return jax.shard_map(
        local, mesh=mesh, in_specs=placed, out_specs=P("orb", None, None, None), check_vma=False
    )
```

```python
import functools

import jax
import jax.numpy as jnp
import ml_dtypes
import numpy as np
from jax import lax
from jax.experimental import pallas as pl
from jax.experimental.pallas import tpu as pltpu
from jax.sharding import PartitionSpec as P

BOX_X, BOX_Y, BOX_Z = 48, 64, 128
BOX = (BOX_X, BOX_Y, BOX_Z)
ROWS = BOX_X * BOX_Y
ORB_DEV = 2
SLOTS = 6
TILES = BOX_Y // 8
PLANE = BOX_Y + 8
STENCIL_ROWS = (BOX_X + 2) * PLANE + 8
MARGIN = 24
WIDE = BOX_Y + MARGIN
SHIFT_PLANES = BOX_X + 2
SHIFT_ROWS = SHIFT_PLANES * WIDE
STENCIL_UNROLL = 8
BLOCK = 24
CHUNKS = 6
F32 = jnp.float32
BF16 = jnp.bfloat16


def sine_basis():
    k = np.arange(1, BOX_Z + 1)
    basis = np.sqrt(2.0 / (BOX_Z + 1)) * np.sin(np.pi * np.outer(k, k) / (BOX_Z + 1))
    high = basis.astype(np.float32).astype(ml_dtypes.bfloat16)
    low = (basis - high.astype(np.float64)).astype(ml_dtypes.bfloat16)
    half = np.concatenate([high, low], 1)
    weights = np.concatenate([half, half], 0)
    values = np.tile(2.0 * np.cos(np.pi * k / (BOX_Z + 1)), (8, 1)).astype(np.float32)
    return weights, values


def stencil_row(x):
    return pl.multiple_of(8 + (x + 1) * PLANE, 8)


def shift_row(x):
    return pl.multiple_of((x + 1) * WIDE + MARGIN, 8)


def shifted_plane(x):
    return jnp.where((x >= 0) & (x < BOX_X), x + 1, 0) * WIDE + MARGIN


def zero_rows(ref, first, rows):
    for k in range(rows // 8):
        ref[pl.ds(first + 8 * k, 8), :] = jnp.zeros((8, BOX_Z), F32)


def zero_margins(ref):
    zero_rows(ref, 0, WIDE)
    zero_rows(ref, SHIFT_ROWS - WIDE, WIDE)

    def plane(p, _):
        zero_rows(ref, pl.multiple_of((p + 1) * WIDE, 8), MARGIN)
        return 0

    lax.fori_loop(0, BOX_X, plane, 0, unroll=8)


def zero_borders(ref):
    zero_rows(ref, 0, 8 + PLANE)
    zero_rows(ref, STENCIL_ROWS - PLANE, PLANE)

    def plane(x, _):
        zero_rows(ref, pl.multiple_of(8 + (x + 1) * PLANE + BOX_Y, 8), 8)
        return 0

    lax.fori_loop(0, BOX_X, plane, 0, unroll=16)


def zero_box(ref):
    def plane(x, _):
        for t in range(TILES):
            ref[x, pl.ds(8 * t, 8), :] = jnp.zeros((8, BOX_Z), F32)
        return 0

    lax.fori_loop(0, BOX_X, plane, 0, unroll=2)


def sweep(source, target, centre, other=None, factor=None):
    def plane(x, carry):
        behind, here = carry
        row = stencil_row(x)
        ahead_row = stencil_row(x + 1)
        ahead = [source[pl.ds(ahead_row + 8 * t, 8), :] for t in range(TILES)]
        for t in range(TILES):
            above = source[pl.ds(row + 8 * t - 1, 8), :]
            below = source[pl.ds(row + 8 * t + 1, 8), :]
            total = (behind[t] + ahead[t]) + (above + below) + centre * here[t]
            if other is not None:
                total = total + factor * other[pl.ds(row + 8 * t, 8), :]
            target[pl.ds(row + 8 * t, 8), :] = total
        return here, ahead

    first = [source[pl.ds(stencil_row(-1) + 8 * t, 8), :] for t in range(TILES)]
    second = [source[pl.ds(stencil_row(0) + 8 * t, 8), :] for t in range(TILES)]
    lax.fori_loop(0, BOX_X, plane, (first, second), unroll=STENCIL_UNROLL)


def along_z(rows, weights):
    high = rows.astype(BF16)
    low = (rows - high.astype(F32)).astype(BF16)
    product = jnp.dot(
        jnp.concatenate([high, low], 1), weights[...], preferred_element_type=F32
    )
    return product[:, :BOX_Z] + product[:, BOX_Z:]


def solve_pair(lead, shift, partner, bufs, weights, values, gap, accum, lead_slot, partner_slot):
    gap_x, gap_y, gap_z = gap
    lane = lax.broadcasted_iota(jnp.int32, (8, BOX_Z), 1)
    one, two, three = bufs
    centre = values[...]

    inside = (lane >= gap_z) & (lane < BOX_Z + gap_z)
    turn = jnp.where(gap_z < 0, gap_z + BOX_Z, gap_z)

    def density_block(block, _):
        parts = []
        for q in range(BLOCK):
            x = block * BLOCK + q
            base = shifted_plane(x - gap_x) - gap_y
            for t in range(TILES):
                value = shift[pl.ds(base + 8 * t, 8), :]
                value = jnp.where(inside, pltpu.roll(value, turn, 1), 0.0)
                partner[x, pl.ds(8 * t, 8), :] = value
                parts.append(value * lead[x, pl.ds(8 * t, 8), :])
        spectral = along_z(jnp.concatenate(parts, 0), weights)
        for q in range(BLOCK):
            row = stencil_row(block * BLOCK + q)
            one[pl.ds(row, BOX_Y), :] = spectral[q * BOX_Y : (q + 1) * BOX_Y]
        return 0

    lax.fori_loop(0, BOX_X // BLOCK, density_block, 0)

    sweep(one, three, centre + 6.0)
    sweep(three, one, centre)
    sweep(one, two, centre, three, 36.0)
    sweep(two, one, centre)
    sweep(one, three, centre, three, 1296.0)
    sweep(three, one, centre)
    sweep(one, two, centre)
    sweep(two, one, centre)
    sweep(one, two, centre)
    sweep(two, one, centre)
    sweep(one, two, centre, three, 46656.0)
    scale = 1.0 / (6.0 * 6.0 * 1296.0 * 46656.0)

    def potential_block(block, _):
        rows = jnp.concatenate(
            [two[pl.ds(stencil_row(block * BLOCK + q), BOX_Y), :] for q in range(BLOCK)], 0
        )
        potential = along_z(rows, weights) * scale
        for q in range(BLOCK):
            x = block * BLOCK + q
            for t in range(TILES):
                at = pl.ds(8 * t, 8)
                value = potential[q * BOX_Y + 8 * t : q * BOX_Y + 8 * t + 8]
                accum[lead_slot, x, at, :] = (
                    accum[lead_slot, x, at, :] + value * partner[x, at, :]
                )
                shift[pl.ds(shift_row(x) + 8 * t, 8), :] = value * lead[x, at, :]
        return 0

    lax.fori_loop(0, BOX_X // BLOCK, potential_block, 0)

    back_inside = (lane >= -gap_z) & (lane < BOX_Z - gap_z)
    back_turn = jnp.where(gap_z > 0, BOX_Z - gap_z, -gap_z)

    def back_block(block, _):
        for q in range(BLOCK):
            x = block * BLOCK + q
            base = shifted_plane(x + gap_x) + gap_y
            for t in range(TILES):
                at = pl.ds(8 * t, 8)
                value = shift[pl.ds(base + 8 * t, 8), :]
                value = jnp.where(back_inside, pltpu.roll(value, back_turn, 1), 0.0)
                accum[partner_slot, x, at, :] = accum[partner_slot, x, at, :] + value
        return 0

    lax.fori_loop(0, BOX_X // BLOCK, back_block, 0)


REMOTE = 4
QUOTA = 2
ROOM = 2


PIECES = [pl.ds(c * (BOX_X // CHUNKS), BOX_X // CHUNKS) for c in range(CHUNKS)]


def start_box(box, buf, arrived):
    for c, at in enumerate(PIECES):
        pltpu.make_async_copy(box.at[at], buf.at[at], arrived.at[c]).start()


def finish_box(box, target, buf, arrived, left):
    for c, at in enumerate(PIECES):
        pltpu.make_async_copy(box.at[at], buf.at[at], arrived.at[c]).wait()
        pltpu.make_async_copy(buf.at[at], target.at[at], left.at[c]).start()
    for c, at in enumerate(PIECES):
        pltpu.make_async_copy(buf.at[at], target.at[at], left.at[c]).wait()


def first_kernel(listed, count, own, payload, row, note, note_sem, buf, arrived, left):
    start_box(own.at[0], buf, arrived)
    copy = pltpu.make_async_copy(listed, row, note_sem)
    copy.start()
    copy.wait()
    lane = lax.broadcasted_iota(jnp.int32, (8, BOX_Z), 1)
    value = jnp.where(lane == 2 * SLOTS, count[0].astype(F32), 0.0)
    for e in range(SLOTS):
        for k in range(2):
            value = jnp.where(lane == 2 * e + k, row[0, k, e].astype(F32), value)
    note[...] = jnp.zeros_like(note)
    note[0:8, :] = value
    extra = pltpu.make_async_copy(note, payload.at[BOX_X], note_sem)
    extra.start()
    finish_box(own.at[0], payload, buf, arrived, left)
    extra.wait()


def second_kernel(own, crossing, target, buf, arrived, left):
    start_box(own.at[1], buf, arrived)
    wide = crossing.reshape(BOX_X + 1, BOX_Y, BOX_Z)
    copies = []
    for c, at in enumerate(PIECES):
        pltpu.make_async_copy(own.at[1].at[at], buf.at[at], arrived.at[c]).wait()
        for k, to in enumerate((wide, target)):
            copies.append(pltpu.make_async_copy(buf.at[at], to.at[at], left.at[k * CHUNKS + c]))
            copies[-1].start()
    extra = pltpu.make_async_copy(buf.at[0], wide.at[BOX_X], arrived.at[0])
    extra.start()
    for copy in copies + [extra]:
        copy.wait()


LIST = 1 + 5 * 2 * SLOTS


def stage_kernel(stage, *refs):
    if stage == 0:
        table, weights, values, own, mate_first, mate_second, accum, queues, *rest = refs
        sources = [mate_first.at[pl.ds(0, BOX_X)], mate_second]
        letter = mate_first
    elif stage == 1:
        table, left_over, weights, values, own, mate_first, mate_second, letter, _, *rest = refs
        accum, leaving, queues, *rest = rest
        sources = [mate_first.at[pl.ds(0, BOX_X)], mate_second, letter.at[pl.ds(0, BOX_X)]]
    else:
        queues, weights, values, own, mate_first, mate_second, remote, _, *rest = refs
        accum, leaving, leave_first, leave_second, *rest = rest
        box = remote.reshape(BOX_X + 1, BOX_Y, BOX_Z).at[pl.ds(0, BOX_X)]
        sources = [mate_first.at[pl.ds(0, BOX_X)], mate_second, box]
    sources = [own.at[0], own.at[1]] + sources
    lead, shift, partner, one, two, three, sem, *rest = rest

    def clear():
        for buf in (one, two, three):
            zero_borders(buf)
        for buf in range(2):
            zero_margins(shift.at[buf])

    if stage < 2:
        note, other, note_sem = rest
        here = table[13]
        mate_id = here ^ 1
        is_left = here % 2 == 1
        across = jnp.where(is_left, here + 1, here - 1)
        copy = pltpu.make_async_copy(letter.at[BOX_X, pl.ds(0, 8), :], note, note_sem)
        copy.start()
        clear()
        copy.wait()
        for k in range(2 * SLOTS + 1):
            other[k] = note[0, k].astype(jnp.int32)
        queues[0] = 0
        queues[LIST] = 0

        def place(orbital):
            device = orbital // ORB_DEV
            local_slot = orbital % ORB_DEV
            return jnp.where(
                device == here, local_slot, jnp.where(device == mate_id, 2 + local_slot, REMOTE)
            )

        def push(which, wanted, lead_id, partner_id):
            @pl.when(wanted)
            def _():
                start = which * LIST
                k = queues[start]
                base = start + 1 + 5 * k
                queues[start] = k + 1
                queues[base] = place(lead_id)
                queues[base + 1] = place(partner_id)
                for axis in range(3):
                    queues[base + 2 + axis] = (
                        table[14 + 3 * partner_id + axis] - table[14 + 3 * lead_id + axis]
                    )

        rows = []
        for side in range(2):
            use_near = (here % 2 == side) if stage == 0 else (is_left if side == 0 else ~is_left)
            owner = jnp.where(use_near, here, mate_id if stage == 0 else across)
            limit = jnp.where(use_near, table[12], other[12])
            entries = []
            for e in range(SLOTS):
                a = jnp.where(use_near, table[2 * e], other[2 * e])
                b = jnp.where(use_near, table[2 * e + 1], other[2 * e + 1])
                entries.append((e < limit, a, b, a // ORB_DEV, b // ORB_DEV))
            rows.append((owner, entries))

    if stage == 0:
        inner, load = [], []
        for owner, entries in rows:
            beyond = jnp.where(owner % 2 == 1, owner + 1, owner - 1)
            crossing = jnp.int32(0)
            for live, a, b, a_dev, b_dev in entries:
                inside = live & (a_dev != beyond) & (b_dev != beyond)
                half = live & ((a_dev == beyond) != (b_dev == beyond))
                crossing = crossing + half.astype(jnp.int32)
                inner.append((inside, a, b))
            load.append(crossing)
        number = jnp.int32(0)
        for inside, _, _ in inner:
            number = number + inside.astype(jnp.int32)
        quota = jnp.where(jnp.where(here % 2 == 0, load[0], load[1]) > 1, QUOTA - 1, QUOTA)
        even_share = jnp.clip((number + load[1] - load[0] + 1) >> 1, 0, number)
        seen = jnp.int32(0)
        for inside, a, b in inner:
            mine = inside & ((seen < even_share) == (here % 2 == 0))
            push(jnp.where(queues[0] < quota, 0, 1), mine, a, b)
            seen = seen + inside.astype(jnp.int32)

    if stage == 1:
        (left, left_row), (right, right_row) = rows
        plan = []
        load_left, load_right = jnp.int32(0), jnp.int32(0)
        for side, (row, far) in enumerate(((left_row, right), (right_row, left))):
            for live, a, b, a_dev, b_dev in row:
                on_left = (a_dev == left) | (b_dev == left)
                on_right = (a_dev == right) | (b_dev == right)
                crosses = live & ((a_dev == far) != (b_dev == far))
                given = live & (a_dev == far) & (b_dev == far)
                free = crosses & on_left & on_right
                fixed = crosses & ~free
                left_bit = jnp.where(a_dev == left, a, b) % ORB_DEV
                right_bit = jnp.where(a_dev == right, a, b) % ORB_DEV
                if side == 0:
                    load_left = load_left + fixed.astype(jnp.int32)
                    load_right = load_right + given.astype(jnp.int32)
                else:
                    load_right = load_right + fixed.astype(jnp.int32)
                    load_left = load_left + given.astype(jnp.int32)
                plan.append((side, a, b, free, fixed, given, left_bit, right_bit))
        rest_of = []
        for side, a, b, free, fixed, given, left_bit, right_bit in plan:
            go_left = (load_left < load_right) | (
                (load_left == load_right) & (right_bit <= left_bit)
            )
            load_left = load_left + (free & go_left).astype(jnp.int32)
            load_right = load_right + (free & ~go_left).astype(jnp.int32)
            stays_left, stays_right = free & go_left, free & ~go_left
            if side == 0:
                stays_left = stays_left | fixed
            else:
                stays_right = stays_right | fixed
            mine = (stays_left & is_left) | (stays_right & ~is_left)
            bit = jnp.where(is_left, right_bit, left_bit)
            push(bit, mine, a, b)
            taken = given & (~is_left if side == 0 else is_left)
            rest_of.append((taken, a, b))
        for taken, a, b in rest_of:
            push(jnp.where(queues[0] < ROOM, 0, 1), taken, a, b)

        def hand_over(k, _):
            source = LIST + 1 + 5 * k
            start = jnp.where(queues[0] < ROOM, 0, LIST)
            base = start + 1 + 5 * queues[start]
            queues[start] = queues[start] + 1
            for field in range(5):
                queues[base + field] = left_over[source + field]
            return 0

        lax.fori_loop(0, left_over[LIST], hand_over, 0)

    first = LIST if stage == 2 else 0
    total = queues[first]

    def window(buf):
        return shift.at[buf].reshape(SHIFT_PLANES, WIDE, BOX_Z).at[
            pl.ds(1, BOX_X), pl.ds(MARGIN, BOX_Y), :
        ]

    def fetch(k, buf):
        for which, target in ((0, lead.at[buf]), (1, window(buf))):
            slot = queues[first + 1 + 5 * k + which]
            for s, source in enumerate(sources):
                @pl.when(slot == s)
                def _():
                    for at in PIECES:
                        pltpu.make_async_copy(
                            source.at[at], target.at[at], sem.at[which, buf]
                        ).start()

    @pl.when(total > 0)
    def _():
        fetch(0, 0)

    if stage == 0:
        for slot in range(REMOTE + 1):
            zero_box(accum.at[slot])
    if stage == 2:
        clear()

    def visit(k, _):
        buf = k % 2
        pltpu.make_async_copy(sources[0], lead.at[buf], sem.at[0, buf]).wait()
        pltpu.make_async_copy(sources[0], window(buf), sem.at[1, buf]).wait()

        @pl.when(k + 1 < total)
        def _():
            fetch(k + 1, 1 - buf)

        base = first + 1 + 5 * k
        solve_pair(
            lead.at[buf], shift.at[buf], partner, (one, two, three), weights, values,
            [queues[base + 2 + axis] for axis in range(3)], accum, queues[base], queues[base + 1],
        )
        return 0

    lax.fori_loop(0, total, visit, 0)

    if stage:
        def leave(x, _):
            for t in range(TILES):
                at = pl.ds(8 * t, 8)
                leaving[pl.ds(pl.multiple_of(x * BOX_Y + 8 * t, 8), 8), :] = accum[REMOTE, x, at, :]
                if stage == 1:
                    accum[REMOTE, x, at, :] = jnp.zeros((8, BOX_Z), F32)
                else:
                    for box in range(ORB_DEV):
                        (leave_first, leave_second)[box][x, at, :] = accum[2 + box, x, at, :]
            return 0

        lax.fori_loop(0, BOX_X, leave, 0, unroll=2)
        zero_rows(leaving, ROWS, leaving.shape[0] - ROWS)


SMEM = pl.BlockSpec(memory_space=pltpu.SMEM)
VMEM = pl.BlockSpec(memory_space=pltpu.VMEM)
HBM = pl.BlockSpec(memory_space=pltpu.HBM)


def run_stage(stage, lists, fixed, remote=(), accum=()):
    operands = [*lists, *fixed, *remote, *accum]
    specs = (
        [SMEM] * len(lists) + [VMEM] * 2 + [HBM] * 3 + [HBM] * len(remote) + [VMEM] * len(accum)
    )
    queue = jax.ShapeDtypeStruct((2 * LIST,), jnp.int32)
    leaving = ([], [(ROWS + 16, BOX_Z)], [(ROWS + 8, BOX_Z), BOX, BOX])[stage]
    shapes = [jax.ShapeDtypeStruct(shape, F32) for shape in [(REMOTE + 1,) + BOX] + leaving]
    outs = [VMEM] * len(shapes)
    scratch = [
        pltpu.VMEM((2,) + BOX, F32),
        pltpu.VMEM((2, SHIFT_ROWS, BOX_Z), F32),
        pltpu.VMEM(BOX, F32),
        pltpu.VMEM((STENCIL_ROWS, BOX_Z), F32),
        pltpu.VMEM((STENCIL_ROWS, BOX_Z), F32),
        pltpu.VMEM((STENCIL_ROWS, BOX_Z), F32),
        pltpu.SemaphoreType.DMA((2, 2)),
    ]
    if stage < 2:
        shapes.append(queue)
        outs.append(SMEM)
        scratch += [
            pltpu.SMEM((8, BOX_Z), F32),
            pltpu.SMEM((2 * SLOTS + 1,), jnp.int32),
            pltpu.SemaphoreType.DMA,
        ]
    return pl.pallas_call(
        functools.partial(stage_kernel, stage),
        out_shape=shapes,
        in_specs=specs,
        out_specs=outs,
        input_output_aliases={len(operands) - 1: 0} if accum else {},
        scratch_shapes=scratch,
        compiler_params=pltpu.CompilerParams(vmem_limit_bytes=24 << 20),
        cost_estimate=pl.CostEstimate(
            flops=1000, bytes_accessed=1000, transcendentals=0
        ),
        name="stage_" + "abc"[stage],
    )(*operands)


def total_kernel(box, accum, mate, remote, *rest):
    result, chunk, sem = rest[-3:]

    def add(x, _):
        for t in range(TILES):
            at = pl.ds(8 * t, 8)
            far = remote[pl.ds(pl.multiple_of(x * BOX_Y + 8 * t, 8), 8), :]
            chunk[x, at, :] = accum[box, x, at, :] + mate[x, at, :] + far
        pltpu.make_async_copy(chunk.at[x], result.at[box, x], sem).start()
        return 0

    lax.fori_loop(0, BOX_X, add, 0, unroll=2)
    pltpu.make_async_copy(chunk, result.at[box], sem).wait()


def run_total(box, accum, mate, remote, result=()):
    return pl.pallas_call(
        functools.partial(total_kernel, box),
        out_shape=jax.ShapeDtypeStruct((ORB_DEV,) + BOX, F32),
        in_specs=[VMEM, VMEM, VMEM] + [HBM] * len(result),
        out_specs=HBM,
        input_output_aliases={3: 0} if result else {},
        scratch_shapes=[pltpu.VMEM(BOX, F32), pltpu.SemaphoreType.DMA],
        compiler_params=pltpu.CompilerParams(vmem_limit_bytes=4 << 20),
        name="total_" + "ab"[box],
    )(accum, mate, remote, *result)


def local(orbitals, pair_list, pair_count, box_offset):
    position = lax.axis_index("orb").astype(jnp.int32)[None]
    devices = lax.axis_size("orb")
    mates = [(d, d ^ 1) for d in range(devices)]
    across = [(d, d + 1) for d in range(1, devices - 1, 2)]
    across = across + [(b, a) for a, b in across]
    staging = [
        pltpu.VMEM(BOX, F32),
        pltpu.SemaphoreType.DMA((CHUNKS,)),
        pltpu.SemaphoreType.DMA((CHUNKS,)),
    ]
    payload = pl.pallas_call(
        first_kernel,
        out_shape=jax.ShapeDtypeStruct((BOX_X + 1, BOX_Y, BOX_Z), F32),
        in_specs=[HBM, SMEM, HBM],
        out_specs=HBM,
        scratch_shapes=[
            pltpu.SMEM((1, 2, SLOTS), jnp.int32),
            pltpu.VMEM((BOX_Y, BOX_Z), F32),
            pltpu.SemaphoreType.DMA,
        ]
        + staging,
        compiler_params=pltpu.CompilerParams(vmem_limit_bytes=60 << 20),
        name="first_box",
    )(jnp.transpose(pair_list, (0, 2, 1)), pair_count, orbitals)
    far_first = lax.ppermute(payload, "orb", across)
    mate_first = lax.ppermute(payload, "orb", mates)
    second_out, second_in = pl.pallas_call(
        second_kernel,
        out_shape=[
            jax.ShapeDtypeStruct((ROWS + BOX_Y, BOX_Z), F32),
            jax.ShapeDtypeStruct(BOX, F32),
        ],
        in_specs=[HBM],
        out_specs=[HBM] * 2,
        scratch_shapes=[
            pltpu.VMEM(BOX, F32),
            pltpu.SemaphoreType.DMA((CHUNKS,)),
            pltpu.SemaphoreType.DMA((2 * CHUNKS,)),
        ],
        compiler_params=pltpu.CompilerParams(vmem_limit_bytes=60 << 20),
        name="second_box",
    )(orbitals)
    far_second = lax.ppermute(second_out, "orb", across)
    mate_second = lax.ppermute(second_in, "orb", mates)
    weights, values = sine_basis()
    fixed = (jnp.asarray(weights), jnp.asarray(values), orbitals, mate_first, mate_second)
    table = jnp.concatenate([pair_list.reshape(-1), pair_count, position, box_offset.reshape(-1)])
    accum, left_over = run_stage(0, [table], fixed)
    accum, for_first, later = run_stage(1, [table, left_over], fixed, [far_first], [accum])
    back_first = lax.ppermute(for_first, "orb", across)
    accum, for_second, *for_mate = run_stage(2, [later], fixed, [far_second], [accum])
    back_second = lax.ppermute(for_second, "orb", across)
    back_mate = [lax.ppermute(box, "orb", mates) for box in for_mate]
    result = run_total(0, accum, back_mate[0], back_first)
    return run_total(1, accum, back_mate[1], back_second, (result,))


def solution(mesh):
    placed = (P("orb", None, None, None), P("orb", None, None), P("orb"), P())
    return jax.shard_map(
        local, mesh=mesh, in_specs=placed, out_specs=P("orb", None, None, None), check_vma=False
    )
```

```python
import functools

import jax
import jax.numpy as jnp
import ml_dtypes
import numpy as np
from jax import lax
from jax.experimental import pallas as pl
from jax.experimental.pallas import tpu as pltpu
from jax.sharding import PartitionSpec as P

BOX_X, BOX_Y, BOX_Z = 48, 64, 128
BOX = (BOX_X, BOX_Y, BOX_Z)
ROWS = BOX_X * BOX_Y
ORB_DEV = 2
SLOTS = 6
TILES = BOX_Y // 8
PLANE = BOX_Y + 8
STENCIL_ROWS = (BOX_X + 2) * PLANE + 8
MARGIN = 24
WIDE = BOX_Y + MARGIN
SHIFT_PLANES = BOX_X + 2
SHIFT_ROWS = SHIFT_PLANES * WIDE
STENCIL_UNROLL = 8
BLOCK = 24
CHUNKS = 6
F32 = jnp.float32
BF16 = jnp.bfloat16


def sine_basis():
    k = np.arange(1, BOX_Z + 1)
    basis = np.sqrt(2.0 / (BOX_Z + 1)) * np.sin(np.pi * np.outer(k, k) / (BOX_Z + 1))
    high = basis.astype(np.float32).astype(ml_dtypes.bfloat16)
    low = (basis - high.astype(np.float64)).astype(ml_dtypes.bfloat16)
    half = np.concatenate([high, low], 1)
    weights = np.concatenate([half, half], 0)
    values = np.tile(2.0 * np.cos(np.pi * k / (BOX_Z + 1)), (8, 1)).astype(np.float32)
    return weights, values


def stencil_row(x):
    return pl.multiple_of(8 + (x + 1) * PLANE, 8)


def shift_row(x):
    return pl.multiple_of((x + 1) * WIDE + MARGIN, 8)


def shifted_plane(x):
    return jnp.where((x >= 0) & (x < BOX_X), x + 1, 0) * WIDE + MARGIN


def zero_rows(ref, first, rows):
    for k in range(rows // 8):
        ref[pl.ds(first + 8 * k, 8), :] = jnp.zeros((8, BOX_Z), F32)


def zero_margins(ref):
    zero_rows(ref, 0, WIDE)
    zero_rows(ref, SHIFT_ROWS - WIDE, WIDE)

    def plane(p, _):
        zero_rows(ref, pl.multiple_of((p + 1) * WIDE, 8), MARGIN)
        return 0

    lax.fori_loop(0, BOX_X, plane, 0, unroll=8)


def zero_borders(ref):
    zero_rows(ref, 0, 8 + PLANE)
    zero_rows(ref, STENCIL_ROWS - PLANE, PLANE)

    def plane(x, _):
        zero_rows(ref, pl.multiple_of(8 + (x + 1) * PLANE + BOX_Y, 8), 8)
        return 0

    lax.fori_loop(0, BOX_X, plane, 0, unroll=16)


def zero_box(ref):
    def plane(x, _):
        for t in range(TILES):
            ref[x, pl.ds(8 * t, 8), :] = jnp.zeros((8, BOX_Z), F32)
        return 0

    lax.fori_loop(0, BOX_X, plane, 0, unroll=2)


def sweep(source, target, centre, other=None, factor=None):
    def plane(x, carry):
        behind, here = carry
        row = stencil_row(x)
        ahead_row = stencil_row(x + 1)
        ahead = [source[pl.ds(ahead_row + 8 * t, 8), :] for t in range(TILES)]
        for t in range(TILES):
            above = source[pl.ds(row + 8 * t - 1, 8), :]
            below = source[pl.ds(row + 8 * t + 1, 8), :]
            total = (behind[t] + ahead[t]) + (above + below) + centre * here[t]
            if other is not None:
                total = total + factor * other[pl.ds(row + 8 * t, 8), :]
            target[pl.ds(row + 8 * t, 8), :] = total
        return here, ahead

    first = [source[pl.ds(stencil_row(-1) + 8 * t, 8), :] for t in range(TILES)]
    second = [source[pl.ds(stencil_row(0) + 8 * t, 8), :] for t in range(TILES)]
    lax.fori_loop(0, BOX_X, plane, (first, second), unroll=STENCIL_UNROLL)


def along_z(rows, weights):
    high = rows.astype(BF16)
    low = (rows - high.astype(F32)).astype(BF16)
    product = jnp.dot(
        jnp.concatenate([high, low], 1), weights[...], preferred_element_type=F32
    )
    return product[:, :BOX_Z] + product[:, BOX_Z:]


def solve_pair(lead, shift, partner, bufs, weights, values, gap, accum, lead_slot, partner_slot):
    gap_x, gap_y, gap_z = gap
    lane = lax.broadcasted_iota(jnp.int32, (8, BOX_Z), 1)
    one, two, three = bufs
    centre = values[...]

    inside = (lane >= gap_z) & (lane < BOX_Z + gap_z)
    turn = jnp.where(gap_z < 0, gap_z + BOX_Z, gap_z)

    def density_block(block, _):
        parts = []
        for q in range(BLOCK):
            x = block * BLOCK + q
            base = shifted_plane(x - gap_x) - gap_y
            for t in range(TILES):
                value = shift[pl.ds(base + 8 * t, 8), :]
                value = jnp.where(inside, pltpu.roll(value, turn, 1), 0.0)
                partner[x, pl.ds(8 * t, 8), :] = value
                parts.append(value * lead[x, pl.ds(8 * t, 8), :])
        spectral = along_z(jnp.concatenate(parts, 0), weights)
        for q in range(BLOCK):
            row = stencil_row(block * BLOCK + q)
            one[pl.ds(row, BOX_Y), :] = spectral[q * BOX_Y : (q + 1) * BOX_Y]
        return 0

    lax.fori_loop(0, BOX_X // BLOCK, density_block, 0)

    sweep(one, three, centre + 6.0)
    sweep(three, one, centre)
    sweep(one, two, centre, three, 36.0)
    sweep(two, one, centre)
    sweep(one, three, centre, three, 1296.0)
    sweep(three, one, centre)
    sweep(one, two, centre)
    sweep(two, one, centre)
    sweep(one, two, centre)
    sweep(two, one, centre)
    sweep(one, two, centre, three, 46656.0)
    scale = 1.0 / (6.0 * 6.0 * 1296.0 * 46656.0)

    def potential_block(block, _):
        rows = jnp.concatenate(
            [two[pl.ds(stencil_row(block * BLOCK + q), BOX_Y), :] for q in range(BLOCK)], 0
        )
        potential = along_z(rows, weights) * scale
        for q in range(BLOCK):
            x = block * BLOCK + q
            for t in range(TILES):
                at = pl.ds(8 * t, 8)
                value = potential[q * BOX_Y + 8 * t : q * BOX_Y + 8 * t + 8]
                accum[lead_slot, x, at, :] = (
                    accum[lead_slot, x, at, :] + value * partner[x, at, :]
                )
                shift[pl.ds(shift_row(x) + 8 * t, 8), :] = value * lead[x, at, :]
        return 0

    lax.fori_loop(0, BOX_X // BLOCK, potential_block, 0)

    back_inside = (lane >= -gap_z) & (lane < BOX_Z - gap_z)
    back_turn = jnp.where(gap_z > 0, BOX_Z - gap_z, -gap_z)

    def back_block(block, _):
        for q in range(BLOCK):
            x = block * BLOCK + q
            base = shifted_plane(x + gap_x) + gap_y
            for t in range(TILES):
                at = pl.ds(8 * t, 8)
                value = shift[pl.ds(base + 8 * t, 8), :]
                value = jnp.where(back_inside, pltpu.roll(value, back_turn, 1), 0.0)
                accum[partner_slot, x, at, :] = accum[partner_slot, x, at, :] + value
        return 0

    lax.fori_loop(0, BOX_X // BLOCK, back_block, 0)


REMOTE = 4
QUOTA = 2
ROOM = 2


PIECES = [pl.ds(c * (BOX_X // CHUNKS), BOX_X // CHUNKS) for c in range(CHUNKS)]


def start_box(box, buf, arrived):
    for c, at in enumerate(PIECES):
        pltpu.make_async_copy(box.at[at], buf.at[at], arrived.at[c]).start()


def finish_box(box, target, buf, arrived, left):
    for c, at in enumerate(PIECES):
        pltpu.make_async_copy(box.at[at], buf.at[at], arrived.at[c]).wait()
        pltpu.make_async_copy(buf.at[at], target.at[at], left.at[c]).start()
    for c, at in enumerate(PIECES):
        pltpu.make_async_copy(buf.at[at], target.at[at], left.at[c]).wait()


def first_kernel(listed, count, own, payload, note, row, note_sem, buf, arrived, left):
    start_box(own.at[0], buf, arrived)
    copy = pltpu.make_async_copy(listed, row, note_sem)
    copy.start()
    copy.wait()
    lane = lax.broadcasted_iota(jnp.int32, (8, BOX_Z), 1)
    value = jnp.where(lane == 2 * SLOTS, count[0].astype(F32), 0.0)
    for e in range(SLOTS):
        for k in range(2):
            value = jnp.where(lane == 2 * e + k, row[0, k, e].astype(F32), value)
    note[...] = jnp.zeros_like(note)
    note[0:8, :] = value
    extra = pltpu.make_async_copy(note, payload.at[BOX_X], note_sem)
    extra.start()
    finish_box(own.at[0], payload, buf, arrived, left)
    extra.wait()


def second_kernel(own, target, buf, arrived, left):
    start_box(own.at[1], buf, arrived)
    finish_box(own.at[1], target, buf, arrived, left)


LIST = 1 + 5 * 2 * SLOTS


def stage_kernel(stage, *refs):
    if stage == 0:
        table, weights, values, own, mate, letter, accum, queues, *rest = refs
    elif stage == 1:
        table, left_over, weights, values, own, mate, letter, _, accum, leaving, queues, *rest = refs
    else:
        queues, weights, values, own, mate, remote, _, accum, leaving, *rest = refs
        leave_first, leave_second, *rest = rest
    sources = [own.at[0], own.at[1], mate.at[0], mate.at[1]]
    if stage == 1:
        sources.append(letter.at[pl.ds(0, BOX_X)])
    elif stage == 2:
        sources.append(remote)
    lead, shift, partner, one, two, three, sem, *rest = rest

    def clear():
        for buf in (one, two, three):
            zero_borders(buf)
        for buf in range(2):
            zero_margins(shift.at[buf])

    if stage < 2:
        note, other, note_sem = rest
        here = table[13]
        mate_id = here ^ 1
        is_left = here % 2 == 1
        across = jnp.where(is_left, here + 1, here - 1)
        page = letter.at[BOX_X] if stage else letter
        copy = pltpu.make_async_copy(page.at[pl.ds(0, 8), :], note, note_sem)
        copy.start()
        clear()
        copy.wait()
        for k in range(2 * SLOTS + 1):
            other[k] = note[0, k].astype(jnp.int32)
        queues[0] = 0
        queues[LIST] = 0

        def place(orbital):
            device = orbital // ORB_DEV
            local_slot = orbital % ORB_DEV
            return jnp.where(
                device == here, local_slot, jnp.where(device == mate_id, 2 + local_slot, REMOTE)
            )

        def push(which, wanted, lead_id, partner_id):
            @pl.when(wanted)
            def _():
                start = which * LIST
                k = queues[start]
                base = start + 1 + 5 * k
                queues[start] = k + 1
                queues[base] = place(lead_id)
                queues[base + 1] = place(partner_id)
                for axis in range(3):
                    queues[base + 2 + axis] = (
                        table[14 + 3 * partner_id + axis] - table[14 + 3 * lead_id + axis]
                    )

        rows = []
        for side in range(2):
            use_near = (here % 2 == side) if stage == 0 else (is_left if side == 0 else ~is_left)
            owner = jnp.where(use_near, here, mate_id if stage == 0 else across)
            limit = jnp.where(use_near, table[12], other[12])
            entries = []
            for e in range(SLOTS):
                a = jnp.where(use_near, table[2 * e], other[2 * e])
                b = jnp.where(use_near, table[2 * e + 1], other[2 * e + 1])
                entries.append((e < limit, a, b, a // ORB_DEV, b // ORB_DEV))
            rows.append((owner, entries))

    if stage == 0:
        inner, load = [], []
        for owner, entries in rows:
            beyond = jnp.where(owner % 2 == 1, owner + 1, owner - 1)
            crossing = jnp.int32(0)
            for live, a, b, a_dev, b_dev in entries:
                inside = live & (a_dev != beyond) & (b_dev != beyond)
                half = live & ((a_dev == beyond) != (b_dev == beyond))
                crossing = crossing + half.astype(jnp.int32)
                inner.append((inside, a, b))
            load.append(crossing)
        number = jnp.int32(0)
        for inside, _, _ in inner:
            number = number + inside.astype(jnp.int32)
        quota = jnp.where(jnp.where(here % 2 == 0, load[0], load[1]) > 1, QUOTA - 1, QUOTA)
        even_share = jnp.clip((number + load[1] - load[0] + 1) >> 1, 0, number)
        seen = jnp.int32(0)
        for inside, a, b in inner:
            mine = inside & ((seen < even_share) == (here % 2 == 0))
            push(jnp.where(queues[0] < quota, 0, 1), mine, a, b)
            seen = seen + inside.astype(jnp.int32)

    if stage == 1:
        (left, left_row), (right, right_row) = rows
        plan = []
        load_left, load_right = jnp.int32(0), jnp.int32(0)
        for side, (row, far) in enumerate(((left_row, right), (right_row, left))):
            for live, a, b, a_dev, b_dev in row:
                on_left = (a_dev == left) | (b_dev == left)
                on_right = (a_dev == right) | (b_dev == right)
                crosses = live & ((a_dev == far) != (b_dev == far))
                given = live & (a_dev == far) & (b_dev == far)
                free = crosses & on_left & on_right
                fixed = crosses & ~free
                left_bit = jnp.where(a_dev == left, a, b) % ORB_DEV
                right_bit = jnp.where(a_dev == right, a, b) % ORB_DEV
                if side == 0:
                    load_left = load_left + fixed.astype(jnp.int32)
                    load_right = load_right + given.astype(jnp.int32)
                else:
                    load_right = load_right + fixed.astype(jnp.int32)
                    load_left = load_left + given.astype(jnp.int32)
                plan.append((side, a, b, free, fixed, given, left_bit, right_bit))
        rest_of = []
        for side, a, b, free, fixed, given, left_bit, right_bit in plan:
            go_left = (load_left < load_right) | (
                (load_left == load_right) & (right_bit <= left_bit)
            )
            load_left = load_left + (free & go_left).astype(jnp.int32)
            load_right = load_right + (free & ~go_left).astype(jnp.int32)
            stays_left, stays_right = free & go_left, free & ~go_left
            if side == 0:
                stays_left = stays_left | fixed
            else:
                stays_right = stays_right | fixed
            mine = (stays_left & is_left) | (stays_right & ~is_left)
            bit = jnp.where(is_left, right_bit, left_bit)
            push(bit, mine, a, b)
            taken = given & (~is_left if side == 0 else is_left)
            rest_of.append((taken, a, b))
        for taken, a, b in rest_of:
            push(jnp.where(queues[0] < ROOM, 0, 1), taken, a, b)

        def hand_over(k, _):
            source = LIST + 1 + 5 * k
            start = jnp.where(queues[0] < ROOM, 0, LIST)
            base = start + 1 + 5 * queues[start]
            queues[start] = queues[start] + 1
            for field in range(5):
                queues[base + field] = left_over[source + field]
            return 0

        lax.fori_loop(0, left_over[LIST], hand_over, 0)

    first = LIST if stage == 2 else 0
    total = queues[first]

    def window(buf):
        return shift.at[buf].reshape(SHIFT_PLANES, WIDE, BOX_Z).at[
            pl.ds(1, BOX_X), pl.ds(MARGIN, BOX_Y), :
        ]

    def fetch(k, buf):
        for which, target in ((0, lead.at[buf]), (1, window(buf))):
            slot = queues[first + 1 + 5 * k + which]
            for s, source in enumerate(sources):
                @pl.when(slot == s)
                def _():
                    for at in PIECES:
                        pltpu.make_async_copy(
                            source.at[at], target.at[at], sem.at[which, buf]
                        ).start()

    @pl.when(total > 0)
    def _():
        fetch(0, 0)

    if stage == 0:
        for slot in range(REMOTE + 1):
            zero_box(accum.at[slot])
    if stage == 2:
        clear()

    def visit(k, _):
        buf = k % 2
        pltpu.make_async_copy(sources[0], lead.at[buf], sem.at[0, buf]).wait()
        pltpu.make_async_copy(sources[0], window(buf), sem.at[1, buf]).wait()

        @pl.when(k + 1 < total)
        def _():
            fetch(k + 1, 1 - buf)

        base = first + 1 + 5 * k
        solve_pair(
            lead.at[buf], shift.at[buf], partner, (one, two, three), weights, values,
            [queues[base + 2 + axis] for axis in range(3)], accum, queues[base], queues[base + 1],
        )
        return 0

    lax.fori_loop(0, total, visit, 0)

    if stage:
        def leave(x, _):
            for t in range(TILES):
                at = pl.ds(8 * t, 8)
                leaving[pl.ds(pl.multiple_of(x * BOX_Y + 8 * t, 8), 8), :] = accum[REMOTE, x, at, :]
                if stage == 1:
                    accum[REMOTE, x, at, :] = jnp.zeros((8, BOX_Z), F32)
                else:
                    for box in range(ORB_DEV):
                        (leave_first, leave_second)[box][x, at, :] = accum[2 + box, x, at, :]
            return 0

        lax.fori_loop(0, BOX_X, leave, 0, unroll=2)
        zero_rows(leaving, ROWS, leaving.shape[0] - ROWS)


SMEM = pl.BlockSpec(memory_space=pltpu.SMEM)
VMEM = pl.BlockSpec(memory_space=pltpu.VMEM)
HBM = pl.BlockSpec(memory_space=pltpu.HBM)


def run_stage(stage, lists, fixed, remote=(), accum=()):
    operands = [*lists, *fixed, *remote, *accum]
    specs = (
        [SMEM] * len(lists) + [VMEM] * 2 + [HBM] * 2 + [HBM] * len(remote) + [VMEM] * len(accum)
    )
    queue = jax.ShapeDtypeStruct((2 * LIST,), jnp.int32)
    leaving = ([], [(ROWS + 16, BOX_Z)], [(ROWS + 8, BOX_Z), BOX, BOX])[stage]
    shapes = [jax.ShapeDtypeStruct(shape, F32) for shape in [(REMOTE + 1,) + BOX] + leaving]
    outs = [VMEM] * len(shapes)
    scratch = [
        pltpu.VMEM((2,) + BOX, F32),
        pltpu.VMEM((2, SHIFT_ROWS, BOX_Z), F32),
        pltpu.VMEM(BOX, F32),
        pltpu.VMEM((STENCIL_ROWS, BOX_Z), F32),
        pltpu.VMEM((STENCIL_ROWS, BOX_Z), F32),
        pltpu.VMEM((STENCIL_ROWS, BOX_Z), F32),
        pltpu.SemaphoreType.DMA((2, 2)),
    ]
    if stage < 2:
        shapes.append(queue)
        outs.append(SMEM)
        scratch += [
            pltpu.SMEM((8, BOX_Z), F32),
            pltpu.SMEM((2 * SLOTS + 1,), jnp.int32),
            pltpu.SemaphoreType.DMA,
        ]
    return pl.pallas_call(
        functools.partial(stage_kernel, stage),
        out_shape=shapes,
        in_specs=specs,
        out_specs=outs,
        input_output_aliases={len(operands) - 1: 0} if accum else {},
        scratch_shapes=scratch,
        compiler_params=pltpu.CompilerParams(vmem_limit_bytes=24 << 20),
        cost_estimate=pl.CostEstimate(
            flops=1000, bytes_accessed=1000, transcendentals=0
        ),
        name="stage_" + "abc"[stage],
    )(*operands)


def total_kernel(box, accum, mate, remote, *rest):
    result, chunk, sem = rest[-3:]

    def add(x, _):
        for t in range(TILES):
            at = pl.ds(8 * t, 8)
            far = remote[pl.ds(pl.multiple_of(x * BOX_Y + 8 * t, 8), 8), :]
            chunk[x, at, :] = accum[box, x, at, :] + mate[x, at, :] + far
        pltpu.make_async_copy(chunk.at[x], result.at[box, x], sem).start()
        return 0

    lax.fori_loop(0, BOX_X, add, 0, unroll=2)
    pltpu.make_async_copy(chunk, result.at[box], sem).wait()


def run_total(box, accum, mate, remote, result=()):
    return pl.pallas_call(
        functools.partial(total_kernel, box),
        out_shape=jax.ShapeDtypeStruct((ORB_DEV,) + BOX, F32),
        in_specs=[VMEM, VMEM, VMEM] + [HBM] * len(result),
        out_specs=HBM,
        input_output_aliases={3: 0} if result else {},
        scratch_shapes=[pltpu.VMEM(BOX, F32), pltpu.SemaphoreType.DMA],
        compiler_params=pltpu.CompilerParams(vmem_limit_bytes=4 << 20),
        name="total_" + "ab"[box],
    )(accum, mate, remote, *result)


def local(orbitals, pair_list, pair_count, box_offset):
    position = lax.axis_index("orb").astype(jnp.int32)[None]
    devices = lax.axis_size("orb")
    mates = [(d, d ^ 1) for d in range(devices)]
    across = [(d, d + 1) for d in range(1, devices - 1, 2)]
    across = across + [(b, a) for a, b in across]
    staging = [
        pltpu.VMEM(BOX, F32),
        pltpu.SemaphoreType.DMA((CHUNKS,)),
        pltpu.SemaphoreType.DMA((CHUNKS,)),
    ]
    payload, note = pl.pallas_call(
        first_kernel,
        out_shape=[
            jax.ShapeDtypeStruct((BOX_X + 1, BOX_Y, BOX_Z), F32),
            jax.ShapeDtypeStruct((BOX_Y, BOX_Z), F32),
        ],
        in_specs=[HBM, SMEM, HBM],
        out_specs=[HBM, VMEM],
        scratch_shapes=[
            pltpu.SMEM((1, 2, SLOTS), jnp.int32),
            pltpu.SemaphoreType.DMA,
        ]
        + staging,
        compiler_params=pltpu.CompilerParams(vmem_limit_bytes=60 << 20),
        name="first_box",
    )(jnp.transpose(pair_list, (0, 2, 1)), pair_count, orbitals)
    far_first = lax.ppermute(payload, "orb", across)
    mate = lax.ppermute(orbitals, "orb", mates)
    mate_note = lax.ppermute(note, "orb", mates)
    second = pl.pallas_call(
        second_kernel,
        out_shape=jax.ShapeDtypeStruct(BOX, F32),
        in_specs=[HBM],
        out_specs=HBM,
        scratch_shapes=staging,
        compiler_params=pltpu.CompilerParams(vmem_limit_bytes=60 << 20),
        name="second_box",
    )(orbitals)
    far_second = lax.ppermute(second, "orb", across)
    weights, values = sine_basis()
    fixed = (jnp.asarray(weights), jnp.asarray(values), orbitals, mate)
    table = jnp.concatenate([pair_list.reshape(-1), pair_count, position, box_offset.reshape(-1)])
    accum, left_over = run_stage(0, [table], fixed, [mate_note])
    accum, for_first, later = run_stage(1, [table, left_over], fixed, [far_first], [accum])
    back_first = lax.ppermute(for_first, "orb", across)
    accum, for_second, *for_mate = run_stage(2, [later], fixed, [far_second], [accum])
    back_second = lax.ppermute(for_second, "orb", across)
    back_mate = [lax.ppermute(box, "orb", mates) for box in for_mate]
    result = run_total(0, accum, back_mate[0], back_first)
    return run_total(1, accum, back_mate[1], back_second, (result,))


def solution(mesh):
    placed = (P("orb", None, None, None), P("orb", None, None), P("orb"), P())
    return jax.shard_map(
        local, mesh=mesh, in_specs=placed, out_specs=P("orb", None, None, None), check_vma=False
    )
```

```python
import functools

import jax
import jax.numpy as jnp
import ml_dtypes
import numpy as np
from jax import lax
from jax.experimental import pallas as pl
from jax.experimental.pallas import tpu as pltpu
from jax.sharding import PartitionSpec as P

BOX_X, BOX_Y, BOX_Z = 48, 64, 128
BOX = (BOX_X, BOX_Y, BOX_Z)
ROWS = BOX_X * BOX_Y
ORB_DEV = 2
SLOTS = 6
TILES = BOX_Y // 8
PLANE = BOX_Y + 8
STENCIL_ROWS = (BOX_X + 2) * PLANE + 8
MARGIN = 24
WIDE = BOX_Y + MARGIN
SHIFT_PLANES = BOX_X + 2
SHIFT_ROWS = SHIFT_PLANES * WIDE
STENCIL_UNROLL = 8
BLOCK = 24
CHUNKS = 6
F32 = jnp.float32
BF16 = jnp.bfloat16


def sine_basis():
    k = np.arange(1, BOX_Z + 1)
    basis = np.sqrt(2.0 / (BOX_Z + 1)) * np.sin(np.pi * np.outer(k, k) / (BOX_Z + 1))
    high = basis.astype(np.float32).astype(ml_dtypes.bfloat16)
    low = (basis - high.astype(np.float64)).astype(ml_dtypes.bfloat16)
    half = np.concatenate([high, low], 1)
    weights = np.concatenate([half, half], 0)
    values = np.tile(2.0 * np.cos(np.pi * k / (BOX_Z + 1)), (8, 1)).astype(np.float32)
    return weights, values


def stencil_row(x):
    return pl.multiple_of(8 + (x + 1) * PLANE, 8)


def shift_row(x):
    return pl.multiple_of((x + 1) * WIDE + MARGIN, 8)


def shifted_plane(x):
    return jnp.where((x >= 0) & (x < BOX_X), x + 1, 0) * WIDE + MARGIN


def zero_rows(ref, first, rows):
    for k in range(rows // 8):
        ref[pl.ds(first + 8 * k, 8), :] = jnp.zeros((8, BOX_Z), F32)


def zero_margins(ref):
    zero_rows(ref, 0, WIDE)
    zero_rows(ref, SHIFT_ROWS - WIDE, WIDE)

    def plane(p, _):
        zero_rows(ref, pl.multiple_of((p + 1) * WIDE, 8), MARGIN)
        return 0

    lax.fori_loop(0, BOX_X, plane, 0, unroll=8)


def zero_borders(ref):
    zero_rows(ref, 0, 8 + PLANE)
    zero_rows(ref, STENCIL_ROWS - PLANE, PLANE)

    def plane(x, _):
        zero_rows(ref, pl.multiple_of(8 + (x + 1) * PLANE + BOX_Y, 8), 8)
        return 0

    lax.fori_loop(0, BOX_X, plane, 0, unroll=16)


def zero_box(ref):
    def plane(x, _):
        for t in range(TILES):
            ref[x, pl.ds(8 * t, 8), :] = jnp.zeros((8, BOX_Z), F32)
        return 0

    lax.fori_loop(0, BOX_X, plane, 0, unroll=2)


def sweep(source, target, centre, other=None, factor=None):
    def plane(x, carry):
        behind, here = carry
        row = stencil_row(x)
        ahead_row = stencil_row(x + 1)
        ahead = [source[pl.ds(ahead_row + 8 * t, 8), :] for t in range(TILES)]
        for t in range(TILES):
            above = source[pl.ds(row + 8 * t - 1, 8), :]
            below = source[pl.ds(row + 8 * t + 1, 8), :]
            total = (behind[t] + ahead[t]) + (above + below) + centre * here[t]
            if other is not None:
                total = total + factor * other[pl.ds(row + 8 * t, 8), :]
            target[pl.ds(row + 8 * t, 8), :] = total
        return here, ahead

    first = [source[pl.ds(stencil_row(-1) + 8 * t, 8), :] for t in range(TILES)]
    second = [source[pl.ds(stencil_row(0) + 8 * t, 8), :] for t in range(TILES)]
    lax.fori_loop(0, BOX_X, plane, (first, second), unroll=STENCIL_UNROLL)


def along_z(rows, weights):
    high = rows.astype(BF16)
    low = (rows - high.astype(F32)).astype(BF16)
    product = jnp.dot(
        jnp.concatenate([high, low], 1), weights[...], preferred_element_type=F32
    )
    return product[:, :BOX_Z] + product[:, BOX_Z:]


def solve_pair(lead, shift, partner, bufs, weights, values, gap, accum, lead_slot, partner_slot):
    gap_x, gap_y, gap_z = gap
    lane = lax.broadcasted_iota(jnp.int32, (8, BOX_Z), 1)
    one, two, three = bufs
    centre = values[...]

    inside = (lane >= gap_z) & (lane < BOX_Z + gap_z)
    turn = jnp.where(gap_z < 0, gap_z + BOX_Z, gap_z)

    def density_block(block, _):
        parts = []
        for q in range(BLOCK):
            x = block * BLOCK + q
            base = shifted_plane(x - gap_x) - gap_y
            for t in range(TILES):
                value = shift[pl.ds(base + 8 * t, 8), :]
                value = jnp.where(inside, pltpu.roll(value, turn, 1), 0.0)
                partner[x, pl.ds(8 * t, 8), :] = value
                parts.append(value * lead[x, pl.ds(8 * t, 8), :])
        spectral = along_z(jnp.concatenate(parts, 0), weights)
        for q in range(BLOCK):
            row = stencil_row(block * BLOCK + q)
            one[pl.ds(row, BOX_Y), :] = spectral[q * BOX_Y : (q + 1) * BOX_Y]
        return 0

    lax.fori_loop(0, BOX_X // BLOCK, density_block, 0)

    sweep(one, three, centre + 6.0)
    sweep(three, one, centre)
    sweep(one, two, centre, three, 36.0)
    sweep(two, one, centre)
    sweep(one, three, centre, three, 1296.0)
    sweep(three, one, centre)
    sweep(one, two, centre)
    sweep(two, one, centre)
    sweep(one, two, centre)
    sweep(two, one, centre)
    scale = 1.0 / (6.0 * 6.0 * 1296.0 * 46656.0)

    def potential_block(block, _):
        planes = [
            [one[pl.ds(stencil_row(block * BLOCK + q - 1) + 8 * t, 8), :] for t in range(TILES)]
            for q in range(BLOCK + 2)
        ]
        parts = []
        for q in range(BLOCK):
            row = stencil_row(block * BLOCK + q)
            for t in range(TILES):
                above = one[pl.ds(row + 8 * t - 1, 8), :]
                below = one[pl.ds(row + 8 * t + 1, 8), :]
                parts.append(
                    (planes[q][t] + planes[q + 2][t])
                    + (above + below)
                    + centre * planes[q + 1][t]
                    + 46656.0 * three[pl.ds(row + 8 * t, 8), :]
                )
        rows = jnp.concatenate(parts, 0)
        potential = along_z(rows, weights) * scale
        for q in range(BLOCK):
            x = block * BLOCK + q
            for t in range(TILES):
                at = pl.ds(8 * t, 8)
                value = potential[q * BOX_Y + 8 * t : q * BOX_Y + 8 * t + 8]
                accum[lead_slot, x, at, :] = (
                    accum[lead_slot, x, at, :] + value * partner[x, at, :]
                )
                shift[pl.ds(shift_row(x) + 8 * t, 8), :] = value * lead[x, at, :]
        return 0

    lax.fori_loop(0, BOX_X // BLOCK, potential_block, 0)

    back_inside = (lane >= -gap_z) & (lane < BOX_Z - gap_z)
    back_turn = jnp.where(gap_z > 0, BOX_Z - gap_z, -gap_z)

    def back_block(block, _):
        for q in range(BLOCK):
            x = block * BLOCK + q
            base = shifted_plane(x + gap_x) + gap_y
            for t in range(TILES):
                at = pl.ds(8 * t, 8)
                value = shift[pl.ds(base + 8 * t, 8), :]
                value = jnp.where(back_inside, pltpu.roll(value, back_turn, 1), 0.0)
                accum[partner_slot, x, at, :] = accum[partner_slot, x, at, :] + value
        return 0

    lax.fori_loop(0, BOX_X // BLOCK, back_block, 0)


REMOTE = 4
QUOTA = 2
ROOM = 1


PIECES = [pl.ds(c * (BOX_X // CHUNKS), BOX_X // CHUNKS) for c in range(CHUNKS)]


def start_box(box, buf, arrived):
    for c, at in enumerate(PIECES):
        pltpu.make_async_copy(box.at[at], buf.at[at], arrived.at[c]).start()


def finish_box(box, target, buf, arrived, left):
    for c, at in enumerate(PIECES):
        pltpu.make_async_copy(box.at[at], buf.at[at], arrived.at[c]).wait()
        pltpu.make_async_copy(buf.at[at], target.at[at], left.at[c]).start()
    for c, at in enumerate(PIECES):
        pltpu.make_async_copy(buf.at[at], target.at[at], left.at[c]).wait()


def first_kernel(listed, count, own, payload, note, row, note_sem, buf, arrived, left):
    start_box(own.at[0], buf, arrived)
    copy = pltpu.make_async_copy(listed, row, note_sem)
    copy.start()
    copy.wait()
    lane = lax.broadcasted_iota(jnp.int32, (8, BOX_Z), 1)
    value = jnp.where(lane == 2 * SLOTS, count[0].astype(F32), 0.0)
    for e in range(SLOTS):
        for k in range(2):
            value = jnp.where(lane == 2 * e + k, row[0, k, e].astype(F32), value)
    note[...] = jnp.zeros_like(note)
    note[0:8, :] = value
    extra = pltpu.make_async_copy(note, payload.at[BOX_X], note_sem)
    extra.start()
    finish_box(own.at[0], payload, buf, arrived, left)
    extra.wait()


def second_kernel(own, target, buf, arrived, left):
    start_box(own.at[1], buf, arrived)
    finish_box(own.at[1], target, buf, arrived, left)


LIST = 1 + 5 * 2 * SLOTS


def stage_kernel(stage, *refs):
    if stage == 0:
        table, weights, values, own, mate, letter, accum, queues, *rest = refs
    elif stage == 1:
        table, left_over, weights, values, own, mate, letter, _, accum, leaving, queues, *rest = refs
    else:
        queues, weights, values, own, mate, remote, _, accum, leaving, *rest = refs
        leave_first, leave_second, *rest = rest
    sources = [own.at[0], own.at[1], mate.at[0], mate.at[1]]
    if stage == 1:
        sources.append(letter.at[pl.ds(0, BOX_X)])
    elif stage == 2:
        sources.append(remote)
    lead, shift, partner, one, two, three, sem, *rest = rest

    def clear():
        for buf in (one, two, three):
            zero_borders(buf)
        for buf in range(2):
            zero_margins(shift.at[buf])

    if stage < 2:
        note, other, note_sem = rest
        here = table[13]
        offset = 15 - 3 * table[14]
        mate_id = here ^ 1
        is_left = here % 2 == 1
        across = jnp.where(is_left, here + 1, here - 1)
        page = letter.at[BOX_X] if stage else letter
        copy = pltpu.make_async_copy(page.at[pl.ds(0, 1), :], note, note_sem)
        copy.start()
        clear()
        copy.wait()
        for k in range(2 * SLOTS + 1):
            other[k] = note[0, k].astype(jnp.int32)
        queues[0] = 0
        queues[LIST] = 0

        def place(orbital):
            device = orbital // ORB_DEV
            local_slot = orbital % ORB_DEV
            return jnp.where(
                device == here, local_slot, jnp.where(device == mate_id, 2 + local_slot, REMOTE)
            )

        def push(which, wanted, lead_id, partner_id):
            @pl.when(wanted)
            def _():
                start = which * LIST
                k = queues[start]
                base = start + 1 + 5 * k
                queues[start] = k + 1
                queues[base] = place(lead_id)
                queues[base + 1] = place(partner_id)
                for axis in range(3):
                    queues[base + 2 + axis] = (
                        table[offset + 3 * partner_id + axis] - table[offset + 3 * lead_id + axis]
                    )

        rows = []
        for side in range(2):
            use_near = (here % 2 == side) if stage == 0 else (is_left if side == 0 else ~is_left)
            owner = jnp.where(use_near, here, mate_id if stage == 0 else across)
            limit = jnp.where(use_near, table[12], other[12])
            entries = []
            for e in range(SLOTS):
                a = jnp.where(use_near, table[2 * e], other[2 * e])
                b = jnp.where(use_near, table[2 * e + 1], other[2 * e + 1])
                entries.append((e < limit, a, b, a // ORB_DEV, b // ORB_DEV))
            rows.append((owner, entries))

    if stage == 0:
        inner, load = [], []
        for owner, entries in rows:
            beyond = jnp.where(owner % 2 == 1, owner + 1, owner - 1)
            crossing = jnp.int32(0)
            for live, a, b, a_dev, b_dev in entries:
                inside = live & (a_dev != beyond) & (b_dev != beyond)
                half = live & ((a_dev == beyond) != (b_dev == beyond))
                crossing = crossing + half.astype(jnp.int32)
                inner.append((inside, a, b))
            load.append(crossing)
        number = jnp.int32(0)
        for inside, _, _ in inner:
            number = number + inside.astype(jnp.int32)
        even_share = jnp.clip((number + load[1] - load[0] + 1) >> 1, 0, number)
        seen = jnp.int32(0)
        for inside, a, b in inner:
            mine = inside & ((seen < even_share) == (here % 2 == 0))
            push(jnp.where(queues[0] < QUOTA, 0, 1), mine, a, b)
            seen = seen + inside.astype(jnp.int32)

    if stage == 1:
        (left, left_row), (right, right_row) = rows
        plan = []
        left_has, right_has = [jnp.int32(0)] * 2, [jnp.int32(0)] * 2
        for side, (row, far) in enumerate(((left_row, right), (right_row, left))):
            for live, a, b, a_dev, b_dev in row:
                on_left = (a_dev == left) | (b_dev == left)
                on_right = (a_dev == right) | (b_dev == right)
                crosses = live & ((a_dev == far) != (b_dev == far))
                given = live & (a_dev == far) & (b_dev == far)
                free = crosses & on_left & on_right
                fixed = crosses & ~free
                left_bit = jnp.where(a_dev == left, a, b) % ORB_DEV
                right_bit = jnp.where(a_dev == right, a, b) % ORB_DEV
                for k in range(2):
                    if side == 0:
                        left_has[k] = left_has[k] + (fixed & (right_bit == k)).astype(jnp.int32)
                    else:
                        right_has[k] = right_has[k] + (fixed & (left_bit == k)).astype(jnp.int32)
                plan.append((side, a, b, free, fixed, given, left_bit, right_bit))
        rest_of = []
        for side, a, b, free, fixed, given, left_bit, right_bit in plan:
            go_left = jnp.where(right_bit == 0, *left_has) <= jnp.where(left_bit == 0, *right_has)
            for k in range(2):
                left_has[k] = left_has[k] + (free & go_left & (right_bit == k)).astype(jnp.int32)
                right_has[k] = right_has[k] + (free & ~go_left & (left_bit == k)).astype(jnp.int32)
            stays_left, stays_right = free & go_left, free & ~go_left
            if side == 0:
                stays_left = stays_left | fixed
            else:
                stays_right = stays_right | fixed
            mine = (stays_left & is_left) | (stays_right & ~is_left)
            bit = jnp.where(is_left, right_bit, left_bit)
            push(bit, mine, a, b)
            taken = given & (~is_left if side == 0 else is_left)
            rest_of.append((taken, a, b))
        for taken, a, b in rest_of:
            push(jnp.where(queues[0] < ROOM, 0, 1), taken, a, b)

        def hand_over(k, _):
            source = LIST + 1 + 5 * k
            start = jnp.where(queues[0] < ROOM, 0, LIST)
            base = start + 1 + 5 * queues[start]
            queues[start] = queues[start] + 1
            for field in range(5):
                queues[base + field] = left_over[source + field]
            return 0

        lax.fori_loop(0, left_over[LIST], hand_over, 0)

    first = LIST if stage == 2 else 0
    total = queues[first]

    def window(buf):
        return shift.at[buf].reshape(SHIFT_PLANES, WIDE, BOX_Z).at[
            pl.ds(1, BOX_X), pl.ds(MARGIN, BOX_Y), :
        ]

    def fetch(k, buf):
        for which, target in ((0, lead.at[buf]), (1, window(buf))):
            slot = queues[first + 1 + 5 * k + which]
            for s, source in enumerate(sources):
                @pl.when(slot == s)
                def _():
                    for at in PIECES:
                        pltpu.make_async_copy(
                            source.at[at], target.at[at], sem.at[which, buf]
                        ).start()

    @pl.when(total > 0)
    def _():
        fetch(0, 0)

    if stage == 0:
        for slot in range(REMOTE + 1):
            zero_box(accum.at[slot])
    if stage == 2:
        clear()

    def visit(k, _):
        buf = k % 2
        pltpu.make_async_copy(sources[0], lead.at[buf], sem.at[0, buf]).wait()
        pltpu.make_async_copy(sources[0], window(buf), sem.at[1, buf]).wait()

        @pl.when(k + 1 < total)
        def _():
            fetch(k + 1, 1 - buf)

        base = first + 1 + 5 * k
        solve_pair(
            lead.at[buf], shift.at[buf], partner, (one, two, three), weights, values,
            [queues[base + 2 + axis] for axis in range(3)], accum, queues[base], queues[base + 1],
        )
        return 0

    lax.fori_loop(0, total, visit, 0)

    if stage:
        def leave(x, _):
            for t in range(TILES):
                at = pl.ds(8 * t, 8)
                leaving[pl.ds(pl.multiple_of(x * BOX_Y + 8 * t, 8), 8), :] = accum[REMOTE, x, at, :]
                if stage == 1:
                    accum[REMOTE, x, at, :] = jnp.zeros((8, BOX_Z), F32)
                else:
                    for box in range(ORB_DEV):
                        (leave_first, leave_second)[box][x, at, :] = accum[2 + box, x, at, :]
            return 0

        lax.fori_loop(0, BOX_X, leave, 0, unroll=2)
        zero_rows(leaving, ROWS, leaving.shape[0] - ROWS)


SMEM = pl.BlockSpec(memory_space=pltpu.SMEM)
VMEM = pl.BlockSpec(memory_space=pltpu.VMEM)
HBM = pl.BlockSpec(memory_space=pltpu.HBM)


def run_stage(stage, lists, fixed, remote=(), accum=()):
    operands = [*lists, *fixed, *remote, *accum]
    specs = (
        [SMEM] * len(lists) + [VMEM] * 2 + [HBM] * 2 + [HBM] * len(remote) + [VMEM] * len(accum)
    )
    queue = jax.ShapeDtypeStruct((2 * LIST,), jnp.int32)
    leaving = ([], [(ROWS + 16, BOX_Z)], [(ROWS + 8, BOX_Z), BOX, BOX])[stage]
    shapes = [jax.ShapeDtypeStruct(shape, F32) for shape in [(REMOTE + 1,) + BOX] + leaving]
    outs = [VMEM] * len(shapes)
    scratch = [
        pltpu.VMEM((2,) + BOX, F32),
        pltpu.VMEM((2, SHIFT_ROWS, BOX_Z), F32),
        pltpu.VMEM(BOX, F32),
        pltpu.VMEM((STENCIL_ROWS, BOX_Z), F32),
        pltpu.VMEM((STENCIL_ROWS, BOX_Z), F32),
        pltpu.VMEM((STENCIL_ROWS, BOX_Z), F32),
        pltpu.SemaphoreType.DMA((2, 2)),
    ]
    if stage < 2:
        shapes.append(queue)
        outs.append(SMEM)
        scratch += [
            pltpu.SMEM((1, BOX_Z), F32),
            pltpu.SMEM((2 * SLOTS + 1,), jnp.int32),
            pltpu.SemaphoreType.DMA,
        ]
    return pl.pallas_call(
        functools.partial(stage_kernel, stage),
        out_shape=shapes,
        in_specs=specs,
        out_specs=outs,
        input_output_aliases={len(operands) - 1: 0} if accum else {},
        scratch_shapes=scratch,
        compiler_params=pltpu.CompilerParams(vmem_limit_bytes=24 << 20),
        cost_estimate=pl.CostEstimate(
            flops=1000, bytes_accessed=1000, transcendentals=0
        ),
        name="stage_" + "abc"[stage],
    )(*operands)


def total_kernel(box, accum, mate, remote, *rest):
    result, chunk, sem = rest[-3:]

    def add(x, _):
        for t in range(TILES):
            at = pl.ds(8 * t, 8)
            far = remote[pl.ds(pl.multiple_of(x * BOX_Y + 8 * t, 8), 8), :]
            chunk[x, at, :] = accum[box, x, at, :] + mate[x, at, :] + far
        pltpu.make_async_copy(chunk.at[x], result.at[box, x], sem).start()
        return 0

    lax.fori_loop(0, BOX_X, add, 0, unroll=2)
    pltpu.make_async_copy(chunk, result.at[box], sem).wait()


def run_total(box, accum, mate, remote, result=()):
    return pl.pallas_call(
        functools.partial(total_kernel, box),
        out_shape=jax.ShapeDtypeStruct((ORB_DEV,) + BOX, F32),
        in_specs=[VMEM, VMEM, VMEM] + [HBM] * len(result),
        out_specs=HBM,
        input_output_aliases={3: 0} if result else {},
        scratch_shapes=[pltpu.VMEM(BOX, F32), pltpu.SemaphoreType.DMA],
        compiler_params=pltpu.CompilerParams(vmem_limit_bytes=4 << 20),
        name="total_" + "ab"[box],
    )(accum, mate, remote, *result)


def local(orbitals, pair_list, pair_count, box_offset):
    position = lax.axis_index("orb").astype(jnp.int32)[None]
    devices = lax.axis_size("orb")
    mates = [(d, d ^ 1) for d in range(devices)]
    across = [(d, d + 1) for d in range(1, devices - 1, 2)]
    across = across + [(b, a) for a, b in across]
    staging = [
        pltpu.VMEM(BOX, F32),
        pltpu.SemaphoreType.DMA((CHUNKS,)),
        pltpu.SemaphoreType.DMA((CHUNKS,)),
    ]
    payload, note = pl.pallas_call(
        first_kernel,
        out_shape=[
            jax.ShapeDtypeStruct((BOX_X + 1, BOX_Y, BOX_Z), F32),
            jax.ShapeDtypeStruct((BOX_Y, BOX_Z), F32),
        ],
        in_specs=[HBM, SMEM, HBM],
        out_specs=[HBM, VMEM],
        scratch_shapes=[
            pltpu.SMEM((1, 2, SLOTS), jnp.int32),
            pltpu.SemaphoreType.DMA,
        ]
        + staging,
        compiler_params=pltpu.CompilerParams(vmem_limit_bytes=60 << 20),
        name="first_box",
    )(jnp.transpose(pair_list, (0, 2, 1)), pair_count, orbitals)
    far_first = lax.ppermute(payload, "orb", across)
    mate = lax.ppermute(orbitals, "orb", mates)
    mate_note = lax.ppermute(note, "orb", mates)
    second = pl.pallas_call(
        second_kernel,
        out_shape=jax.ShapeDtypeStruct(BOX, F32),
        in_specs=[HBM],
        out_specs=HBM,
        scratch_shapes=staging,
        compiler_params=pltpu.CompilerParams(vmem_limit_bytes=60 << 20),
        name="second_box",
    )(orbitals)
    far_second = lax.ppermute(second, "orb", across)
    weights, values = sine_basis()
    fixed = (jnp.asarray(weights), jnp.asarray(values), orbitals, mate)
    nearest = jnp.clip(ORB_DEV * (position - 3), 0, ORB_DEV * (devices - 7))
    offsets = lax.dynamic_slice(box_offset, (nearest[0], 0), (7 * ORB_DEV, 3)).reshape(-1)
    table = jnp.concatenate([pair_list.reshape(-1), pair_count, position, nearest, offsets])
    accum, left_over = run_stage(0, [table], fixed, [mate_note])
    accum, for_first, later = run_stage(1, [table, left_over], fixed, [far_first], [accum])
    back_first = lax.ppermute(for_first, "orb", across)
    accum, for_second, *for_mate = run_stage(2, [later], fixed, [far_second], [accum])
    back_second = lax.ppermute(for_second, "orb", across)
    back_mate = [lax.ppermute(box, "orb", mates) for box in for_mate]
    result = run_total(0, accum, back_mate[0], back_first)
    return run_total(1, accum, back_mate[1], back_second, (result,))


def solution(mesh):
    placed = (P("orb", None, None, None), P("orb", None, None), P("orb"), P())
    return jax.shard_map(
        local, mesh=mesh, in_specs=placed, out_specs=P("orb", None, None, None), check_vma=False
    )
```

```python
import functools

import jax
import jax.numpy as jnp
import ml_dtypes
import numpy as np
from jax import lax
from jax.experimental import pallas as pl
from jax.experimental.pallas import tpu as pltpu
from jax.sharding import PartitionSpec as P

BOX_X, BOX_Y, BOX_Z = 48, 64, 128
BOX = (BOX_X, BOX_Y, BOX_Z)
ROWS = BOX_X * BOX_Y
ORB_DEV = 2
SLOTS = 6
TILES = BOX_Y // 8
PLANE = BOX_Y + 8
STENCIL_ROWS = (BOX_X + 2) * PLANE + 8
MARGIN = 24
WIDE = BOX_Y + MARGIN
SHIFT_PLANES = BOX_X + 2
SHIFT_ROWS = SHIFT_PLANES * WIDE
STENCIL_UNROLL = 24
BLOCK = 24
CHUNKS = 6
F32 = jnp.float32
BF16 = jnp.bfloat16


def sine_basis():
    k = np.arange(1, BOX_Z + 1)
    basis = np.sqrt(2.0 / (BOX_Z + 1)) * np.sin(np.pi * np.outer(k, k) / (BOX_Z + 1))
    high = basis.astype(np.float32).astype(ml_dtypes.bfloat16)
    low = (basis - high.astype(np.float64)).astype(ml_dtypes.bfloat16)
    half = np.concatenate([high, low], 1)
    weights = np.concatenate([half, half], 0)
    values = np.tile(2.0 * np.cos(np.pi * k / (BOX_Z + 1)), (8, 1)).astype(np.float32)
    return weights, values


def stencil_row(x):
    return pl.multiple_of(8 + (x + 1) * PLANE, 8)


def shift_row(x):
    return pl.multiple_of((x + 1) * WIDE + MARGIN, 8)


def shifted_plane(x):
    return jnp.where((x >= 0) & (x < BOX_X), x + 1, 0) * WIDE + MARGIN


def zero_rows(ref, first, rows):
    for k in range(rows // 8):
        ref[pl.ds(first + 8 * k, 8), :] = jnp.zeros((8, BOX_Z), F32)


def zero_margins(ref):
    zero_rows(ref, 0, WIDE)
    zero_rows(ref, SHIFT_ROWS - WIDE, WIDE)

    def plane(p, _):
        zero_rows(ref, pl.multiple_of((p + 1) * WIDE, 8), MARGIN)
        return 0

    lax.fori_loop(0, BOX_X, plane, 0, unroll=8)


def zero_borders(ref):
    zero_rows(ref, 0, 8 + PLANE)
    zero_rows(ref, STENCIL_ROWS - PLANE, PLANE)

    def plane(x, _):
        zero_rows(ref, pl.multiple_of(8 + (x + 1) * PLANE + BOX_Y, 8), 8)
        return 0

    lax.fori_loop(0, BOX_X, plane, 0, unroll=16)


def zero_box(ref):
    def plane(x, _):
        for t in range(TILES):
            ref[x, pl.ds(8 * t, 8), :] = jnp.zeros((8, BOX_Z), F32)
        return 0

    lax.fori_loop(0, BOX_X, plane, 0, unroll=2)


def sweep(source, target, centre, other=None, factor=None):
    def plane(x, carry):
        behind, here = carry
        row = stencil_row(x)
        ahead_row = stencil_row(x + 1)
        ahead = [source[pl.ds(ahead_row + 8 * t, 8), :] for t in range(TILES)]
        for t in range(TILES):
            above = source[pl.ds(row + 8 * t - 1, 8), :]
            below = source[pl.ds(row + 8 * t + 1, 8), :]
            total = (behind[t] + ahead[t]) + (above + below) + centre * here[t]
            if other is not None:
                total = total + factor * other[pl.ds(row + 8 * t, 8), :]
            target[pl.ds(row + 8 * t, 8), :] = total
        return here, ahead

    first = [source[pl.ds(stencil_row(-1) + 8 * t, 8), :] for t in range(TILES)]
    second = [source[pl.ds(stencil_row(0) + 8 * t, 8), :] for t in range(TILES)]
    lax.fori_loop(0, BOX_X, plane, (first, second), unroll=STENCIL_UNROLL)


def along_z(rows, weights):
    high = rows.astype(BF16)
    low = (rows - high.astype(F32)).astype(BF16)
    product = jnp.dot(
        jnp.concatenate([high, low], 1), weights[...], preferred_element_type=F32
    )
    return product[:, :BOX_Z] + product[:, BOX_Z:]


def solve_pair(lead, shift, partner, bufs, weights, values, gap, accum, lead_slot, partner_slot):
    gap_x, gap_y, gap_z = gap
    lane = lax.broadcasted_iota(jnp.int32, (8, BOX_Z), 1)
    one, two, three = bufs
    centre = values[...]

    inside = (lane >= gap_z) & (lane < BOX_Z + gap_z)
    turn = jnp.where(gap_z < 0, gap_z + BOX_Z, gap_z)

    def density_block(block, _):
        parts = []
        for q in range(BLOCK):
            x = block * BLOCK + q
            base = shifted_plane(x - gap_x) - gap_y
            for t in range(TILES):
                value = shift[pl.ds(base + 8 * t, 8), :]
                value = jnp.where(inside, pltpu.roll(value, turn, 1), 0.0)
                partner[x, pl.ds(8 * t, 8), :] = value
                parts.append(value * lead[x, pl.ds(8 * t, 8), :])
        spectral = along_z(jnp.concatenate(parts, 0), weights)
        for q in range(BLOCK):
            row = stencil_row(block * BLOCK + q)
            one[pl.ds(row, BOX_Y), :] = spectral[q * BOX_Y : (q + 1) * BOX_Y]
        return 0

    lax.fori_loop(0, BOX_X // BLOCK, density_block, 0)

    sweep(one, three, centre + 6.0)
    sweep(three, one, centre)
    sweep(one, two, centre, three, 36.0)
    sweep(two, one, centre)
    sweep(one, three, centre, three, 1296.0)
    sweep(three, one, centre)
    sweep(one, two, centre)
    sweep(two, one, centre)
    sweep(one, two, centre)
    sweep(two, one, centre)
    scale = 1.0 / (6.0 * 6.0 * 1296.0 * 46656.0)

    def potential_block(block, _):
        planes = [
            [one[pl.ds(stencil_row(block * BLOCK + q - 1) + 8 * t, 8), :] for t in range(TILES)]
            for q in range(BLOCK + 2)
        ]
        parts = []
        for q in range(BLOCK):
            row = stencil_row(block * BLOCK + q)
            for t in range(TILES):
                above = one[pl.ds(row + 8 * t - 1, 8), :]
                below = one[pl.ds(row + 8 * t + 1, 8), :]
                parts.append(
                    (planes[q][t] + planes[q + 2][t])
                    + (above + below)
                    + centre * planes[q + 1][t]
                    + 46656.0 * three[pl.ds(row + 8 * t, 8), :]
                )
        rows = jnp.concatenate(parts, 0)
        potential = along_z(rows, weights) * scale
        for q in range(BLOCK):
            x = block * BLOCK + q
            for t in range(TILES):
                at = pl.ds(8 * t, 8)
                value = potential[q * BOX_Y + 8 * t : q * BOX_Y + 8 * t + 8]
                accum[lead_slot, x, at, :] = (
                    accum[lead_slot, x, at, :] + value * partner[x, at, :]
                )
                shift[pl.ds(shift_row(x) + 8 * t, 8), :] = value * lead[x, at, :]
        return 0

    lax.fori_loop(0, BOX_X // BLOCK, potential_block, 0)

    back_inside = (lane >= -gap_z) & (lane < BOX_Z - gap_z)
    back_turn = jnp.where(gap_z > 0, BOX_Z - gap_z, -gap_z)

    def back_block(block, _):
        for q in range(BLOCK):
            x = block * BLOCK + q
            base = shifted_plane(x + gap_x) + gap_y
            for t in range(TILES):
                at = pl.ds(8 * t, 8)
                value = shift[pl.ds(base + 8 * t, 8), :]
                value = jnp.where(back_inside, pltpu.roll(value, back_turn, 1), 0.0)
                accum[partner_slot, x, at, :] = accum[partner_slot, x, at, :] + value
        return 0

    lax.fori_loop(0, BOX_X // BLOCK, back_block, 0)


REMOTE = 4
QUOTA = 2
ROOM = 1


PIECES = [pl.ds(c * (BOX_X // CHUNKS), BOX_X // CHUNKS) for c in range(CHUNKS)]


def start_box(box, buf, arrived):
    for c, at in enumerate(PIECES):
        pltpu.make_async_copy(box.at[at], buf.at[at], arrived.at[c]).start()


def finish_box(box, target, buf, arrived, left):
    for c, at in enumerate(PIECES):
        pltpu.make_async_copy(box.at[at], buf.at[at], arrived.at[c]).wait()
        pltpu.make_async_copy(buf.at[at], target.at[at], left.at[c]).start()
    for c, at in enumerate(PIECES):
        pltpu.make_async_copy(buf.at[at], target.at[at], left.at[c]).wait()


def first_kernel(listed, count, own, payload, note, row, note_sem, buf, arrived, left):
    start_box(own.at[0], buf, arrived)
    copy = pltpu.make_async_copy(listed, row, note_sem)
    copy.start()
    copy.wait()
    lane = lax.broadcasted_iota(jnp.int32, (8, BOX_Z), 1)
    value = jnp.where(lane == 2 * SLOTS, count[0].astype(F32), 0.0)
    for e in range(SLOTS):
        for k in range(2):
            value = jnp.where(lane == 2 * e + k, row[0, k, e].astype(F32), value)
    note[...] = jnp.zeros_like(note)
    note[0:8, :] = value
    extra = pltpu.make_async_copy(note, payload.at[BOX_X], note_sem)
    extra.start()
    finish_box(own.at[0], payload, buf, arrived, left)
    extra.wait()


def second_kernel(own, target, buf, arrived, left):
    start_box(own.at[1], buf, arrived)
    finish_box(own.at[1], target, buf, arrived, left)


LIST = 1 + 5 * 2 * SLOTS


def stage_kernel(stage, *refs):
    if stage == 0:
        table, weights, values, own, mate, letter, accum, queues, *rest = refs
    elif stage == 1:
        table, left_over, weights, values, own, mate, letter, _, accum, leaving, queues, *rest = refs
    else:
        queues, weights, values, own, mate, remote, _, accum, leaving, *rest = refs
        leave_first, leave_second, *rest = rest
    sources = [own.at[0], own.at[1], mate.at[0], mate.at[1]]
    if stage == 1:
        sources.append(letter.at[pl.ds(0, BOX_X)])
    elif stage == 2:
        sources.append(remote)
    lead, shift, partner, one, two, three, sem, *rest = rest

    def clear():
        for buf in (one, two, three):
            zero_borders(buf)
        for buf in range(2):
            zero_margins(shift.at[buf])

    if stage < 2:
        note, other, note_sem = rest
        here = table[13]
        offset = 15 - 3 * table[14]
        mate_id = here ^ 1
        is_left = here % 2 == 1
        across = jnp.where(is_left, here + 1, here - 1)
        page = letter.at[BOX_X] if stage else letter
        copy = pltpu.make_async_copy(page.at[pl.ds(0, 1), :], note, note_sem)
        copy.start()
        clear()
        copy.wait()
        for k in range(2 * SLOTS + 1):
            other[k] = note[0, k].astype(jnp.int32)
        queues[0] = 0
        queues[LIST] = 0

        def place(orbital):
            device = orbital // ORB_DEV
            local_slot = orbital % ORB_DEV
            return jnp.where(
                device == here, local_slot, jnp.where(device == mate_id, 2 + local_slot, REMOTE)
            )

        def push(which, wanted, lead_id, partner_id):
            @pl.when(wanted)
            def _():
                start = which * LIST
                k = queues[start]
                base = start + 1 + 5 * k
                queues[start] = k + 1
                queues[base] = place(lead_id)
                queues[base + 1] = place(partner_id)
                for axis in range(3):
                    queues[base + 2 + axis] = (
                        table[offset + 3 * partner_id + axis] - table[offset + 3 * lead_id + axis]
                    )

        rows = []
        for side in range(2):
            use_near = (here % 2 == side) if stage == 0 else (is_left if side == 0 else ~is_left)
            owner = jnp.where(use_near, here, mate_id if stage == 0 else across)
            limit = jnp.where(use_near, table[12], other[12])
            entries = []
            for e in range(SLOTS):
                a = jnp.where(use_near, table[2 * e], other[2 * e])
                b = jnp.where(use_near, table[2 * e + 1], other[2 * e + 1])
                entries.append((e < limit, a, b, a // ORB_DEV, b // ORB_DEV))
            rows.append((owner, entries))

    if stage == 0:
        inner, load = [], []
        for owner, entries in rows:
            beyond = jnp.where(owner % 2 == 1, owner + 1, owner - 1)
            crossing = jnp.int32(0)
            for live, a, b, a_dev, b_dev in entries:
                inside = live & (a_dev != beyond) & (b_dev != beyond)
                half = live & ((a_dev == beyond) != (b_dev == beyond))
                crossing = crossing + half.astype(jnp.int32)
                inner.append((inside, a, b))
            load.append(crossing)
        number = jnp.int32(0)
        for inside, _, _ in inner:
            number = number + inside.astype(jnp.int32)
        even_share = jnp.clip((number + load[1] - load[0] + 1) >> 1, 0, number)
        seen = jnp.int32(0)
        for inside, a, b in inner:
            mine = inside & ((seen < even_share) == (here % 2 == 0))
            push(jnp.where(queues[0] < QUOTA, 0, 1), mine, a, b)
            seen = seen + inside.astype(jnp.int32)

    if stage == 1:
        (left, left_row), (right, right_row) = rows
        plan = []
        left_has, right_has = [jnp.int32(0)] * 2, [jnp.int32(0)] * 2
        for side, (row, far) in enumerate(((left_row, right), (right_row, left))):
            for live, a, b, a_dev, b_dev in row:
                on_left = (a_dev == left) | (b_dev == left)
                on_right = (a_dev == right) | (b_dev == right)
                crosses = live & ((a_dev == far) != (b_dev == far))
                given = live & (a_dev == far) & (b_dev == far)
                free = crosses & on_left & on_right
                fixed = crosses & ~free
                left_bit = jnp.where(a_dev == left, a, b) % ORB_DEV
                right_bit = jnp.where(a_dev == right, a, b) % ORB_DEV
                for k in range(2):
                    if side == 0:
                        left_has[k] = left_has[k] + (fixed & (right_bit == k)).astype(jnp.int32)
                    else:
                        right_has[k] = right_has[k] + (fixed & (left_bit == k)).astype(jnp.int32)
                plan.append((side, a, b, free, fixed, given, left_bit, right_bit))
        rest_of = []
        for side, a, b, free, fixed, given, left_bit, right_bit in plan:
            go_left = jnp.where(right_bit == 0, *left_has) <= jnp.where(left_bit == 0, *right_has)
            for k in range(2):
                left_has[k] = left_has[k] + (free & go_left & (right_bit == k)).astype(jnp.int32)
                right_has[k] = right_has[k] + (free & ~go_left & (left_bit == k)).astype(jnp.int32)
            stays_left, stays_right = free & go_left, free & ~go_left
            if side == 0:
                stays_left = stays_left | fixed
            else:
                stays_right = stays_right | fixed
            mine = (stays_left & is_left) | (stays_right & ~is_left)
            bit = jnp.where(is_left, right_bit, left_bit)
            push(bit, mine, a, b)
            taken = given & (~is_left if side == 0 else is_left)
            rest_of.append((taken, a, b))
        for taken, a, b in rest_of:
            push(jnp.where(queues[0] < ROOM, 0, 1), taken, a, b)

        def hand_over(k, _):
            source = LIST + 1 + 5 * k
            start = jnp.where(queues[0] < ROOM, 0, LIST)
            base = start + 1 + 5 * queues[start]
            queues[start] = queues[start] + 1
            for field in range(5):
                queues[base + field] = left_over[source + field]
            return 0

        lax.fori_loop(0, left_over[LIST], hand_over, 0)

    first = LIST if stage == 2 else 0
    total = queues[first]

    def window(buf):
        return shift.at[buf].reshape(SHIFT_PLANES, WIDE, BOX_Z).at[
            pl.ds(1, BOX_X), pl.ds(MARGIN, BOX_Y), :
        ]

    def fetch(k, buf):
        for which, target in ((0, lead.at[buf]), (1, window(buf))):
            slot = queues[first + 1 + 5 * k + which]
            for s, source in enumerate(sources):
                @pl.when(slot == s)
                def _():
                    for at in PIECES:
                        pltpu.make_async_copy(
                            source.at[at], target.at[at], sem.at[which, buf]
                        ).start()

    @pl.when(total > 0)
    def _():
        fetch(0, 0)

    if stage == 0:
        for slot in range(REMOTE + 1):
            zero_box(accum.at[slot])
    if stage == 2:
        clear()

    def visit(k, _):
        buf = k % 2
        pltpu.make_async_copy(sources[0], lead.at[buf], sem.at[0, buf]).wait()
        pltpu.make_async_copy(sources[0], window(buf), sem.at[1, buf]).wait()

        @pl.when(k + 1 < total)
        def _():
            fetch(k + 1, 1 - buf)

        base = first + 1 + 5 * k
        solve_pair(
            lead.at[buf], shift.at[buf], partner, (one, two, three), weights, values,
            [queues[base + 2 + axis] for axis in range(3)], accum, queues[base], queues[base + 1],
        )
        return 0

    lax.fori_loop(0, total, visit, 0)

    if stage:
        def leave(x, _):
            for t in range(TILES):
                at = pl.ds(8 * t, 8)
                leaving[pl.ds(pl.multiple_of(x * BOX_Y + 8 * t, 8), 8), :] = accum[REMOTE, x, at, :]
                if stage == 1:
                    accum[REMOTE, x, at, :] = jnp.zeros((8, BOX_Z), F32)
                else:
                    for box in range(ORB_DEV):
                        (leave_first, leave_second)[box][x, at, :] = accum[2 + box, x, at, :]
            return 0

        lax.fori_loop(0, BOX_X, leave, 0, unroll=2)
        zero_rows(leaving, ROWS, leaving.shape[0] - ROWS)


SMEM = pl.BlockSpec(memory_space=pltpu.SMEM)
VMEM = pl.BlockSpec(memory_space=pltpu.VMEM)
HBM = pl.BlockSpec(memory_space=pltpu.HBM)


def run_stage(stage, lists, fixed, remote=(), accum=()):
    operands = [*lists, *fixed, *remote, *accum]
    specs = (
        [SMEM] * len(lists) + [VMEM] * 2 + [HBM] * 2 + [HBM] * len(remote) + [VMEM] * len(accum)
    )
    queue = jax.ShapeDtypeStruct((2 * LIST,), jnp.int32)
    leaving = ([], [(ROWS + 16, BOX_Z)], [(ROWS + 8, BOX_Z), BOX, BOX])[stage]
    shapes = [jax.ShapeDtypeStruct(shape, F32) for shape in [(REMOTE + 1,) + BOX] + leaving]
    outs = [VMEM] * len(shapes)
    scratch = [
        pltpu.VMEM((2,) + BOX, F32),
        pltpu.VMEM((2, SHIFT_ROWS, BOX_Z), F32),
        pltpu.VMEM(BOX, F32),
        pltpu.VMEM((STENCIL_ROWS, BOX_Z), F32),
        pltpu.VMEM((STENCIL_ROWS, BOX_Z), F32),
        pltpu.VMEM((STENCIL_ROWS, BOX_Z), F32),
        pltpu.SemaphoreType.DMA((2, 2)),
    ]
    if stage < 2:
        shapes.append(queue)
        outs.append(SMEM)
        scratch += [
            pltpu.SMEM((1, BOX_Z), F32),
            pltpu.SMEM((2 * SLOTS + 1,), jnp.int32),
            pltpu.SemaphoreType.DMA,
        ]
    return pl.pallas_call(
        functools.partial(stage_kernel, stage),
        out_shape=shapes,
        in_specs=specs,
        out_specs=outs,
        input_output_aliases={len(operands) - 1: 0} if accum else {},
        scratch_shapes=scratch,
        compiler_params=pltpu.CompilerParams(vmem_limit_bytes=24 << 20),
        cost_estimate=pl.CostEstimate(
            flops=1000, bytes_accessed=1000, transcendentals=0
        ),
        name="stage_" + "abc"[stage],
    )(*operands)


def total_kernel(box, accum, mate, remote, *rest):
    result, chunk, sem = rest[-3:]

    def add(x, _):
        for t in range(TILES):
            at = pl.ds(8 * t, 8)
            far = remote[pl.ds(pl.multiple_of(x * BOX_Y + 8 * t, 8), 8), :]
            chunk[x, at, :] = accum[box, x, at, :] + mate[x, at, :] + far
        pltpu.make_async_copy(chunk.at[x], result.at[box, x], sem).start()
        return 0

    lax.fori_loop(0, BOX_X, add, 0, unroll=2)
    pltpu.make_async_copy(chunk, result.at[box], sem).wait()


def run_total(box, accum, mate, remote, result=()):
    return pl.pallas_call(
        functools.partial(total_kernel, box),
        out_shape=jax.ShapeDtypeStruct((ORB_DEV,) + BOX, F32),
        in_specs=[VMEM, VMEM, VMEM] + [HBM] * len(result),
        out_specs=HBM,
        input_output_aliases={3: 0} if result else {},
        scratch_shapes=[pltpu.VMEM(BOX, F32), pltpu.SemaphoreType.DMA],
        compiler_params=pltpu.CompilerParams(vmem_limit_bytes=4 << 20),
        name="total_" + "ab"[box],
    )(accum, mate, remote, *result)


def local(orbitals, pair_list, pair_count, box_offset):
    position = lax.axis_index("orb").astype(jnp.int32)[None]
    devices = lax.axis_size("orb")
    mates = [(d, d ^ 1) for d in range(devices)]
    across = [(d, d + 1) for d in range(1, devices - 1, 2)]
    across = across + [(b, a) for a, b in across]
    staging = [
        pltpu.VMEM(BOX, F32),
        pltpu.SemaphoreType.DMA((CHUNKS,)),
        pltpu.SemaphoreType.DMA((CHUNKS,)),
    ]
    payload, note = pl.pallas_call(
        first_kernel,
        out_shape=[
            jax.ShapeDtypeStruct((BOX_X + 1, BOX_Y, BOX_Z), F32),
            jax.ShapeDtypeStruct((BOX_Y, BOX_Z), F32),
        ],
        in_specs=[HBM, SMEM, HBM],
        out_specs=[HBM, VMEM],
        scratch_shapes=[
            pltpu.SMEM((1, 2, SLOTS), jnp.int32),
            pltpu.SemaphoreType.DMA,
        ]
        + staging,
        compiler_params=pltpu.CompilerParams(vmem_limit_bytes=60 << 20),
        name="first_box",
    )(jnp.transpose(pair_list, (0, 2, 1)), pair_count, orbitals)
    payload, held = lax.optimization_barrier((payload, orbitals))
    far_first = lax.ppermute(payload, "orb", across)
    mate = lax.ppermute(held, "orb", mates)
    mate_note = lax.ppermute(note, "orb", mates)
    second = pl.pallas_call(
        second_kernel,
        out_shape=jax.ShapeDtypeStruct(BOX, F32),
        in_specs=[HBM],
        out_specs=HBM,
        scratch_shapes=staging,
        compiler_params=pltpu.CompilerParams(vmem_limit_bytes=60 << 20),
        name="second_box",
    )(orbitals)
    far_second = lax.ppermute(second, "orb", across)
    weights, values = sine_basis()
    fixed = (jnp.asarray(weights), jnp.asarray(values), orbitals, mate)
    nearest = jnp.clip(ORB_DEV * (position - 3), 0, ORB_DEV * (devices - 7))
    offsets = lax.dynamic_slice(box_offset, (nearest[0], 0), (7 * ORB_DEV, 3)).reshape(-1)
    table = jnp.concatenate([pair_list.reshape(-1), pair_count, position, nearest, offsets])
    accum, left_over = run_stage(0, [table], fixed, [mate_note])
    accum, for_first, later = run_stage(1, [table, left_over], fixed, [far_first], [accum])
    back_first = lax.ppermute(for_first, "orb", across)
    accum, for_second, *for_mate = run_stage(2, [later], fixed, [far_second], [accum])
    back_second = lax.ppermute(for_second, "orb", across)
    back_mate = [lax.ppermute(box, "orb", mates) for box in for_mate]
    result = run_total(0, accum, back_mate[0], back_first)
    return run_total(1, accum, back_mate[1], back_second, (result,))


def solution(mesh):
    placed = (P("orb", None, None, None), P("orb", None, None), P("orb"), P())
    return jax.shard_map(
        local, mesh=mesh, in_specs=placed, out_specs=P("orb", None, None, None), check_vma=False
    )
```

```python
import functools

import jax
import jax.numpy as jnp
import ml_dtypes
import numpy as np
from jax import lax
from jax.experimental import pallas as pl
from jax.experimental.pallas import tpu as pltpu
from jax.sharding import PartitionSpec as P

BOX_X, BOX_Y, BOX_Z = 48, 64, 128
BOX = (BOX_X, BOX_Y, BOX_Z)
ROWS = BOX_X * BOX_Y
ORB_DEV = 2
SLOTS = 6
TILES = BOX_Y // 8
PLANE = BOX_Y + 8
STENCIL_ROWS = (BOX_X + 2) * PLANE + 8
MARGIN = 24
WIDE = BOX_Y + MARGIN
SHIFT_PLANES = BOX_X + 2
SHIFT_ROWS = SHIFT_PLANES * WIDE
STENCIL_UNROLL = 24
BLOCK = 24
CHUNKS = 6
F32 = jnp.float32
BF16 = jnp.bfloat16


def sine_basis():
    k = np.arange(1, BOX_Z + 1)
    basis = np.sqrt(2.0 / (BOX_Z + 1)) * np.sin(np.pi * np.outer(k, k) / (BOX_Z + 1))
    high = basis.astype(np.float32).astype(ml_dtypes.bfloat16)
    low = (basis - high.astype(np.float64)).astype(ml_dtypes.bfloat16)
    half = np.concatenate([high, low], 1)
    weights = np.concatenate([half, half], 0)
    values = np.tile(2.0 * np.cos(np.pi * k / (BOX_Z + 1)), (8, 1)).astype(np.float32)
    return weights, values


def stencil_row(x):
    return pl.multiple_of(8 + (x + 1) * PLANE, 8)


def shift_row(x):
    return pl.multiple_of((x + 1) * WIDE + MARGIN, 8)


def shifted_plane(x):
    return jnp.where((x >= 0) & (x < BOX_X), x + 1, 0) * WIDE + MARGIN


def zero_rows(ref, first, rows):
    for k in range(rows // 8):
        ref[pl.ds(first + 8 * k, 8), :] = jnp.zeros((8, BOX_Z), F32)


def zero_margins(ref):
    zero_rows(ref, 0, WIDE)
    zero_rows(ref, SHIFT_ROWS - WIDE, WIDE)

    def plane(p, _):
        zero_rows(ref, pl.multiple_of((p + 1) * WIDE, 8), MARGIN)
        return 0

    lax.fori_loop(0, BOX_X, plane, 0, unroll=8)


def zero_borders(ref):
    zero_rows(ref, 0, 8 + PLANE)
    zero_rows(ref, STENCIL_ROWS - PLANE, PLANE)

    def plane(x, _):
        zero_rows(ref, pl.multiple_of(8 + (x + 1) * PLANE + BOX_Y, 8), 8)
        return 0

    lax.fori_loop(0, BOX_X, plane, 0, unroll=16)


def zero_box(ref):
    def plane(x, _):
        for t in range(TILES):
            ref[x, pl.ds(8 * t, 8), :] = jnp.zeros((8, BOX_Z), F32)
        return 0

    lax.fori_loop(0, BOX_X, plane, 0, unroll=2)


def sweep(source, target, centre, other=None, factor=None):
    def plane(x, carry):
        behind, here = carry
        row = stencil_row(x)
        ahead_row = stencil_row(x + 1)
        ahead = [source[pl.ds(ahead_row + 8 * t, 8), :] for t in range(TILES)]
        for t in range(TILES):
            above = source[pl.ds(row + 8 * t - 1, 8), :]
            below = source[pl.ds(row + 8 * t + 1, 8), :]
            total = (behind[t] + ahead[t]) + (above + below) + centre * here[t]
            if other is not None:
                total = total + factor * other[pl.ds(row + 8 * t, 8), :]
            target[pl.ds(row + 8 * t, 8), :] = total
        return here, ahead

    first = [source[pl.ds(stencil_row(-1) + 8 * t, 8), :] for t in range(TILES)]
    second = [source[pl.ds(stencil_row(0) + 8 * t, 8), :] for t in range(TILES)]
    lax.fori_loop(0, BOX_X, plane, (first, second), unroll=STENCIL_UNROLL)


def along_z(rows, weights):
    high = rows.astype(BF16)
    low = (rows - high.astype(F32)).astype(BF16)
    product = jnp.dot(
        jnp.concatenate([high, low], 1), weights[...], preferred_element_type=F32
    )
    return product[:, :BOX_Z] + product[:, BOX_Z:]


def solve_pair(lead, shift, partner, bufs, weights, values, gap, accum, lead_slot, partner_slot):
    gap_x, gap_y, gap_z = gap
    lane = lax.broadcasted_iota(jnp.int32, (8, BOX_Z), 1)
    one, two, three = bufs
    centre = values[...]

    inside = (lane >= gap_z) & (lane < BOX_Z + gap_z)
    turn = jnp.where(gap_z < 0, gap_z + BOX_Z, gap_z)

    def density_block(block, _):
        parts = []
        for q in range(BLOCK):
            x = block * BLOCK + q
            base = shifted_plane(x - gap_x) - gap_y
            for t in range(TILES):
                value = shift[pl.ds(base + 8 * t, 8), :]
                value = jnp.where(inside, pltpu.roll(value, turn, 1), 0.0)
                partner[x, pl.ds(8 * t, 8), :] = value
                parts.append(value * lead[x, pl.ds(8 * t, 8), :])
        spectral = along_z(jnp.concatenate(parts, 0), weights)
        for q in range(BLOCK):
            row = stencil_row(block * BLOCK + q)
            one[pl.ds(row, BOX_Y), :] = spectral[q * BOX_Y : (q + 1) * BOX_Y]
        return 0

    lax.fori_loop(0, BOX_X // BLOCK, density_block, 0)

    sweep(one, three, centre + 6.0)
    sweep(three, one, centre)
    sweep(one, two, centre, three, 36.0)
    sweep(two, one, centre)
    sweep(one, three, centre, three, 1296.0)
    sweep(three, one, centre)
    sweep(one, two, centre)
    sweep(two, one, centre)
    sweep(one, two, centre)
    sweep(two, one, centre)
    scale = 1.0 / (6.0 * 6.0 * 1296.0 * 46656.0)

    def potential_block(block, _):
        planes = [
            [one[pl.ds(stencil_row(block * BLOCK + q - 1) + 8 * t, 8), :] for t in range(TILES)]
            for q in range(BLOCK + 2)
        ]
        parts = []
        for q in range(BLOCK):
            row = stencil_row(block * BLOCK + q)
            for t in range(TILES):
                above = one[pl.ds(row + 8 * t - 1, 8), :]
                below = one[pl.ds(row + 8 * t + 1, 8), :]
                parts.append(
                    (planes[q][t] + planes[q + 2][t])
                    + (above + below)
                    + centre * planes[q + 1][t]
                    + 46656.0 * three[pl.ds(row + 8 * t, 8), :]
                )
        rows = jnp.concatenate(parts, 0)
        potential = along_z(rows, weights) * scale
        for q in range(BLOCK):
            x = block * BLOCK + q
            for t in range(TILES):
                at = pl.ds(8 * t, 8)
                value = potential[q * BOX_Y + 8 * t : q * BOX_Y + 8 * t + 8]
                accum[lead_slot, x, at, :] = (
                    accum[lead_slot, x, at, :] + value * partner[x, at, :]
                )
                shift[pl.ds(shift_row(x) + 8 * t, 8), :] = value * lead[x, at, :]
        return 0

    lax.fori_loop(0, BOX_X // BLOCK, potential_block, 0)

    back_inside = (lane >= -gap_z) & (lane < BOX_Z - gap_z)
    back_turn = jnp.where(gap_z > 0, BOX_Z - gap_z, -gap_z)

    def back_block(block, _):
        for q in range(BLOCK):
            x = block * BLOCK + q
            base = shifted_plane(x + gap_x) + gap_y
            for t in range(TILES):
                at = pl.ds(8 * t, 8)
                value = shift[pl.ds(base + 8 * t, 8), :]
                value = jnp.where(back_inside, pltpu.roll(value, back_turn, 1), 0.0)
                accum[partner_slot, x, at, :] = accum[partner_slot, x, at, :] + value
        return 0

    lax.fori_loop(0, BOX_X // BLOCK, back_block, 0)


REMOTE = 4
QUOTA = 2
ROOM = 1


PIECES = [pl.ds(c * (BOX_X // CHUNKS), BOX_X // CHUNKS) for c in range(CHUNKS)]


def start_box(box, buf, arrived):
    for c, at in enumerate(PIECES):
        pltpu.make_async_copy(box.at[at], buf.at[at], arrived.at[c]).start()


def finish_box(box, target, buf, arrived, left):
    for c, at in enumerate(PIECES):
        pltpu.make_async_copy(box.at[at], buf.at[at], arrived.at[c]).wait()
        pltpu.make_async_copy(buf.at[at], target.at[at], left.at[c]).start()
    for c, at in enumerate(PIECES):
        pltpu.make_async_copy(buf.at[at], target.at[at], left.at[c]).wait()


def first_kernel(listed, count, own, payload, note, row, page, note_sem, buf, arrived, left):
    start_box(own.at[0], buf, arrived)
    copy = pltpu.make_async_copy(listed, row, note_sem.at[0])
    copy.start()
    copy.wait()
    lane = lax.broadcasted_iota(jnp.int32, (8, BOX_Z), 1)
    value = jnp.where(lane == 2 * SLOTS, count[0].astype(F32), 0.0)
    for e in range(SLOTS):
        for k in range(2):
            value = jnp.where(lane == 2 * e + k, row[0, k, e].astype(F32), value)
    page[...] = jnp.zeros_like(page)
    page[0:8, :] = value
    extras = [
        pltpu.make_async_copy(page, payload.at[BOX_X], note_sem.at[0]),
        pltpu.make_async_copy(page.at[pl.ds(0, 8)], note, note_sem.at[1]),
    ]
    for extra in extras:
        extra.start()
    finish_box(own.at[0], payload, buf, arrived, left)
    for extra in extras:
        extra.wait()


def second_kernel(own, target, buf, arrived, left):
    start_box(own.at[1], buf, arrived)
    finish_box(own.at[1], target, buf, arrived, left)


LIST = 1 + 5 * 2 * SLOTS


def stage_kernel(stage, *refs):
    if stage == 0:
        table, weights, values, own, mate, letter, accum, queues, *rest = refs
    elif stage == 1:
        table, left_over, weights, values, own, mate, letter, _, accum, leaving, queues, *rest = refs
    else:
        queues, weights, values, own, mate, remote, _, accum, leaving, *rest = refs
        leave_first, leave_second, *rest = rest
    sources = [own.at[0], own.at[1], mate.at[0], mate.at[1]]
    if stage == 1:
        sources.append(letter.at[pl.ds(0, BOX_X)])
    elif stage == 2:
        sources.append(remote)
    lead, shift, partner, one, two, three, sem, *rest = rest

    def clear():
        for buf in (one, two, three):
            zero_borders(buf)
        for buf in range(2):
            zero_margins(shift.at[buf])

    if stage < 2:
        note, other, note_sem = rest
        here = table[13]
        offset = 15 - 3 * table[14]
        mate_id = here ^ 1
        is_left = here % 2 == 1
        across = jnp.where(is_left, here + 1, here - 1)
        page = letter.at[BOX_X] if stage else letter
        copy = pltpu.make_async_copy(page.at[pl.ds(0, 1), :], note, note_sem)
        copy.start()
        clear()
        copy.wait()
        for k in range(2 * SLOTS + 1):
            other[k] = note[0, k].astype(jnp.int32)
        queues[0] = 0
        queues[LIST] = 0

        def place(orbital):
            device = orbital // ORB_DEV
            local_slot = orbital % ORB_DEV
            return jnp.where(
                device == here, local_slot, jnp.where(device == mate_id, 2 + local_slot, REMOTE)
            )

        def push(which, wanted, lead_id, partner_id):
            @pl.when(wanted)
            def _():
                start = which * LIST
                k = queues[start]
                base = start + 1 + 5 * k
                queues[start] = k + 1
                queues[base] = place(lead_id)
                queues[base + 1] = place(partner_id)
                for axis in range(3):
                    queues[base + 2 + axis] = (
                        table[offset + 3 * partner_id + axis] - table[offset + 3 * lead_id + axis]
                    )

        rows = []
        for side in range(2):
            use_near = (here % 2 == side) if stage == 0 else (is_left if side == 0 else ~is_left)
            owner = jnp.where(use_near, here, mate_id if stage == 0 else across)
            limit = jnp.where(use_near, table[12], other[12])
            entries = []
            for e in range(SLOTS):
                a = jnp.where(use_near, table[2 * e], other[2 * e])
                b = jnp.where(use_near, table[2 * e + 1], other[2 * e + 1])
                entries.append((e < limit, a, b, a // ORB_DEV, b // ORB_DEV))
            rows.append((owner, entries))

    if stage == 0:
        inner, load = [], []
        for owner, entries in rows:
            beyond = jnp.where(owner % 2 == 1, owner + 1, owner - 1)
            crossing = jnp.int32(0)
            for live, a, b, a_dev, b_dev in entries:
                inside = live & (a_dev != beyond) & (b_dev != beyond)
                half = live & ((a_dev == beyond) != (b_dev == beyond))
                crossing = crossing + half.astype(jnp.int32)
                inner.append((inside, a, b))
            load.append(crossing)
        number = jnp.int32(0)
        for inside, _, _ in inner:
            number = number + inside.astype(jnp.int32)
        even_share = jnp.clip((number + load[1] - load[0] + 1) >> 1, 0, number)
        seen = jnp.int32(0)
        for inside, a, b in inner:
            mine = inside & ((seen < even_share) == (here % 2 == 0))
            push(jnp.where(queues[0] < QUOTA, 0, 1), mine, a, b)
            seen = seen + inside.astype(jnp.int32)

    if stage == 1:
        (left, left_row), (right, right_row) = rows
        plan = []
        left_has, right_has = [jnp.int32(0)] * 2, [jnp.int32(0)] * 2
        for side, (row, far) in enumerate(((left_row, right), (right_row, left))):
            for live, a, b, a_dev, b_dev in row:
                on_left = (a_dev == left) | (b_dev == left)
                on_right = (a_dev == right) | (b_dev == right)
                crosses = live & ((a_dev == far) != (b_dev == far))
                given = live & (a_dev == far) & (b_dev == far)
                free = crosses & on_left & on_right
                fixed = crosses & ~free
                left_bit = jnp.where(a_dev == left, a, b) % ORB_DEV
                right_bit = jnp.where(a_dev == right, a, b) % ORB_DEV
                for k in range(2):
                    if side == 0:
                        left_has[k] = left_has[k] + (fixed & (right_bit == k)).astype(jnp.int32)
                    else:
                        right_has[k] = right_has[k] + (fixed & (left_bit == k)).astype(jnp.int32)
                plan.append((side, a, b, free, fixed, given, left_bit, right_bit))
        rest_of = []
        for side, a, b, free, fixed, given, left_bit, right_bit in plan:
            go_left = jnp.where(right_bit == 0, *left_has) <= jnp.where(left_bit == 0, *right_has)
            for k in range(2):
                left_has[k] = left_has[k] + (free & go_left & (right_bit == k)).astype(jnp.int32)
                right_has[k] = right_has[k] + (free & ~go_left & (left_bit == k)).astype(jnp.int32)
            stays_left, stays_right = free & go_left, free & ~go_left
            if side == 0:
                stays_left = stays_left | fixed
            else:
                stays_right = stays_right | fixed
            mine = (stays_left & is_left) | (stays_right & ~is_left)
            bit = jnp.where(is_left, right_bit, left_bit)
            push(bit, mine, a, b)
            taken = given & (~is_left if side == 0 else is_left)
            rest_of.append((taken, a, b))
        for taken, a, b in rest_of:
            push(jnp.where(queues[0] < ROOM, 0, 1), taken, a, b)

        def hand_over(k, _):
            source = LIST + 1 + 5 * k
            start = jnp.where(queues[0] < ROOM, 0, LIST)
            base = start + 1 + 5 * queues[start]
            queues[start] = queues[start] + 1
            for field in range(5):
                queues[base + field] = left_over[source + field]
            return 0

        lax.fori_loop(0, left_over[LIST], hand_over, 0)

    first = LIST if stage == 2 else 0
    total = queues[first]

    def window(buf):
        return shift.at[buf].reshape(SHIFT_PLANES, WIDE, BOX_Z).at[
            pl.ds(1, BOX_X), pl.ds(MARGIN, BOX_Y), :
        ]

    def fetch(k, buf):
        for which, target in ((0, lead.at[buf]), (1, window(buf))):
            slot = queues[first + 1 + 5 * k + which]
            for s, source in enumerate(sources):
                @pl.when(slot == s)
                def _():
                    for at in PIECES:
                        pltpu.make_async_copy(
                            source.at[at], target.at[at], sem.at[which, buf]
                        ).start()

    @pl.when(total > 0)
    def _():
        fetch(0, 0)

    if stage == 0:
        for slot in range(REMOTE + 1):
            zero_box(accum.at[slot])
    if stage == 2:
        clear()

    def visit(k, _):
        buf = k % 2
        pltpu.make_async_copy(sources[0], lead.at[buf], sem.at[0, buf]).wait()
        pltpu.make_async_copy(sources[0], window(buf), sem.at[1, buf]).wait()

        @pl.when(k + 1 < total)
        def _():
            fetch(k + 1, 1 - buf)

        base = first + 1 + 5 * k
        solve_pair(
            lead.at[buf], shift.at[buf], partner, (one, two, three), weights, values,
            [queues[base + 2 + axis] for axis in range(3)], accum, queues[base], queues[base + 1],
        )
        return 0

    lax.fori_loop(0, total, visit, 0)

    if stage:
        def leave(x, _):
            for t in range(TILES):
                at = pl.ds(8 * t, 8)
                leaving[pl.ds(pl.multiple_of(x * BOX_Y + 8 * t, 8), 8), :] = accum[REMOTE, x, at, :]
                if stage == 1:
                    accum[REMOTE, x, at, :] = jnp.zeros((8, BOX_Z), F32)
                else:
                    for box in range(ORB_DEV):
                        (leave_first, leave_second)[box][x, at, :] = accum[2 + box, x, at, :]
            return 0

        lax.fori_loop(0, BOX_X, leave, 0, unroll=2)
        zero_rows(leaving, ROWS, leaving.shape[0] - ROWS)


SMEM = pl.BlockSpec(memory_space=pltpu.SMEM)
VMEM = pl.BlockSpec(memory_space=pltpu.VMEM)
HBM = pl.BlockSpec(memory_space=pltpu.HBM)


def run_stage(stage, lists, fixed, remote=(), accum=()):
    operands = [*lists, *fixed, *remote, *accum]
    specs = (
        [SMEM] * len(lists) + [VMEM] * 2 + [HBM] * 2 + [HBM] * len(remote) + [VMEM] * len(accum)
    )
    queue = jax.ShapeDtypeStruct((2 * LIST,), jnp.int32)
    leaving = ([], [(ROWS + 16, BOX_Z)], [(ROWS + 8, BOX_Z), BOX, BOX])[stage]
    shapes = [jax.ShapeDtypeStruct(shape, F32) for shape in [(REMOTE + 1,) + BOX] + leaving]
    outs = [VMEM] * len(shapes)
    scratch = [
        pltpu.VMEM((2,) + BOX, F32),
        pltpu.VMEM((2, SHIFT_ROWS, BOX_Z), F32),
        pltpu.VMEM(BOX, F32),
        pltpu.VMEM((STENCIL_ROWS, BOX_Z), F32),
        pltpu.VMEM((STENCIL_ROWS, BOX_Z), F32),
        pltpu.VMEM((STENCIL_ROWS, BOX_Z), F32),
        pltpu.SemaphoreType.DMA((2, 2)),
    ]
    if stage < 2:
        shapes.append(queue)
        outs.append(SMEM)
        scratch += [
            pltpu.SMEM((1, BOX_Z), F32),
            pltpu.SMEM((2 * SLOTS + 1,), jnp.int32),
            pltpu.SemaphoreType.DMA,
        ]
    return pl.pallas_call(
        functools.partial(stage_kernel, stage),
        out_shape=shapes,
        in_specs=specs,
        out_specs=outs,
        input_output_aliases={len(operands) - 1: 0} if accum else {},
        scratch_shapes=scratch,
        compiler_params=pltpu.CompilerParams(vmem_limit_bytes=24 << 20),
        cost_estimate=pl.CostEstimate(
            flops=1000, bytes_accessed=1000, transcendentals=0
        ),
        name="stage_" + "abc"[stage],
    )(*operands)


def total_kernel(box, accum, mate, remote, *rest):
    result, chunk, sem = rest[-3:]

    def add(x, _):
        for t in range(TILES):
            at = pl.ds(8 * t, 8)
            far = remote[pl.ds(pl.multiple_of(x * BOX_Y + 8 * t, 8), 8), :]
            chunk[x, at, :] = accum[box, x, at, :] + mate[x, at, :] + far
        pltpu.make_async_copy(chunk.at[x], result.at[box, x], sem).start()
        return 0

    lax.fori_loop(0, BOX_X, add, 0, unroll=2)
    pltpu.make_async_copy(chunk, result.at[box], sem).wait()


def run_total(box, accum, mate, remote, result=()):
    return pl.pallas_call(
        functools.partial(total_kernel, box),
        out_shape=jax.ShapeDtypeStruct((ORB_DEV,) + BOX, F32),
        in_specs=[VMEM, VMEM, VMEM] + [HBM] * len(result),
        out_specs=HBM,
        input_output_aliases={3: 0} if result else {},
        scratch_shapes=[pltpu.VMEM(BOX, F32), pltpu.SemaphoreType.DMA],
        compiler_params=pltpu.CompilerParams(vmem_limit_bytes=4 << 20),
        name="total_" + "ab"[box],
    )(accum, mate, remote, *result)


def local(orbitals, pair_list, pair_count, box_offset):
    position = lax.axis_index("orb").astype(jnp.int32)[None]
    devices = lax.axis_size("orb")
    mates = [(d, d ^ 1) for d in range(devices)]
    across = [(d, d + 1) for d in range(1, devices - 1, 2)]
    across = across + [(b, a) for a, b in across]
    staging = [
        pltpu.VMEM(BOX, F32),
        pltpu.SemaphoreType.DMA((CHUNKS,)),
        pltpu.SemaphoreType.DMA((CHUNKS,)),
    ]
    payload, note = pl.pallas_call(
        first_kernel,
        out_shape=[
            jax.ShapeDtypeStruct((BOX_X + 1, BOX_Y, BOX_Z), F32),
            jax.ShapeDtypeStruct((8, BOX_Z), F32),
        ],
        in_specs=[HBM, SMEM, HBM],
        out_specs=[HBM, HBM],
        scratch_shapes=[
            pltpu.SMEM((1, 2, SLOTS), jnp.int32),
            pltpu.VMEM((BOX_Y, BOX_Z), F32),
            pltpu.SemaphoreType.DMA((2,)),
        ]
        + staging,
        compiler_params=pltpu.CompilerParams(vmem_limit_bytes=60 << 20),
        name="first_box",
    )(jnp.transpose(pair_list, (0, 2, 1)), pair_count, orbitals)
    payload, held = lax.optimization_barrier((payload, orbitals))
    far_first = lax.ppermute(payload, "orb", across)
    mate = lax.ppermute(held, "orb", mates)
    mate_note = lax.ppermute(note, "orb", mates)
    second = pl.pallas_call(
        second_kernel,
        out_shape=jax.ShapeDtypeStruct(BOX, F32),
        in_specs=[HBM],
        out_specs=HBM,
        scratch_shapes=staging,
        compiler_params=pltpu.CompilerParams(vmem_limit_bytes=60 << 20),
        name="second_box",
    )(orbitals)
    far_second = lax.ppermute(second, "orb", across)
    weights, values = sine_basis()
    fixed = (jnp.asarray(weights), jnp.asarray(values), orbitals, mate)
    nearest = jnp.clip(ORB_DEV * (position - 3), 0, ORB_DEV * (devices - 7))
    offsets = lax.dynamic_slice(box_offset, (nearest[0], 0), (7 * ORB_DEV, 3)).reshape(-1)
    table = jnp.concatenate([pair_list.reshape(-1), pair_count, position, nearest, offsets])
    accum, left_over = run_stage(0, [table], fixed, [mate_note])
    accum, for_first, later = run_stage(1, [table, left_over], fixed, [far_first], [accum])
    back_first = lax.ppermute(for_first, "orb", across)
    accum, for_second, *for_mate = run_stage(2, [later], fixed, [far_second], [accum])
    back_second = lax.ppermute(for_second, "orb", across)
    back_mate = [lax.ppermute(box, "orb", mates) for box in for_mate]
    result = run_total(0, accum, back_mate[0], back_first)
    return run_total(1, accum, back_mate[1], back_second, (result,))


def solution(mesh):
    placed = (P("orb", None, None, None), P("orb", None, None), P("orb"), P())
    return jax.shard_map(
        local, mesh=mesh, in_specs=placed, out_specs=P("orb", None, None, None), check_vma=False
    )
```

```python
import functools

import jax
import jax.numpy as jnp
import ml_dtypes
import numpy as np
from jax import lax
from jax.experimental import pallas as pl
from jax.experimental.pallas import tpu as pltpu
from jax.sharding import PartitionSpec as P

BOX_X, BOX_Y, BOX_Z = 48, 64, 128
BOX = (BOX_X, BOX_Y, BOX_Z)
ROWS = BOX_X * BOX_Y
ORB_DEV = 2
SLOTS = 6
TILES = BOX_Y // 8
PLANE = BOX_Y + 8
STENCIL_ROWS = (BOX_X + 2) * PLANE + 8
MARGIN = 24
WIDE = BOX_Y + MARGIN
SHIFT_PLANES = BOX_X + 2
SHIFT_ROWS = SHIFT_PLANES * WIDE
STENCIL_UNROLL = 24
BLOCK = 24
CHUNKS = 6
F32 = jnp.float32
BF16 = jnp.bfloat16


def sine_basis():
    k = np.arange(1, BOX_Z + 1)
    basis = np.sqrt(2.0 / (BOX_Z + 1)) * np.sin(np.pi * np.outer(k, k) / (BOX_Z + 1))
    high = basis.astype(np.float32).astype(ml_dtypes.bfloat16)
    low = (basis - high.astype(np.float64)).astype(ml_dtypes.bfloat16)
    half = np.concatenate([high, low], 1)
    weights = np.concatenate([half, half], 0)
    values = np.tile(2.0 * np.cos(np.pi * k / (BOX_Z + 1)), (8, 1)).astype(np.float32)
    return weights, values


def stencil_row(x):
    return pl.multiple_of(8 + (x + 1) * PLANE, 8)


def shift_row(x):
    return pl.multiple_of((x + 1) * WIDE + MARGIN, 8)


def shifted_plane(x):
    return jnp.where((x >= 0) & (x < BOX_X), x + 1, 0) * WIDE + MARGIN


def zero_rows(ref, first, rows):
    for k in range(rows // 8):
        ref[pl.ds(first + 8 * k, 8), :] = jnp.zeros((8, BOX_Z), F32)


def zero_margins(ref):
    zero_rows(ref, 0, WIDE)
    zero_rows(ref, SHIFT_ROWS - WIDE, WIDE)

    def plane(p, _):
        zero_rows(ref, pl.multiple_of((p + 1) * WIDE, 8), MARGIN)
        return 0

    lax.fori_loop(0, BOX_X, plane, 0, unroll=8)


def zero_borders(ref):
    zero_rows(ref, 0, 8 + PLANE)
    zero_rows(ref, STENCIL_ROWS - PLANE, PLANE)

    def plane(x, _):
        zero_rows(ref, pl.multiple_of(8 + (x + 1) * PLANE + BOX_Y, 8), 8)
        return 0

    lax.fori_loop(0, BOX_X, plane, 0, unroll=16)


def zero_box(ref):
    def plane(x, _):
        for t in range(TILES):
            ref[x, pl.ds(8 * t, 8), :] = jnp.zeros((8, BOX_Z), F32)
        return 0

    lax.fori_loop(0, BOX_X, plane, 0, unroll=8)


def sweep(source, target, centre, other=None, factor=None):
    def plane(x, carry):
        behind, here = carry
        row = stencil_row(x)
        ahead_row = stencil_row(x + 1)
        ahead = [source[pl.ds(ahead_row + 8 * t, 8), :] for t in range(TILES)]
        for t in range(TILES):
            above = source[pl.ds(row + 8 * t - 1, 8), :]
            below = source[pl.ds(row + 8 * t + 1, 8), :]
            total = (behind[t] + ahead[t]) + (above + below) + centre * here[t]
            if other is not None:
                total = total + factor * other[pl.ds(row + 8 * t, 8), :]
            target[pl.ds(row + 8 * t, 8), :] = total
        return here, ahead

    first = [source[pl.ds(stencil_row(-1) + 8 * t, 8), :] for t in range(TILES)]
    second = [source[pl.ds(stencil_row(0) + 8 * t, 8), :] for t in range(TILES)]
    lax.fori_loop(0, BOX_X, plane, (first, second), unroll=STENCIL_UNROLL)


def along_z(rows, weights):
    high = rows.astype(BF16)
    low = (rows - high.astype(F32)).astype(BF16)
    product = jnp.dot(
        jnp.concatenate([high, low], 1), weights[...], preferred_element_type=F32
    )
    return product[:, :BOX_Z] + product[:, BOX_Z:]


def solve_pair(lead, shift, partner, bufs, weights, values, gap, accum, lead_slot, partner_slot):
    gap_x, gap_y, gap_z = gap
    lane = lax.broadcasted_iota(jnp.int32, (8, BOX_Z), 1)
    one, two, three = bufs
    centre = values[...]

    inside = (lane >= gap_z) & (lane < BOX_Z + gap_z)
    turn = jnp.where(gap_z < 0, gap_z + BOX_Z, gap_z)

    def density_block(block, _):
        parts = []
        for q in range(BLOCK):
            x = block * BLOCK + q
            base = shifted_plane(x - gap_x) - gap_y
            for t in range(TILES):
                value = shift[pl.ds(base + 8 * t, 8), :]
                value = jnp.where(inside, pltpu.roll(value, turn, 1), 0.0)
                partner[x, pl.ds(8 * t, 8), :] = value
                parts.append(value * lead[x, pl.ds(8 * t, 8), :])
        spectral = along_z(jnp.concatenate(parts, 0), weights)
        for q in range(BLOCK):
            row = stencil_row(block * BLOCK + q)
            one[pl.ds(row, BOX_Y), :] = spectral[q * BOX_Y : (q + 1) * BOX_Y]
        return 0

    lax.fori_loop(0, BOX_X // BLOCK, density_block, 0)

    sweep(one, three, centre + 6.0)
    sweep(three, one, centre)
    sweep(one, two, centre, three, 36.0)
    sweep(two, one, centre)
    sweep(one, three, centre, three, 1296.0)
    sweep(three, one, centre)
    sweep(one, two, centre)
    sweep(two, one, centre)
    sweep(one, two, centre)
    sweep(two, one, centre)
    scale = 1.0 / (6.0 * 6.0 * 1296.0 * 46656.0)

    def potential_block(block, _):
        planes = [
            [one[pl.ds(stencil_row(block * BLOCK + q - 1) + 8 * t, 8), :] for t in range(TILES)]
            for q in range(BLOCK + 2)
        ]
        parts = []
        for q in range(BLOCK):
            row = stencil_row(block * BLOCK + q)
            for t in range(TILES):
                above = one[pl.ds(row + 8 * t - 1, 8), :]
                below = one[pl.ds(row + 8 * t + 1, 8), :]
                parts.append(
                    (planes[q][t] + planes[q + 2][t])
                    + (above + below)
                    + centre * planes[q + 1][t]
                    + 46656.0 * three[pl.ds(row + 8 * t, 8), :]
                )
        rows = jnp.concatenate(parts, 0)
        potential = along_z(rows, weights) * scale
        for q in range(BLOCK):
            x = block * BLOCK + q
            for t in range(TILES):
                at = pl.ds(8 * t, 8)
                value = potential[q * BOX_Y + 8 * t : q * BOX_Y + 8 * t + 8]
                accum[lead_slot, x, at, :] = (
                    accum[lead_slot, x, at, :] + value * partner[x, at, :]
                )
                shift[pl.ds(shift_row(x) + 8 * t, 8), :] = value * lead[x, at, :]
        return 0

    lax.fori_loop(0, BOX_X // BLOCK, potential_block, 0)

    back_inside = (lane >= -gap_z) & (lane < BOX_Z - gap_z)
    back_turn = jnp.where(gap_z > 0, BOX_Z - gap_z, -gap_z)

    def back_block(block, _):
        for q in range(BLOCK):
            x = block * BLOCK + q
            base = shifted_plane(x + gap_x) + gap_y
            for t in range(TILES):
                at = pl.ds(8 * t, 8)
                value = shift[pl.ds(base + 8 * t, 8), :]
                value = jnp.where(back_inside, pltpu.roll(value, back_turn, 1), 0.0)
                accum[partner_slot, x, at, :] = accum[partner_slot, x, at, :] + value
        return 0

    lax.fori_loop(0, BOX_X // BLOCK, back_block, 0)


REMOTE = 4
QUOTA = 2
ROOM = 1


PIECES = [pl.ds(c * (BOX_X // CHUNKS), BOX_X // CHUNKS) for c in range(CHUNKS)]


def start_box(box, buf, arrived):
    for c, at in enumerate(PIECES):
        pltpu.make_async_copy(box.at[at], buf.at[at], arrived.at[c]).start()


def finish_box(box, target, buf, arrived, left):
    for c, at in enumerate(PIECES):
        pltpu.make_async_copy(box.at[at], buf.at[at], arrived.at[c]).wait()
        pltpu.make_async_copy(buf.at[at], target.at[at], left.at[c]).start()
    for c, at in enumerate(PIECES):
        pltpu.make_async_copy(buf.at[at], target.at[at], left.at[c]).wait()


def first_kernel(listed, count, own, payload, note, row, page, note_sem, buf, arrived, left):
    start_box(own.at[0], buf, arrived)
    copy = pltpu.make_async_copy(listed, row, note_sem.at[0])
    copy.start()
    copy.wait()
    lane = lax.broadcasted_iota(jnp.int32, (8, BOX_Z), 1)
    value = jnp.where(lane == 2 * SLOTS, count[0].astype(F32), 0.0)
    for e in range(SLOTS):
        for k in range(2):
            value = jnp.where(lane == 2 * e + k, row[0, k, e].astype(F32), value)
    page[...] = jnp.zeros_like(page)
    page[0:8, :] = value
    extras = [
        pltpu.make_async_copy(page, payload.at[BOX_X], note_sem.at[0]),
        pltpu.make_async_copy(page.at[pl.ds(0, 8)], note, note_sem.at[1]),
    ]
    for extra in extras:
        extra.start()
    finish_box(own.at[0], payload, buf, arrived, left)
    for extra in extras:
        extra.wait()


def second_kernel(own, target, buf, arrived, left):
    start_box(own.at[1], buf, arrived)
    finish_box(own.at[1], target, buf, arrived, left)


LIST = 1 + 5 * 2 * SLOTS


def stage_kernel(stage, *refs):
    if stage == 0:
        table, weights, values, own, mate, letter, accum, queues, *rest = refs
    elif stage == 1:
        table, left_over, weights, values, own, mate, letter, _, accum, leaving, queues, *rest = refs
    else:
        queues, weights, values, own, mate, remote, _, accum, leaving, *rest = refs
        leave_first, leave_second, *rest = rest
    sources = [own.at[0], own.at[1], mate.at[0], mate.at[1]]
    if stage == 1:
        sources.append(letter.at[pl.ds(0, BOX_X)])
    elif stage == 2:
        sources.append(remote)
    lead, shift, partner, one, two, three, sem, *rest = rest

    def clear():
        for buf in (one, two, three):
            zero_borders(buf)
        for buf in range(2):
            zero_margins(shift.at[buf])

    if stage < 2:
        note, other, note_sem = rest
        here = table[13]
        offset = 15 - 3 * table[14]
        mate_id = here ^ 1
        is_left = here % 2 == 1
        across = jnp.where(is_left, here + 1, here - 1)
        page = letter.at[BOX_X] if stage else letter
        copy = pltpu.make_async_copy(page.at[pl.ds(0, 1), :], note, note_sem)
        copy.start()
        clear()
        copy.wait()
        for k in range(2 * SLOTS + 1):
            other[k] = note[0, k].astype(jnp.int32)
        queues[0] = 0
        queues[LIST] = 0

        def place(orbital):
            device = orbital // ORB_DEV
            local_slot = orbital % ORB_DEV
            return jnp.where(
                device == here, local_slot, jnp.where(device == mate_id, 2 + local_slot, REMOTE)
            )

        def push(which, wanted, lead_id, partner_id):
            @pl.when(wanted)
            def _():
                start = which * LIST
                k = queues[start]
                base = start + 1 + 5 * k
                queues[start] = k + 1
                queues[base] = place(lead_id)
                queues[base + 1] = place(partner_id)
                for axis in range(3):
                    queues[base + 2 + axis] = (
                        table[offset + 3 * partner_id + axis] - table[offset + 3 * lead_id + axis]
                    )

        rows = []
        for side in range(2):
            use_near = (here % 2 == side) if stage == 0 else (is_left if side == 0 else ~is_left)
            owner = jnp.where(use_near, here, mate_id if stage == 0 else across)
            limit = jnp.where(use_near, table[12], other[12])
            entries = []
            for e in range(SLOTS):
                a = jnp.where(use_near, table[2 * e], other[2 * e])
                b = jnp.where(use_near, table[2 * e + 1], other[2 * e + 1])
                entries.append((e < limit, a, b, a // ORB_DEV, b // ORB_DEV))
            rows.append((owner, entries))

    if stage == 0:
        inner, load = [], []
        for owner, entries in rows:
            beyond = jnp.where(owner % 2 == 1, owner + 1, owner - 1)
            crossing = jnp.int32(0)
            for live, a, b, a_dev, b_dev in entries:
                inside = live & (a_dev != beyond) & (b_dev != beyond)
                half = live & ((a_dev == beyond) != (b_dev == beyond))
                crossing = crossing + half.astype(jnp.int32)
                inner.append((inside, a, b))
            load.append(crossing)
        number = jnp.int32(0)
        for inside, _, _ in inner:
            number = number + inside.astype(jnp.int32)
        even_share = jnp.clip((number + load[1] - load[0] + 1) >> 1, 0, number)
        seen = jnp.int32(0)
        for inside, a, b in inner:
            mine = inside & ((seen < even_share) == (here % 2 == 0))
            push(jnp.where(queues[0] < QUOTA, 0, 1), mine, a, b)
            seen = seen + inside.astype(jnp.int32)

    if stage == 1:
        (left, left_row), (right, right_row) = rows
        plan = []
        left_has, right_has = [jnp.int32(0)] * 2, [jnp.int32(0)] * 2
        for side, (row, far) in enumerate(((left_row, right), (right_row, left))):
            for live, a, b, a_dev, b_dev in row:
                on_left = (a_dev == left) | (b_dev == left)
                on_right = (a_dev == right) | (b_dev == right)
                crosses = live & ((a_dev == far) != (b_dev == far))
                given = live & (a_dev == far) & (b_dev == far)
                free = crosses & on_left & on_right
                fixed = crosses & ~free
                left_bit = jnp.where(a_dev == left, a, b) % ORB_DEV
                right_bit = jnp.where(a_dev == right, a, b) % ORB_DEV
                for k in range(2):
                    if side == 0:
                        left_has[k] = left_has[k] + (fixed & (right_bit == k)).astype(jnp.int32)
                    else:
                        right_has[k] = right_has[k] + (fixed & (left_bit == k)).astype(jnp.int32)
                plan.append((side, a, b, free, fixed, given, left_bit, right_bit))
        rest_of = []
        for side, a, b, free, fixed, given, left_bit, right_bit in plan:
            go_left = jnp.where(right_bit == 0, *left_has) <= jnp.where(left_bit == 0, *right_has)
            for k in range(2):
                left_has[k] = left_has[k] + (free & go_left & (right_bit == k)).astype(jnp.int32)
                right_has[k] = right_has[k] + (free & ~go_left & (left_bit == k)).astype(jnp.int32)
            stays_left, stays_right = free & go_left, free & ~go_left
            if side == 0:
                stays_left = stays_left | fixed
            else:
                stays_right = stays_right | fixed
            mine = (stays_left & is_left) | (stays_right & ~is_left)
            bit = jnp.where(is_left, right_bit, left_bit)
            push(bit, mine, a, b)
            taken = given & (~is_left if side == 0 else is_left)
            rest_of.append((taken, a, b))
        for taken, a, b in rest_of:
            push(jnp.where(queues[0] < ROOM, 0, 1), taken, a, b)

        def hand_over(k, _):
            source = LIST + 1 + 5 * k
            start = jnp.where(queues[0] < ROOM, 0, LIST)
            base = start + 1 + 5 * queues[start]
            queues[start] = queues[start] + 1
            for field in range(5):
                queues[base + field] = left_over[source + field]
            return 0

        lax.fori_loop(0, left_over[LIST], hand_over, 0)

    first = LIST if stage == 2 else 0
    total = queues[first]

    def window(buf):
        return shift.at[buf].reshape(SHIFT_PLANES, WIDE, BOX_Z).at[
            pl.ds(1, BOX_X), pl.ds(MARGIN, BOX_Y), :
        ]

    def fetch(k, buf):
        for which, target in ((0, lead.at[buf]), (1, window(buf))):
            slot = queues[first + 1 + 5 * k + which]
            for s, source in enumerate(sources):
                @pl.when(slot == s)
                def _():
                    for at in PIECES:
                        pltpu.make_async_copy(
                            source.at[at], target.at[at], sem.at[which, buf]
                        ).start()

    @pl.when(total > 0)
    def _():
        fetch(0, 0)

    if stage == 0:
        for slot in range(REMOTE + 1):
            zero_box(accum.at[slot])
    if stage == 2:
        clear()

    def visit(k, _):
        buf = k % 2
        pltpu.make_async_copy(sources[0], lead.at[buf], sem.at[0, buf]).wait()
        pltpu.make_async_copy(sources[0], window(buf), sem.at[1, buf]).wait()

        @pl.when(k + 1 < total)
        def _():
            fetch(k + 1, 1 - buf)

        base = first + 1 + 5 * k
        solve_pair(
            lead.at[buf], shift.at[buf], partner, (one, two, three), weights, values,
            [queues[base + 2 + axis] for axis in range(3)], accum, queues[base], queues[base + 1],
        )
        return 0

    lax.fori_loop(0, total, visit, 0)

    if stage:
        def leave(x, _):
            for t in range(TILES):
                at = pl.ds(8 * t, 8)
                leaving[pl.ds(pl.multiple_of(x * BOX_Y + 8 * t, 8), 8), :] = accum[REMOTE, x, at, :]
                if stage == 1:
                    accum[REMOTE, x, at, :] = jnp.zeros((8, BOX_Z), F32)
                else:
                    for box in range(ORB_DEV):
                        (leave_first, leave_second)[box][x, at, :] = accum[2 + box, x, at, :]
            return 0

        lax.fori_loop(0, BOX_X, leave, 0, unroll=8)
        zero_rows(leaving, ROWS, leaving.shape[0] - ROWS)


SMEM = pl.BlockSpec(memory_space=pltpu.SMEM)
VMEM = pl.BlockSpec(memory_space=pltpu.VMEM)
HBM = pl.BlockSpec(memory_space=pltpu.HBM)


def run_stage(stage, lists, fixed, remote=(), accum=()):
    operands = [*lists, *fixed, *remote, *accum]
    specs = (
        [SMEM] * len(lists) + [VMEM] * 2 + [HBM] * 2 + [HBM] * len(remote) + [VMEM] * len(accum)
    )
    queue = jax.ShapeDtypeStruct((2 * LIST,), jnp.int32)
    leaving = ([], [(ROWS + 16, BOX_Z)], [(ROWS + 8, BOX_Z), BOX, BOX])[stage]
    shapes = [jax.ShapeDtypeStruct(shape, F32) for shape in [(REMOTE + 1,) + BOX] + leaving]
    outs = [VMEM] * len(shapes)
    scratch = [
        pltpu.VMEM((2,) + BOX, F32),
        pltpu.VMEM((2, SHIFT_ROWS, BOX_Z), F32),
        pltpu.VMEM(BOX, F32),
        pltpu.VMEM((STENCIL_ROWS, BOX_Z), F32),
        pltpu.VMEM((STENCIL_ROWS, BOX_Z), F32),
        pltpu.VMEM((STENCIL_ROWS, BOX_Z), F32),
        pltpu.SemaphoreType.DMA((2, 2)),
    ]
    if stage < 2:
        shapes.append(queue)
        outs.append(SMEM)
        scratch += [
            pltpu.SMEM((1, BOX_Z), F32),
            pltpu.SMEM((2 * SLOTS + 1,), jnp.int32),
            pltpu.SemaphoreType.DMA,
        ]
    return pl.pallas_call(
        functools.partial(stage_kernel, stage),
        out_shape=shapes,
        in_specs=specs,
        out_specs=outs,
        input_output_aliases={len(operands) - 1: 0} if accum else {},
        scratch_shapes=scratch,
        compiler_params=pltpu.CompilerParams(vmem_limit_bytes=24 << 20),
        cost_estimate=pl.CostEstimate(
            flops=1000, bytes_accessed=1000, transcendentals=0
        ),
        name="stage_" + "abc"[stage],
    )(*operands)


def total_kernel(box, accum, mate, remote, *rest):
    result, chunk, sem = rest[-3:]

    def add(x, _):
        for t in range(TILES):
            at = pl.ds(8 * t, 8)
            far = remote[pl.ds(pl.multiple_of(x * BOX_Y + 8 * t, 8), 8), :]
            chunk[x, at, :] = accum[box, x, at, :] + mate[x, at, :] + far
        pltpu.make_async_copy(chunk.at[x], result.at[box, x], sem).start()
        return 0

    lax.fori_loop(0, BOX_X, add, 0, unroll=8)
    pltpu.make_async_copy(chunk, result.at[box], sem).wait()


def run_total(box, accum, mate, remote, result=()):
    return pl.pallas_call(
        functools.partial(total_kernel, box),
        out_shape=jax.ShapeDtypeStruct((ORB_DEV,) + BOX, F32),
        in_specs=[VMEM, VMEM, VMEM] + [HBM] * len(result),
        out_specs=HBM,
        input_output_aliases={3: 0} if result else {},
        scratch_shapes=[pltpu.VMEM(BOX, F32), pltpu.SemaphoreType.DMA],
        compiler_params=pltpu.CompilerParams(vmem_limit_bytes=4 << 20),
        name="total_" + "ab"[box],
    )(accum, mate, remote, *result)


def local(orbitals, pair_list, pair_count, box_offset):
    position = lax.axis_index("orb").astype(jnp.int32)[None]
    devices = lax.axis_size("orb")
    mates = [(d, d ^ 1) for d in range(devices)]
    across = [(d, d + 1) for d in range(1, devices - 1, 2)]
    across = across + [(b, a) for a, b in across]
    staging = [
        pltpu.VMEM(BOX, F32),
        pltpu.SemaphoreType.DMA((CHUNKS,)),
        pltpu.SemaphoreType.DMA((CHUNKS,)),
    ]
    payload, note = pl.pallas_call(
        first_kernel,
        out_shape=[
            jax.ShapeDtypeStruct((BOX_X + 1, BOX_Y, BOX_Z), F32),
            jax.ShapeDtypeStruct((8, BOX_Z), F32),
        ],
        in_specs=[HBM, SMEM, HBM],
        out_specs=[HBM, HBM],
        scratch_shapes=[
            pltpu.SMEM((1, 2, SLOTS), jnp.int32),
            pltpu.VMEM((BOX_Y, BOX_Z), F32),
            pltpu.SemaphoreType.DMA((2,)),
        ]
        + staging,
        compiler_params=pltpu.CompilerParams(vmem_limit_bytes=60 << 20),
        name="first_box",
    )(jnp.transpose(pair_list, (0, 2, 1)), pair_count, orbitals)
    payload, held = lax.optimization_barrier((payload, orbitals))
    far_first = lax.ppermute(payload, "orb", across)
    mate = lax.ppermute(held, "orb", mates)
    mate_note = lax.ppermute(note, "orb", mates)
    second = pl.pallas_call(
        second_kernel,
        out_shape=jax.ShapeDtypeStruct(BOX, F32),
        in_specs=[HBM],
        out_specs=HBM,
        scratch_shapes=staging,
        compiler_params=pltpu.CompilerParams(vmem_limit_bytes=60 << 20),
        name="second_box",
    )(orbitals)
    far_second = lax.ppermute(second, "orb", across)
    weights, values = sine_basis()
    fixed = (jnp.asarray(weights), jnp.asarray(values), orbitals, mate)
    nearest = jnp.clip(ORB_DEV * (position - 3), 0, ORB_DEV * (devices - 7))
    offsets = lax.dynamic_slice(box_offset, (nearest[0], 0), (7 * ORB_DEV, 3)).reshape(-1)
    table = jnp.concatenate([pair_list.reshape(-1), pair_count, position, nearest, offsets])
    accum, left_over = run_stage(0, [table], fixed, [mate_note])
    accum, for_first, later = run_stage(1, [table, left_over], fixed, [far_first], [accum])
    back_first = lax.ppermute(for_first, "orb", across)
    accum, for_second, *for_mate = run_stage(2, [later], fixed, [far_second], [accum])
    back_second = lax.ppermute(for_second, "orb", across)
    back_mate = [lax.ppermute(box, "orb", mates) for box in for_mate]
    result = run_total(0, accum, back_mate[0], back_first)
    return run_total(1, accum, back_mate[1], back_second, (result,))


def solution(mesh):
    placed = (P("orb", None, None, None), P("orb", None, None), P("orb"), P())
    return jax.shard_map(
        local, mesh=mesh, in_specs=placed, out_specs=P("orb", None, None, None), check_vma=False
    )
```
